32 devices in a mesh: req: 4 (over z), head: 8 (over y, x, core).
Axes of the slice: x: 2, y: 2, z: 4, core: 2. Of those that a mesh axis runs over, the one named last changes fastest.
Arguments:
- hidden_in: bfloat16 [64, 1024], P(('req', 'head')), may hold values from -6 to 6
- lengths: int32 [64], P('req'), may hold values from 2 to 1024, as said below
- request_order: int32 [64], replicated, may hold values from 0 to 63, each once
- key_cache: bfloat16 [2, 64, 16, 64, 1024], P(None, 'req', 'head')
- value_cache: bfloat16 [2, 64, 16, 64, 1024], P(None, 'req', 'head'), may hold values from -6 to 6
- w_qkv: bfloat16 [2, 16, 1024, 192], P(None, 'head'), may hold values from -0.1875 to 0.1875
- w_out: bfloat16 [2, 16, 64, 1024], P(None, 'head'), may hold values from -0.1875 to 0.1875
- w_up: bfloat16 [2, 1024, 4096], P(None, None, ('req', 'head')), may hold values from -0.1875 to 0.1875
- bias_up: bfloat16 [2, 4096], P(None, ('req', 'head')), may hold values from -3 to 3
- w_down: bfloat16 [2, 1024, 4096], P(None, None, ('req', 'head')), may hold values from -0.09375 to 0.09375
- norm_gain: float32 [2, 2, 1024], replicated, may hold values from 0.1 to 1.9
- norm_bias: float32 [2, 2, 1024], replicated, may hold values from -3 to 3
- embedding: bfloat16 [49152, 1024], P(('req', 'head')), may hold values from -0.59765625 to 0.59765625
Outputs:
- logits: float32 [64, 49152], P(None, ('req', 'head'))
The draws below stay inside these ranges and needn't reach their ends.
Inputs may be any that keep to these rules, and one draw needn't show every extreme that they name: `lengths`: the largest length is 1024. Slot s of the caches and of lengths belongs to request request_order[s]; each request once.
All inputs are finite; a program needn't handle non-finite values.
Results may differ from the reference program's by a relative error of at most 0.0095.
Values may be sent and summed in bfloat16 or wider, within the bound.
A program may use at most 64 MiB of HBM per device.

```python
import jax
import jax.numpy as jnp
from jax import lax

D = 1024
HEADS = 16
HEAD_DIM = 64
FF = 4096
VOCAB = 49152
LAYERS = 2
CACHE_MAX = 1024
REQUESTS = 64


def draw_lengths(key, part):
    first_key, second_key = jax.random.split(key)
    drawn = jax.random.randint(first_key, (REQUESTS,), 2, CACHE_MAX + 1)
    where_max = jax.random.randint(second_key, (), 0, REQUESTS)
    return drawn.at[where_max].set(CACHE_MAX).astype(jnp.int32)


def draw_key_cache(key, part):
    keys_all = jax.random.split(key, 1)
    shape_full = (LAYERS, REQUESTS, HEADS, HEAD_DIM, CACHE_MAX)
    base = jax.random.normal(keys_all[0], shape_full, jnp.float32)
    return base.astype(jnp.bfloat16)


def levels(key, extent, cuts, low, largest):
    def one(position, blocks):
        steps = jax.random.uniform(jax.random.fold_in(jax.random.fold_in(key, 6), position), (blocks,), jnp.float32, low / len(cuts), largest / len(cuts))
        return jnp.repeat(jnp.exp(steps), extent[position] // blocks).reshape((-1,) + (1,) * (len(extent) - position - 1))

    factor_of = one(*cuts[0])
    for cut in cuts[1:]:
        factor_of = factor_of * one(*cut)
    return factor_of


def gaussian(key, shape, width, bound, cuts=(), kind=jnp.bfloat16):
    entries = width * jax.random.normal(key, shape, jnp.float32)
    if cuts:
        entries = entries * levels(key, shape, cuts, -0.22, 0.18)
    return jnp.clip(entries, -bound, bound).astype(kind)


def setup_inputs(seed: int = 0) -> dict:
    splits = jax.random.split(jax.random.key(seed), 14)
    return {
        "hidden_in": gaussian(splits[0], (REQUESTS, D), 1.0, 6.0, ((0, 32),)),
        "lengths": draw_lengths(jax.random.fold_in(splits[13], 71), 0),
        "request_order": jax.random.permutation(splits[2], REQUESTS).astype(jnp.int32),
        "key_cache": draw_key_cache(jax.random.fold_in(splits[13], 71), 0),
        "value_cache": gaussian(splits[4], (LAYERS, REQUESTS, HEADS, HEAD_DIM, CACHE_MAX), 1.0, 6.0, ((1, 4), (2, 8))),
        "w_qkv": gaussian(splits[5], (LAYERS, HEADS, D, 3 * HEAD_DIM), D ** -0.5, 0.1875, ((1, 8),)),
        "w_out": gaussian(splits[6], (LAYERS, HEADS, HEAD_DIM, D), D ** -0.5, 0.1875, ((1, 8),)),
        "w_up": gaussian(splits[7], (LAYERS, D, FF), D ** -0.5, 0.1875, ((2, 32),)),
        "bias_up": gaussian(splits[8], (LAYERS, FF), 0.5, 3.0, ((1, 32),)),
        "w_down": gaussian(splits[9], (LAYERS, D, FF), FF ** -0.5, 0.09375, ((2, 32),)),
        "norm_gain": jnp.clip(1.0 + 0.18 * jax.random.normal(splits[10], (LAYERS, 2, D), jnp.float32), 0.1, 1.9),
        "norm_bias": gaussian(splits[11], (LAYERS, 2, D), 0.5, 3.0, (), jnp.float32),
        "embedding": gaussian(splits[12], (VOCAB, D), 0.1, 0.59765625, ((0, 32),)),
    }


def layer_norm(values, gain_vec, bias_vec):
    average = lax.optimization_barrier(jnp.mean(values, axis=-1, keepdims=True))
    centred = values - average
    variance = lax.optimization_barrier(jnp.mean(centred * centred, axis=-1, keepdims=True))
    return centred * lax.rsqrt(variance + 1e-05) * gain_vec + bias_vec

def one_head(query, own_key, own_value, keys, values, lengths, score_scale):
    positions = jnp.arange(CACHE_MAX, dtype=jnp.int32)
    scores = jnp.einsum('rd,rdl->rl', query, keys.astype(jnp.float32)) * score_scale
    scores = jnp.where(positions[None, :] < lengths[:, None], scores, -jnp.inf)
    own = lax.optimization_barrier(jnp.sum(query * own_key, axis=-1)) * score_scale
    row_max = jnp.maximum(lax.optimization_barrier(jnp.max(scores, axis=-1)), own)
    expo = jnp.exp(scores - row_max[:, None])
    own_exp = jnp.exp(own - row_max)
    denom = lax.optimization_barrier(jnp.sum(expo, axis=-1)) + own_exp
    expo_b = lax.optimization_barrier(expo.astype(jnp.bfloat16)).astype(jnp.float32)
    own_b = lax.optimization_barrier(own_exp.astype(jnp.bfloat16)).astype(jnp.float32)
    mixed = jnp.einsum('rl,rdl->rd', expo_b, values.astype(jnp.float32)) + own_b[:, None] * own_value
    return (mixed / denom[:, None]).astype(jnp.bfloat16)

def reference(hidden_in, lengths, request_order, key_cache, value_cache, w_qkv, w_out, w_up, bias_up, w_down, norm_gain, norm_bias, embedding):
    score_scale = HEAD_DIM ** (-0.5)
    state = hidden_in[request_order]
    for layer_idx in range(LAYERS):
        projected = jnp.einsum('rd,hde->rhe', state.astype(jnp.float32), w_qkv[layer_idx].astype(jnp.float32)).astype(jnp.bfloat16).astype(jnp.float32)
        outputs = []
        for head_idx in range(HEADS):
            outputs.append(one_head(projected[:, head_idx, :HEAD_DIM], projected[:, head_idx, HEAD_DIM:2 * HEAD_DIM], projected[:, head_idx, 2 * HEAD_DIM:], key_cache[layer_idx, :, head_idx], value_cache[layer_idx, :, head_idx], lengths, score_scale))
        head_out = jnp.stack(outputs, axis=1)
        attn_out = jnp.einsum('rhd,hde->re', head_out.astype(jnp.float32), w_out[layer_idx].astype(jnp.float32))
        normed = layer_norm(state.astype(jnp.float32) + attn_out, norm_gain[layer_idx, 0], norm_bias[layer_idx, 0]).astype(jnp.bfloat16)
        pre_act = jnp.dot(normed, w_up[layer_idx], preferred_element_type=jnp.float32) + bias_up[layer_idx].astype(jnp.float32)
        hidden = jax.nn.gelu(pre_act, approximate=False).astype(jnp.bfloat16)
        mlp_out = jnp.einsum('rf,df->rd', hidden.astype(jnp.float32), w_down[layer_idx].astype(jnp.float32))
        state = layer_norm(normed.astype(jnp.float32) + mlp_out, norm_gain[layer_idx, 1], norm_bias[layer_idx, 1]).astype(jnp.bfloat16)
    inverse = jnp.zeros_like(request_order).at[request_order].set(jnp.arange(REQUESTS, dtype=jnp.int32))
    return jnp.dot(state[inverse], embedding.T, preferred_element_type=jnp.float32)
```

```python
import functools

import jax
import jax.numpy as jnp
from jax import lax
from jax.experimental import pallas as pl
from jax.experimental.pallas import tpu as pltpu
from jax.sharding import PartitionSpec as P

LAYERS = 2
MESH = pl.DeviceIdType.MESH
F32 = jnp.float32
BF16 = jnp.bfloat16
NT = (((1,), (1,)), ((), ()))


def layer_norm(values, gain_vec, bias_vec):
    average = jnp.mean(values, axis=-1, keepdims=True)
    centred = values - average
    variance = jnp.mean(centred * centred, axis=-1, keepdims=True)
    return centred * lax.rsqrt(variance + 1e-05) * gain_vec + bias_vec


def peer_offsets(n_req, n_head):
    every = [(a, b) for a in range(n_req) for b in range(n_head) if a or b]
    return sorted(every, key=lambda o: (-(o[0] + bin(o[1] >> 1).count("1")), -o[1]))


def flip(index, mask):
    bit = 1
    while bit <= mask:
        if mask & bit:
            index = index + bit - 2 * bit * lax.rem(index // bit, 2)
        bit *= 2
    return index


def pair_kernel(
    n_req,
    n_head,
    hidden_ref,
    lengths_ref,
    order_ref,
    key_hbm,
    value_hbm,
    qkv_hbm,
    out_w_hbm,
    up_hbm,
    bias_up_ref,
    down_hbm,
    gain_ref,
    bias_ref,
    emb_hbm,
    logits_ref,
    key_v,
    value_v,
    qkv_v,
    out_w_v,
    up_v,
    down_v,
    emb_v,
    load_sem,
    emb_sem,
    bias_v,
    state_v,
    first,
    attn_out,
    attn_in,
    spread,
    mlp_out,
    mlp_in,
    own_out,
    own_in,
    near,
    last,
    first_send,
    first_recv,
    pair_send,
    pair_recv,
    attn_send,
    attn_recv,
    spread_send,
    spread_recv,
    mlp_send,
    mlp_recv,
    own_send,
    own_recv,
    near_send,
    near_recv,
    last_send,
    last_recv,
):
    me_r = lax.axis_index("req")
    me_h = lax.axis_index("head")
    me = me_r * n_head + me_h
    core = lax.rem(me_h, 2)
    chip = me // 2
    partner = (me_r, flip(me_h, 1))
    rows, width = hidden_ref.shape
    group, heads, head_size, cached = key_v.shape[1:]
    units = up_hbm.shape[2]
    slots = n_req * group
    devices = n_req * n_head
    chips = devices // 2
    part = width // n_head
    offsets = peer_offsets(n_req, n_head)
    everywhere = [(flip(me_r, a), flip(me_h, b)) for a, b in offsets]
    plane = [(me_r, flip(me_h, b)) for a, b in offsets if not a]
    middle = n_req // 2
    taker = lax.rem((me_r + 1) // middle, 2)
    mine = taker == core
    near_group = jnp.where(me_r < middle, core, n_req - 1 - core)
    far_group = n_req - 1 - near_group

    barrier = pltpu.get_barrier_semaphore()
    for peer in everywhere:
        pl.semaphore_signal(barrier, inc=1, device_id=peer, device_id_type=MESH)

    def up_part(ref, layer, which):
        return ref.at[layer, :, pl.ds(which * units, units)]

    def load(layer, which):
        source, target = (
            (qkv_hbm.at[layer], qkv_v.at[layer]),
            (key_hbm.at[layer], key_v.at[layer]),
            (value_hbm.at[layer], value_v.at[layer]),
            (out_w_hbm.at[layer], out_w_v.at[layer]),
            (up_hbm.at[layer], up_part(up_v, layer, 0)),
            (down_hbm.at[layer], up_part(down_v, layer, 0)),
        )[which]
        return pltpu.make_async_copy(source, target, load_sem.at[layer, which])

    for layer in range(LAYERS):
        for which in range(6):
            load(layer, which).start()
    emb_load = pltpu.make_async_copy(emb_hbm, emb_v, emb_sem)
    emb_load.start()

    def remote(source, target, sender, receiver, peer):
        return pltpu.make_async_remote_copy(
            src_ref=source,
            dst_ref=target,
            send_sem=sender,
            recv_sem=receiver,
            device_id=peer,
            device_id_type=MESH,
        )

    def wait(sem, ref, count):
        block = ref.at[pl.ds(0, count)]
        pltpu.make_async_copy(block, block, sem).wait()

    def either(held, given):
        pl.when(mine)(held)
        pl.when(jnp.logical_not(mine))(given)

    def pair_copies(layer):
        return (
            remote(up_hbm.at[layer], up_part(up_v, layer, 1), pair_send.at[layer, 0], pair_recv.at[layer, 0], partner),
            remote(
                down_hbm.at[layer], up_part(down_v, layer, 1), pair_send.at[layer, 1], pair_recv.at[layer, 1], partner
            ),
        )

    bias_copy = remote(bias_v.at[0], bias_v.at[1], pair_send.at[LAYERS, 0], pair_recv.at[LAYERS, 0], partner)

    chunks = width // 128
    tile = first.shape[1]
    hidden = hidden_ref[...].astype(F32)
    pieces = [hidden[:, c * 128 : (c + 1) * 128] for c in range(chunks)]
    if tile > chunks * rows:
        pieces.append(jnp.zeros((tile - chunks * rows, 128), F32))
    first[me] = jnp.concatenate(pieces, axis=0).astype(BF16)
    bias_v[0] = jnp.concatenate(
        [bias_up_ref[...].astype(F32), jnp.zeros((bias_v.shape[1] - LAYERS, units), F32)], axis=0
    )
    for layer in range(LAYERS):
        mlp_in[layer, chip] = jnp.zeros((group, part), BF16)

    order_row = order_ref[...]
    ids_row = lax.broadcasted_iota(jnp.int32, (group, slots), 0) + me_r * group
    ids_col = lax.broadcasted_iota(jnp.int32, (group, slots), 1)
    order_here = jnp.sum(
        jnp.where(ids_row == ids_col, jnp.broadcast_to(order_row, (group, slots)).astype(F32), 0.0),
        axis=1,
        keepdims=True,
    ).astype(jnp.int32)
    wanted = (order_here // rows) * tile + lax.rem(order_here, rows)
    wide = lax.broadcasted_iota(jnp.int32, (group, devices * tile), 1)
    wanted = jnp.broadcast_to(wanted, (group, devices * tile))
    choose = jnp.concatenate(
        [(wide == wanted + c * rows).astype(F32) for c in range(chunks)], axis=0
    ).astype(BF16)

    square = lax.broadcasted_iota(jnp.int32, (group, group), 0) == lax.broadcasted_iota(
        jnp.int32, (group, group), 1
    )
    limit = jnp.sum(
        jnp.where(square, jnp.broadcast_to(lengths_ref[...], (group, group)).astype(F32), 0.0), axis=1, keepdims=True
    ).astype(jnp.int32)
    limit = jnp.broadcast_to(limit, (group, cached))
    valid = lax.broadcasted_iota(jnp.int32, (group, cached), 1) < limit
    flat = group * head_size
    diagonal = lax.broadcasted_iota(jnp.int32, (group, flat), 0) == (
        lax.broadcasted_iota(jnp.int32, (group, flat), 1) // head_size
    )
    score_scale = head_size ** (-0.5)

    pl.semaphore_wait(barrier, devices - 1)
    for peer in everywhere:
        remote(first.at[me], first.at[me], first_send, first_recv, peer).start()
    for layer in range(LAYERS):
        for copy in pair_copies(layer):
            copy.start()
    bias_copy.start()
    wait(first_recv, first, devices - 1)
    chosen = jnp.dot(choose, first[...].reshape(devices * tile, 128), preferred_element_type=F32)
    state = jnp.concatenate([chosen[c * group : (c + 1) * group] for c in range(chunks)], axis=1)
    for head in range(n_head):
        state_v[head] = state[:, head * part : (head + 1) * part].astype(BF16)

    def joined(ref, lead):
        return jnp.concatenate([ref[lead + (head,)] for head in range(n_head)], axis=1)

    def layer_step(layer, carry):
        state = joined(state_v, ())
        load(layer, 0).wait()
        attn = jnp.zeros((group, width), F32)
        parts = []
        for head in range(heads):
            projected = (
                lax.dot_general(state, qkv_v[layer, head], NT, preferred_element_type=F32).astype(BF16).astype(F32)
            )
            parts.append(
                (
                    projected[:, :head_size],
                    projected[:, head_size : 2 * head_size],
                    projected[:, 2 * head_size :],
                )
            )
        load(layer, 1).wait()
        expos = []
        for head in range(heads):
            query, own_key, own_value = parts[head]
            tiled = jnp.where(diagonal, jnp.concatenate([query] * group, axis=1), 0.0).astype(BF16)
            keys = key_v[layer, :, head].reshape(flat, cached)
            scores = jnp.dot(tiled, keys, preferred_element_type=F32) * score_scale
            scores = jnp.where(valid, scores, -jnp.inf)
            own = jnp.sum(query * own_key, axis=-1, keepdims=True) * score_scale
            row_max = jnp.maximum(jnp.max(scores, axis=-1, keepdims=True), own)
            expo = jnp.exp(scores - row_max)
            own_exp = jnp.exp(own - row_max)
            denom = jnp.sum(expo, axis=-1, keepdims=True) + own_exp
            expos.append((expo.astype(BF16), own_exp.astype(BF16).astype(F32), denom))
        load(layer, 2).wait()
        load(layer, 3).wait()
        for head in range(heads):
            expo, own_exp, denom = expos[head]
            values = value_v[layer, :, head].reshape(flat, cached)
            every = lax.dot_general(expo, values, NT, preferred_element_type=F32)
            every = jnp.where(diagonal, every, 0.0)
            mixed = every[:, :head_size]
            for block in range(1, group):
                mixed += every[:, block * head_size : (block + 1) * head_size]
            mixed += own_exp * parts[head][2]
            head_out = (mixed / denom).astype(BF16)
            attn += jnp.dot(head_out, out_w_v[layer, head], preferred_element_type=F32)
        for head in range(n_head):
            attn_out[layer, head] = attn[:, head * part : (head + 1) * part].astype(BF16)
        for peer in plane:
            remote(
                attn_out.at[layer, peer[1]], attn_in.at[layer, me_h], attn_send.at[layer], attn_recv.at[layer], peer
            ).start()
        attn_in[layer, me_h] = attn_out[layer, me_h]
        wait(attn_recv.at[layer], attn_in.at[layer], n_head - 1)
        total = attn_in[layer, 0].astype(F32)
        for head in range(1, n_head):
            total += attn_in[layer, head].astype(F32)
        spread[layer, me_r, me_h] = (total + state_v[me_h].astype(F32)).astype(BF16)

        def spread_copy(a, b):
            base = flip(me_h, b)
            peer = (flip(me_r, a), base - lax.rem(base, 2) + taker)
            block = spread.at[layer, me_r, me_h]
            return remote(block, block, spread_send.at[layer], spread_recv.at[layer, me_r], peer)

        for a, b in offsets:
            if b % 2 == 0:
                spread_copy(a, b).start()

        @pl.when(jnp.logical_not(mine))
        def _():
            spread_copy(0, 0).start()

        gains, biases = gain_ref[layer], bias_ref[layer]
        bias_rows = []
        for source in range(2):
            bias_up = bias_v[source]
            bias_row = bias_up[0:1]
            for other in range(1, LAYERS):
                bias_row = jnp.where(layer == other, bias_up[other : other + 1], bias_row)
            bias_rows.append(bias_row)
        bias_row = jnp.concatenate(bias_rows, axis=1)

        def feed(which, block):
            before = jnp.concatenate([spread[layer, block, head] for head in range(n_head)], axis=1).astype(F32)
            normed = layer_norm(before, gains[0:1], biases[0:1]).astype(BF16)
            pre_act = jnp.dot(normed, up_v[layer], preferred_element_type=F32) + bias_row
            hidden = (0.5 * pre_act * (1.0 + lax.erf(pre_act * 0.7071067811865476))).astype(BF16)
            mlp = lax.dot_general(hidden, down_v[layer], NT, preferred_element_type=F32)
            for head in range(n_head):
                mlp_out[layer, which, head] = mlp[:, head * part : (head + 1) * part].astype(BF16)
            return mlp + normed.astype(F32)

        def mlp_copy(which, block, b):
            peer = (block, flip(me_h, b))
            return remote(
                mlp_out.at[layer, which, peer[1]], mlp_in.at[layer, chip], mlp_send.at[layer], mlp_recv.at[layer], peer
            )

        def own_copy():
            return remote(own_out.at[layer, partner[1]], own_in.at[layer], own_send.at[layer], own_recv.at[layer], partner)

        load(layer, 4).wait()
        load(layer, 5).wait()
        for copy in pair_copies(layer):
            copy.wait_recv()
        either(
            lambda: wait(spread_recv.at[layer, near_group], spread.at[layer, 0], n_head - 1),
            lambda: wait(spread_recv.at[layer, near_group], spread.at[layer, 0], n_head),
        )

        whole = feed(0, near_group)
        for head in range(n_head):
            own_out[layer, head] = whole[:, head * part : (head + 1) * part]
        for b in range(2, n_head):
            mlp_copy(0, near_group, b).start()

        @pl.when(mine)
        def _():
            own_copy().start()
            own_in[layer] = own_out[layer, me_h]

        @pl.when(jnp.logical_not(mine))
        def _():
            for b in range(2):
                mlp_copy(0, near_group, b).start()

        wait(spread_recv.at[layer, far_group], spread.at[layer, 0], n_head)
        feed(1, far_group)
        for b in range(n_head - 1, -1, -1):
            mlp_copy(1, far_group, b).start()

        @pl.when(jnp.logical_not(mine))
        def _():
            own_copy().wait_recv()

        wait(mlp_recv.at[layer], mlp_in.at[layer], chips - 1)
        total = own_in[layer]
        for source in range(chips):
            total += mlp_in[layer, source].astype(F32)
        after = total.astype(BF16)

        @pl.when(layer < LAYERS - 1)
        def _():
            near[layer, me_h] = after
            for peer in plane:
                block = near.at[layer, me_h]
                remote(block, block, near_send.at[layer], near_recv.at[layer], peer).start()
            wait(near_recv.at[layer], near.at[layer], n_head - 1)
            fresh = joined(near, (layer,)).astype(F32)
            fresh = layer_norm(fresh, gains[1:2], biases[1:2]).astype(BF16)
            for head in range(n_head):
                state_v[head] = fresh[:, head * part : (head + 1) * part]

        @pl.when(layer == LAYERS - 1)
        def _():
            last[me] = after

        return carry

    bias_copy.wait_recv()
    for layer in range(LAYERS):
        layer_step(layer, 0)
    for peer in everywhere:
        remote(last.at[me], last.at[me], last_send, last_recv, peer).start()
    pick = (
        (
            lax.broadcasted_iota(jnp.int32, (slots, slots), 0)
            == jnp.broadcast_to(order_row, (slots, slots))
        )
        .astype(F32)
        .astype(BF16)
    )
    emb_load.wait()
    wait(first_send, first, devices - 1)
    bias_copy.wait_send()
    for layer in range(LAYERS):
        for copy in pair_copies(layer):
            copy.wait_send()
        wait(attn_send.at[layer], attn_in.at[layer], n_head - 1)
        if layer < LAYERS - 1:
            wait(near_send.at[layer], near.at[layer], n_head - 1)

        @pl.when(mine)
        def _():
            wait(spread_send.at[layer], mlp_in.at[layer], chips - 1)
            wait(mlp_send.at[layer], mlp_in.at[layer], 2 * n_head - 2)
            remote(
                own_out.at[layer, 0], own_in.at[layer], own_send.at[layer], own_recv.at[layer], partner
            ).wait_send()

        @pl.when(jnp.logical_not(mine))
        def _():
            wait(spread_send.at[layer], mlp_in.at[layer], chips)
            wait(mlp_send.at[layer], mlp_in.at[layer], 2 * n_head)

    wait(last_recv, last, devices - 1)
    before = jnp.concatenate(
        [
            jnp.concatenate([last[req * n_head + head] for head in range(n_head)], axis=1)
            for req in range(n_req)
        ],
        axis=0,
    ).astype(F32)
    gains, biases = gain_ref[LAYERS - 1], bias_ref[LAYERS - 1]
    final = layer_norm(before, gains[1:2], biases[1:2]).astype(BF16)
    ordered = jnp.dot(pick, final, preferred_element_type=F32).astype(BF16)
    logits_ref[...] = lax.dot_general(ordered, emb_v[...], NT, preferred_element_type=F32)
    wait(last_send, last, devices - 1)


def kernel(
    n_req,
    n_head,
    hidden_ref,
    lengths_ref,
    order_ref,
    key_hbm,
    value_hbm,
    qkv_hbm,
    out_w_hbm,
    up_hbm,
    bias_up_ref,
    down_hbm,
    gain_ref,
    bias_ref,
    emb_hbm,
    logits_ref,
    key_v,
    value_v,
    qkv_v,
    out_w_v,
    up_v,
    down_v,
    emb_v,
    load_sem,
    emb_sem,
    state_v,
    normed_v,
    first,
    attn_out,
    attn_in,
    spread,
    mlp_out,
    mlp_in,
    near,
    send_sem,
    recv_sem,
):
    me_r = lax.axis_index("req")
    me_h = lax.axis_index("head")
    me = me_r * n_head + me_h
    rows, width = hidden_ref.shape
    group, heads, head_size, cached = key_v.shape[1:]
    slots = n_req * group
    devices = n_req * n_head
    part = width // n_head
    offsets = peer_offsets(n_req, n_head)
    everywhere = [(flip(me_r, a), flip(me_h, b)) for a, b in offsets]
    plane = [(me_r, flip(me_h, b)) for a, b in offsets if not a]

    barrier = pltpu.get_barrier_semaphore()
    for peer in everywhere:
        pl.semaphore_signal(barrier, inc=1, device_id=peer, device_id_type=MESH)

    pairs = (
        (qkv_hbm, qkv_v),
        (key_hbm, key_v),
        (value_hbm, value_v),
        (out_w_hbm, out_w_v),
        (up_hbm, up_v),
        (down_hbm, down_v),
    )

    def load(layer, which):
        source, target = pairs[which]
        return pltpu.make_async_copy(source.at[layer], target.at[layer], load_sem.at[layer, which])

    for layer in range(LAYERS):
        for which in range(len(pairs)):
            load(layer, which).start()
    emb_load = pltpu.make_async_copy(emb_hbm, emb_v, emb_sem)
    emb_load.start()

    def send(turn, source, target, peers):
        for peer in peers:
            pltpu.make_async_remote_copy(
                src_ref=source(peer),
                dst_ref=target,
                send_sem=send_sem.at[turn],
                recv_sem=recv_sem.at[turn],
                device_id=peer,
                device_id_type=MESH,
            ).start()

    def wait(sem, turn, ref, count):
        block = ref.at[pl.ds(0, count)]
        pltpu.make_async_copy(block, block, sem.at[turn]).wait()

    chunks = width // 128
    tile = first.shape[1]
    hidden = hidden_ref[...].astype(F32)
    pieces = [hidden[:, c * 128 : (c + 1) * 128] for c in range(chunks)]
    if tile > chunks * rows:
        pieces.append(jnp.zeros((tile - chunks * rows, 128), F32))
    first[me] = jnp.concatenate(pieces, axis=0).astype(BF16)

    order_row = order_ref[...]
    ids_row = lax.broadcasted_iota(jnp.int32, (group, slots), 0) + me_r * group
    ids_col = lax.broadcasted_iota(jnp.int32, (group, slots), 1)
    order_here = jnp.sum(
        jnp.where(ids_row == ids_col, jnp.broadcast_to(order_row, (group, slots)).astype(F32), 0.0),
        axis=1,
        keepdims=True,
    ).astype(jnp.int32)
    wanted = (order_here // rows) * tile + lax.rem(order_here, rows)
    wide = lax.broadcasted_iota(jnp.int32, (group, devices * tile), 1)
    wanted = jnp.broadcast_to(wanted, (group, devices * tile))
    choose = jnp.concatenate(
        [(wide == wanted + c * rows).astype(F32) for c in range(chunks)], axis=0
    ).astype(BF16)

    square = lax.broadcasted_iota(jnp.int32, (group, group), 0) == lax.broadcasted_iota(
        jnp.int32, (group, group), 1
    )
    limit = jnp.sum(
        jnp.where(square, jnp.broadcast_to(lengths_ref[...], (group, group)).astype(F32), 0.0), axis=1, keepdims=True
    ).astype(jnp.int32)
    limit = jnp.broadcast_to(limit, (group, cached))
    valid = lax.broadcasted_iota(jnp.int32, (group, cached), 1) < limit
    flat = group * head_size
    diagonal = lax.broadcasted_iota(jnp.int32, (group, flat), 0) == (
        lax.broadcasted_iota(jnp.int32, (group, flat), 1) // head_size
    )
    score_scale = head_size ** (-0.5)

    pl.semaphore_wait(barrier, devices - 1)
    send(0, lambda peer: first.at[me], first.at[me], everywhere)
    wait(recv_sem, 0, first, devices - 1)
    chosen = jnp.dot(choose, first[...].reshape(devices * tile, 128), preferred_element_type=F32)
    state = jnp.concatenate([chosen[c * group : (c + 1) * group] for c in range(chunks)], axis=1)
    for head in range(n_head):
        state_v[head] = state[:, head * part : (head + 1) * part].astype(BF16)

    def joined(ref, lead):
        return jnp.concatenate([ref[lead + (head,)] for head in range(n_head)], axis=1)

    def layer_step(layer, carry):
        attn_turn, spread_turn, mlp_turn, near_turn = 1 + 4 * layer, 2 + 4 * layer, 3 + 4 * layer, 4 + 4 * layer
        state = joined(state_v, ())
        load(layer, 0).wait()
        attn = jnp.zeros((group, width), F32)
        parts = []
        for head in range(heads):
            projected = (
                lax.dot_general(state, qkv_v[layer, head], NT, preferred_element_type=F32).astype(BF16).astype(F32)
            )
            parts.append(
                (
                    projected[:, :head_size],
                    projected[:, head_size : 2 * head_size],
                    projected[:, 2 * head_size :],
                )
            )
        load(layer, 1).wait()
        expos = []
        for head in range(heads):
            query, own_key, own_value = parts[head]
            tiled = jnp.where(diagonal, jnp.concatenate([query] * group, axis=1), 0.0).astype(BF16)
            keys = key_v[layer, :, head].reshape(flat, cached)
            scores = jnp.dot(tiled, keys, preferred_element_type=F32) * score_scale
            scores = jnp.where(valid, scores, -jnp.inf)
            own = jnp.sum(query * own_key, axis=-1, keepdims=True) * score_scale
            row_max = jnp.maximum(jnp.max(scores, axis=-1, keepdims=True), own)
            expo = jnp.exp(scores - row_max)
            own_exp = jnp.exp(own - row_max)
            denom = jnp.sum(expo, axis=-1, keepdims=True) + own_exp
            expos.append((expo.astype(BF16), own_exp.astype(BF16).astype(F32), denom))
        load(layer, 2).wait()
        load(layer, 3).wait()
        for head in range(heads):
            expo, own_exp, denom = expos[head]
            values = value_v[layer, :, head].reshape(flat, cached)
            every = lax.dot_general(expo, values, NT, preferred_element_type=F32)
            every = jnp.where(diagonal, every, 0.0)
            mixed = every[:, :head_size]
            for block in range(1, group):
                mixed += every[:, block * head_size : (block + 1) * head_size]
            mixed += own_exp * parts[head][2]
            head_out = (mixed / denom).astype(BF16)
            attn += jnp.dot(head_out, out_w_v[layer, head], preferred_element_type=F32)
        for head in range(n_head):
            attn_out[layer, head] = attn[:, head * part : (head + 1) * part].astype(BF16)
        send(attn_turn, lambda peer: attn_out.at[layer, peer[1]], attn_in.at[layer, me_h], plane)
        attn_in[layer, me_h] = attn_out[layer, me_h]
        wait(recv_sem, attn_turn, attn_in.at[layer], n_head - 1)
        total = attn_in[layer, 0].astype(F32)
        for head in range(1, n_head):
            total += attn_in[layer, head].astype(F32)
        spread[layer, me] = (total + state_v[me_h].astype(F32)).astype(BF16)
        send(spread_turn, lambda peer: spread.at[layer, me], spread.at[layer, me], everywhere)
        gains, biases = gain_ref[layer], bias_ref[layer]
        bias_up = bias_up_ref[...].astype(F32)
        bias_row = bias_up[0:1]
        for other in range(1, LAYERS):
            bias_row = jnp.where(layer == other, bias_up[other : other + 1], bias_row)
        load(layer, 4).wait()
        load(layer, 5).wait()
        wait(recv_sem, spread_turn, spread.at[layer], devices - 1)
        before = jnp.concatenate(
            [
                jnp.concatenate([spread[layer, req * n_head + head] for head in range(n_head)], axis=1)
                for req in range(n_req)
            ],
            axis=0,
        ).astype(F32)
        normed = layer_norm(before, gains[0:1], biases[0:1]).astype(BF16)
        for req in range(n_req):
            for head in range(n_head):
                normed_v[req * n_head + head] = normed[
                    req * group : (req + 1) * group, head * part : (head + 1) * part
                ]
        pre_act = jnp.dot(normed, up_v[layer], preferred_element_type=F32) + bias_row
        hidden = (0.5 * pre_act * (1.0 + lax.erf(pre_act * 0.7071067811865476))).astype(BF16)
        mlp = lax.dot_general(hidden, down_v[layer], NT, preferred_element_type=F32).astype(BF16)
        for req in range(n_req):
            for head in range(n_head):
                mlp_out[layer, req * n_head + head] = mlp[
                    req * group : (req + 1) * group, head * part : (head + 1) * part
                ]
        send(mlp_turn, lambda peer: mlp_out.at[layer, peer[0] * n_head + peer[1]], mlp_in.at[layer, me], everywhere)
        mlp_in[layer, me] = mlp_out[layer, me]
        wait(recv_sem, mlp_turn, mlp_in.at[layer], devices - 1)
        total = mlp_in[layer, 0].astype(F32)
        for device in range(1, devices):
            total += mlp_in[layer, device].astype(F32)
        after = (total + normed_v[me].astype(F32)).astype(BF16)

        @pl.when(layer < LAYERS - 1)
        def _():
            near[layer, me_h] = after
            send(near_turn, lambda peer: near.at[layer, me_h], near.at[layer, me_h], plane)
            wait(recv_sem, near_turn, near.at[layer], n_head - 1)
            fresh = joined(near, (layer,)).astype(F32)
            fresh = layer_norm(fresh, gains[1:2], biases[1:2]).astype(BF16)
            for head in range(n_head):
                state_v[head] = fresh[:, head * part : (head + 1) * part]

        @pl.when(layer == LAYERS - 1)
        def _():
            spread[LAYERS, me] = after

        return carry

    lax.fori_loop(0, LAYERS, layer_step, 0)
    last = 4 * LAYERS
    send(last, lambda peer: spread.at[LAYERS, me], spread.at[LAYERS, me], everywhere)
    pick = (
        (
            lax.broadcasted_iota(jnp.int32, (slots, slots), 0)
            == jnp.broadcast_to(order_row, (slots, slots))
        )
        .astype(F32)
        .astype(BF16)
    )
    emb_load.wait()
    wait(send_sem, 0, first, devices - 1)
    for layer in range(LAYERS):
        wait(send_sem, 1 + 4 * layer, attn_in.at[layer], n_head - 1)
        wait(send_sem, 2 + 4 * layer, spread.at[layer], devices - 1)
        wait(send_sem, 3 + 4 * layer, mlp_in.at[layer], devices - 1)
        if layer < LAYERS - 1:
            wait(send_sem, 4 + 4 * layer, near.at[layer], n_head - 1)
    wait(recv_sem, last, spread.at[LAYERS], devices - 1)
    before = jnp.concatenate(
        [
            jnp.concatenate([spread[LAYERS, req * n_head + head] for head in range(n_head)], axis=1)
            for req in range(n_req)
        ],
        axis=0,
    ).astype(F32)
    gains, biases = gain_ref[LAYERS - 1], bias_ref[LAYERS - 1]
    final = layer_norm(before, gains[1:2], biases[1:2]).astype(BF16)
    ordered = jnp.dot(pick, final, preferred_element_type=F32).astype(BF16)
    logits_ref[...] = lax.dot_general(ordered, emb_v[...], NT, preferred_element_type=F32)
    wait(send_sem, last, spread.at[LAYERS], devices - 1)


def body(n_req, n_head, *args):
    (hidden_in, lengths, request_order, key_cache, value_cache, w_qkv, w_out, w_up, bias_up, w_down) = args[:10]
    norm_gain, norm_bias, embedding = args[10:]
    group = lengths.shape[0]
    width = hidden_in.shape[1]
    w_qkv = jnp.swapaxes(w_qkv, 2, 3)
    slots = request_order.shape[0]
    devices = n_req * n_head
    part = width // n_head
    tile = max(16, hidden_in.shape[0] * width // 128)
    vmem = pl.BlockSpec(memory_space=pltpu.VMEM)
    hbm = pl.BlockSpec(memory_space=pltpu.HBM)
    dma = pltpu.SemaphoreType.DMA
    pin = lambda array: pltpu.with_memory_space_constraint(array, pltpu.HBM)
    held = [key_cache, value_cache, w_qkv, w_out, w_up, w_down, embedding]
    return pl.pallas_call(
        functools.partial(kernel, n_req, n_head),
        out_shape=jax.ShapeDtypeStruct((slots, embedding.shape[0]), F32),
        in_specs=[vmem] * 3 + [hbm] * 5 + [vmem, hbm, vmem, vmem, hbm],
        out_specs=vmem,
        scratch_shapes=[pltpu.VMEM(array.shape, array.dtype) for array in held]
        + [
            dma((LAYERS, 6)),
            dma,
            pltpu.VMEM((n_head, group, part), BF16),
            pltpu.VMEM((devices, group, part), BF16),
            pltpu.VMEM((devices, tile, 128), BF16),
            pltpu.VMEM((LAYERS, n_head, group, part), BF16),
            pltpu.VMEM((LAYERS, n_head, group, part), BF16),
            pltpu.VMEM((1 + LAYERS, devices, group, part), BF16),
            pltpu.VMEM((LAYERS, devices, group, part), BF16),
            pltpu.VMEM((LAYERS, devices, group, part), BF16),
            pltpu.VMEM((LAYERS, n_head, group, part), BF16),
            dma((1 + 4 * LAYERS,)),
            dma((1 + 4 * LAYERS,)),
        ],
        compiler_params=pltpu.CompilerParams(
            collective_id=0, has_side_effects=True, vmem_limit_bytes=40 * 1024 * 1024
        ),
    )(
        pin(hidden_in),
        pin(lengths.reshape(1, group)),
        pin(request_order.reshape(1, slots)),
        pin(key_cache),
        pin(value_cache),
        pin(w_qkv),
        pin(w_out),
        pin(w_up),
        pin(bias_up),
        pin(w_down),
        pin(norm_gain),
        pin(norm_bias),
        pin(embedding),
    )


def pair_body(n_req, n_head, *args):
    (hidden_in, lengths, request_order, key_cache, value_cache, w_qkv, w_out, w_up, bias_up, w_down) = args[:10]
    norm_gain, norm_bias, embedding = args[10:]
    group = lengths.shape[0]
    width = hidden_in.shape[1]
    w_qkv = jnp.swapaxes(w_qkv, 2, 3)
    slots = request_order.shape[0]
    devices = n_req * n_head
    part = width // n_head
    tile = max(16, hidden_in.shape[0] * width // 128)
    vmem = pl.BlockSpec(memory_space=pltpu.VMEM)
    hbm = pl.BlockSpec(memory_space=pltpu.HBM)
    dma = pltpu.SemaphoreType.DMA
    pin = lambda array: pltpu.with_memory_space_constraint(array, pltpu.HBM)
    units = w_up.shape[2]
    chips = devices // 2
    sizes = [key_cache.shape, value_cache.shape, w_qkv.shape, w_out.shape]
    sizes += [(LAYERS, width, 2 * units)] * 2 + [embedding.shape]
    block = (group, part)
    return pl.pallas_call(
        functools.partial(pair_kernel, n_req, n_head),
        out_shape=jax.ShapeDtypeStruct((slots, embedding.shape[0]), F32),
        in_specs=[vmem] * 3 + [hbm] * 5 + [vmem, hbm, vmem, vmem, hbm],
        out_specs=vmem,
        scratch_shapes=[pltpu.VMEM(size, BF16) for size in sizes]
        + [
            dma((LAYERS, 6)),
            dma,
            pltpu.VMEM((2, 8, units), F32),
            pltpu.VMEM((n_head,) + block, BF16),
            pltpu.VMEM((devices, tile, 128), BF16),
            pltpu.VMEM((LAYERS, n_head) + block, BF16),
            pltpu.VMEM((LAYERS, n_head) + block, BF16),
            pltpu.VMEM((LAYERS, n_req, n_head) + block, BF16),
            pltpu.VMEM((LAYERS, 2, n_head) + block, BF16),
            pltpu.VMEM((LAYERS, chips) + block, BF16),
            pltpu.VMEM((LAYERS, n_head) + block, F32),
            pltpu.VMEM((LAYERS,) + block, F32),
            pltpu.VMEM((LAYERS, n_head) + block, BF16),
            pltpu.VMEM((devices,) + block, BF16),
            dma,
            dma,
            dma((LAYERS + 1, 2)),
            dma((LAYERS + 1, 2)),
            dma((LAYERS,)),
            dma((LAYERS,)),
            dma((LAYERS,)),
            dma((LAYERS, n_req)),
            dma((LAYERS,)),
            dma((LAYERS,)),
            dma((LAYERS,)),
            dma((LAYERS,)),
            dma((LAYERS,)),
            dma((LAYERS,)),
            dma,
            dma,
        ],
        compiler_params=pltpu.CompilerParams(
            collective_id=0, has_side_effects=True, vmem_limit_bytes=40 * 1024 * 1024
        ),
    )(
        pin(hidden_in),
        pin(lengths.reshape(1, group)),
        pin(request_order.reshape(1, slots)),
        pin(key_cache),
        pin(value_cache),
        pin(w_qkv),
        pin(w_out),
        pin(w_up),
        pin(bias_up),
        pin(w_down),
        pin(norm_gain),
        pin(norm_bias),
        pin(embedding),
    )


def solution(mesh):
    placed = (
        P(("req", "head"), None),
        P("req"),
        P(),
        P(None, "req", "head", None, None),
        P(None, "req", "head", None, None),
        P(None, "head", None, None),
        P(None, "head", None, None),
        P(None, None, ("req", "head")),
        P(None, ("req", "head")),
        P(None, None, ("req", "head")),
        P(),
        P(),
        P(("req", "head"), None),
    )
    inner = pair_body if (mesh.shape["req"], mesh.shape["head"]) == (4, 8) else body
    return jax.shard_map(
        functools.partial(inner, mesh.shape["req"], mesh.shape["head"]),
        mesh=mesh,
        in_specs=placed,
        out_specs=P(None, ("req", "head")),
        check_vma=False,
    )
```

```python
import functools

import jax
import jax.numpy as jnp
from jax import lax
from jax.experimental import pallas as pl
from jax.experimental.pallas import tpu as pltpu
from jax.sharding import PartitionSpec as P

LAYERS = 2
MESH = pl.DeviceIdType.MESH
F32 = jnp.float32
BF16 = jnp.bfloat16
NT = (((1,), (1,)), ((), ()))


def layer_norm(values, gain_vec, bias_vec):
    average = jnp.mean(values, axis=-1, keepdims=True)
    centred = values - average
    variance = jnp.mean(centred * centred, axis=-1, keepdims=True)
    return centred * lax.rsqrt(variance + 1e-05) * gain_vec + bias_vec


def peer_offsets(n_req, n_head):
    every = [(a, b) for a in range(n_req) for b in range(n_head) if a or b]
    return sorted(every, key=lambda o: (-(o[0] + bin(o[1] >> 1).count("1")), -o[1]))


def flip(index, mask):
    bit = 1
    while bit <= mask:
        if mask & bit:
            index = index + bit - 2 * bit * lax.rem(index // bit, 2)
        bit *= 2
    return index


def pair_kernel(
    n_req,
    n_head,
    hidden_hbm,
    lengths_hbm,
    order_hbm,
    key_hbm,
    value_hbm,
    qkv_hbm,
    out_w_hbm,
    up_hbm,
    bias_up_hbm,
    down_hbm,
    gain_hbm,
    bias_hbm,
    emb_hbm,
    logits_ref,
    key_v,
    value_v,
    qkv_v,
    out_w_v,
    up_v,
    down_v,
    emb_v,
    hidden_ref,
    lengths_ref,
    order_ref,
    bias_up_ref,
    gain_ref,
    bias_ref,
    small_sem,
    load_sem,
    emb_sem,
    bias_v,
    state_v,
    first,
    attn_out,
    attn_in,
    spread,
    mlp_out,
    mlp_in,
    own_out,
    own_in,
    near,
    last,
    end_in,
    end_own_in,
    first_send,
    first_recv,
    pair_send,
    pair_recv,
    attn_send,
    attn_recv,
    spread_send,
    spread_recv,
    mlp_send,
    mlp_recv,
    own_send,
    own_recv,
    near_send,
    near_recv,
    last_send,
    last_recv,
    pass_send,
    pass_recv,
    end_send,
    end_recv,
):
    me_r = lax.axis_index("req")
    me_h = lax.axis_index("head")
    me = me_r * n_head + me_h
    core = lax.rem(me_h, 2)
    chip = me // 2
    partner = (me_r, flip(me_h, 1))
    rows, width = hidden_hbm.shape
    group, heads, head_size, cached = key_v.shape[1:]
    units = up_hbm.shape[2]
    slots = n_req * group
    devices = n_req * n_head
    chips = devices // 2
    part = width // n_head
    offsets = peer_offsets(n_req, n_head)
    everywhere = [(flip(me_r, a), flip(me_h, b)) for a, b in offsets]
    plane = [(me_r, flip(me_h, b)) for a, b in offsets if not a]
    middle = n_req // 2
    owner = (me_r + 1) // middle == 1
    near_owner = me_r // middle
    reach = (0, 1, 2, 1)
    end_offsets = sorted(
        [(a, b) for a, b in offsets if b % 2 == 0], key=lambda o: -(reach[o[0]] + bin(o[1]).count("1"))
    )
    taker = lax.rem((me_r + 1) // middle, 2)
    mine = taker == core
    near_group = jnp.where(me_r < middle, core, n_req - 1 - core)
    far_group = n_req - 1 - near_group

    barrier = pltpu.get_barrier_semaphore()
    for peer in everywhere:
        pl.semaphore_signal(barrier, inc=1, device_id=peer, device_id_type=MESH)

    smalls = [
        pltpu.make_async_copy(source, target, small_sem.at[place])
        for place, (source, target) in enumerate(
            (
                (hidden_hbm, hidden_ref),
                (order_hbm, order_ref),
                (lengths_hbm, lengths_ref),
                (bias_up_hbm, bias_up_ref),
                (gain_hbm, gain_ref),
                (bias_hbm, bias_ref),
            )
        )
    ]
    for copy in smalls:
        copy.start()

    def up_part(ref, layer, which):
        return ref.at[layer, :, pl.ds(which * units, units)]

    def load(layer, which):
        source, target = (
            (qkv_hbm.at[layer], qkv_v.at[layer]),
            (key_hbm.at[layer], key_v.at[layer]),
            (value_hbm.at[layer], value_v.at[layer]),
            (out_w_hbm.at[layer], out_w_v.at[layer]),
            (up_hbm.at[layer], up_part(up_v, layer, 0)),
            (down_hbm.at[layer], up_part(down_v, layer, 0)),
        )[which]
        return pltpu.make_async_copy(source, target, load_sem.at[layer, which])

    emb_load = pltpu.make_async_copy(emb_hbm, emb_v, emb_sem)

    def remote(source, target, sender, receiver, peer):
        return pltpu.make_async_remote_copy(
            src_ref=source,
            dst_ref=target,
            send_sem=sender,
            recv_sem=receiver,
            device_id=peer,
            device_id_type=MESH,
        )

    def wait(sem, ref, count):
        block = ref.at[pl.ds(0, count)]
        pltpu.make_async_copy(block, block, sem).wait()

    def either(held, given):
        pl.when(mine)(held)
        pl.when(jnp.logical_not(mine))(given)

    def pair_copies(layer):
        return (
            remote(up_hbm.at[layer], up_part(up_v, layer, 1), pair_send.at[layer, 0], pair_recv.at[layer, 0], partner),
            remote(
                down_hbm.at[layer], up_part(down_v, layer, 1), pair_send.at[layer, 1], pair_recv.at[layer, 1], partner
            ),
        )

    bias_copy = remote(bias_v.at[0], bias_v.at[1], pair_send.at[LAYERS, 0], pair_recv.at[LAYERS, 0], partner)

    chunks = width // 128
    tile = first.shape[1]
    for copy in smalls:
        copy.wait()
    for layer in range(LAYERS):
        for which in range(6):
            load(layer, which).start()
    emb_load.start()
    hidden = hidden_ref[...].astype(F32)
    pieces = [hidden[:, c * 128 : (c + 1) * 128] for c in range(chunks)]
    if tile > chunks * rows:
        pieces.append(jnp.zeros((tile - chunks * rows, 128), F32))
    first[me] = jnp.concatenate(pieces, axis=0).astype(BF16)
    bias_v[0] = jnp.concatenate(
        [bias_up_ref[...].astype(F32), jnp.zeros((bias_v.shape[1] - LAYERS, units), F32)], axis=0
    )
    for layer in range(LAYERS - 1):
        mlp_in[layer, chip] = jnp.zeros((group, part), BF16)
    for which in range(2):
        end_in[which * chips + chip] = jnp.zeros((group, part), BF16)

    order_row = order_ref[...]
    ids_row = lax.broadcasted_iota(jnp.int32, (group, slots), 0) + me_r * group
    ids_col = lax.broadcasted_iota(jnp.int32, (group, slots), 1)
    order_here = jnp.sum(
        jnp.where(ids_row == ids_col, jnp.broadcast_to(order_row, (group, slots)).astype(F32), 0.0),
        axis=1,
        keepdims=True,
    ).astype(jnp.int32)
    wanted = (order_here // rows) * tile + lax.rem(order_here, rows)
    wide = lax.broadcasted_iota(jnp.int32, (group, devices * tile), 1)
    wanted = jnp.broadcast_to(wanted, (group, devices * tile))
    choose = jnp.concatenate(
        [(wide == wanted + c * rows).astype(F32) for c in range(chunks)], axis=0
    ).astype(BF16)

    square = lax.broadcasted_iota(jnp.int32, (group, group), 0) == lax.broadcasted_iota(
        jnp.int32, (group, group), 1
    )
    limit = jnp.sum(
        jnp.where(square, jnp.broadcast_to(lengths_ref[...], (group, group)).astype(F32), 0.0), axis=1, keepdims=True
    ).astype(jnp.int32)
    limit = jnp.broadcast_to(limit, (group, cached))
    valid = lax.broadcasted_iota(jnp.int32, (group, cached), 1) < limit
    flat = group * head_size
    diagonal = lax.broadcasted_iota(jnp.int32, (group, flat), 0) == (
        lax.broadcasted_iota(jnp.int32, (group, flat), 1) // head_size
    )
    score_scale = head_size ** (-0.5)

    pl.semaphore_wait(barrier, devices - 1)
    for peer in everywhere:
        remote(first.at[me], first.at[me], first_send, first_recv, peer).start()
    for layer in range(LAYERS):
        for copy in pair_copies(layer):
            copy.start()
    bias_copy.start()
    wait(first_recv, first, devices - 1)
    chosen = jnp.dot(choose, first[...].reshape(devices * tile, 128), preferred_element_type=F32)
    state = jnp.concatenate([chosen[c * group : (c + 1) * group] for c in range(chunks)], axis=1)
    for head in range(n_head):
        state_v[head] = state[:, head * part : (head + 1) * part].astype(BF16)

    def joined(ref, lead):
        return jnp.concatenate([ref[lead + (head,)] for head in range(n_head)], axis=1)

    def layer_step(layer, carry):
        state = joined(state_v, ())
        load(layer, 0).wait()
        attn = jnp.zeros((group, width), F32)
        parts = []
        for head in range(heads):
            projected = (
                lax.dot_general(state, qkv_v[layer, head], NT, preferred_element_type=F32).astype(BF16).astype(F32)
            )
            parts.append(
                (
                    projected[:, :head_size],
                    projected[:, head_size : 2 * head_size],
                    projected[:, 2 * head_size :],
                )
            )
        load(layer, 1).wait()
        expos = []
        for head in range(heads):
            query, own_key, own_value = parts[head]
            tiled = jnp.where(diagonal, jnp.concatenate([query] * group, axis=1), 0.0).astype(BF16)
            keys = key_v[layer, :, head].reshape(flat, cached)
            scores = jnp.dot(tiled, keys, preferred_element_type=F32) * score_scale
            scores = jnp.where(valid, scores, -jnp.inf)
            own = jnp.sum(query * own_key, axis=-1, keepdims=True) * score_scale
            row_max = jnp.maximum(jnp.max(scores, axis=-1, keepdims=True), own)
            expo = jnp.exp(scores - row_max)
            own_exp = jnp.exp(own - row_max)
            denom = jnp.sum(expo, axis=-1, keepdims=True) + own_exp
            expos.append((expo.astype(BF16), own_exp.astype(BF16).astype(F32), denom))
        load(layer, 2).wait()
        load(layer, 3).wait()
        for head in range(heads):
            expo, own_exp, denom = expos[head]
            values = value_v[layer, :, head].reshape(flat, cached)
            every = lax.dot_general(expo, values, NT, preferred_element_type=F32)
            every = jnp.where(diagonal, every, 0.0)
            lanes = 2 * head_size
            folded = every[:, :lanes]
            for block in range(1, group // 2):
                folded += every[:, block * lanes : (block + 1) * lanes]
            mixed = folded[:, :head_size] + folded[:, head_size:] + own_exp * parts[head][2]
            head_out = (mixed / denom).astype(BF16)
            attn += jnp.dot(head_out, out_w_v[layer, head], preferred_element_type=F32)
        for head in range(n_head):
            attn_out[layer, head] = attn[:, head * part : (head + 1) * part].astype(BF16)
        for peer in plane:
            remote(
                attn_out.at[layer, peer[1]], attn_in.at[layer, me_h], attn_send.at[layer], attn_recv.at[layer], peer
            ).start()
        attn_in[layer, me_h] = attn_out[layer, me_h]
        wait(attn_recv.at[layer], attn_in.at[layer], n_head - 1)
        total = attn_in[layer, 0].astype(F32)
        for head in range(1, n_head):
            total += attn_in[layer, head].astype(F32)
        spread[layer, me_r, me_h] = (total + state_v[me_h].astype(F32)).astype(BF16)

        def spread_copy(a, b):
            base = flip(me_h, b)
            peer = (flip(me_r, a), base - lax.rem(base, 2) + taker)
            block = spread.at[layer, me_r, me_h]
            return remote(block, block, spread_send.at[layer], spread_recv.at[layer, me_r], peer)

        for a, b in offsets:
            if b % 2 == 0:
                spread_copy(a, b).start()

        @pl.when(jnp.logical_not(mine))
        def _():
            spread_copy(0, 0).start()

        gains, biases = gain_ref[layer], bias_ref[layer]
        bias_rows = []
        for source in range(2):
            bias_up = bias_v[source]
            bias_row = bias_up[0:1]
            for other in range(1, LAYERS):
                bias_row = jnp.where(layer == other, bias_up[other : other + 1], bias_row)
            bias_rows.append(bias_row)
        bias_row = jnp.concatenate(bias_rows, axis=1)

        def mlp_copy(which, block, b):
            peer = (block, flip(me_h, b))
            return remote(
                mlp_out.at[layer, which, peer[1]], mlp_in.at[layer, chip], mlp_send.at[layer], mlp_recv.at[layer], peer
            )

        def end_copy(which, block, b):
            peer = (jnp.where(block < middle, middle - 1, middle), flip(me_h, b))
            return remote(
                mlp_out.at[layer, which, peer[1]],
                end_in.at[lax.rem(block, 2) * chips + chip],
                end_send,
                end_recv,
                peer,
            )

        def own_copy():
            return remote(own_out.at[layer, partner[1]], own_in.at[layer], own_send.at[layer], own_recv.at[layer], partner)

        load(layer, 4).wait()
        load(layer, 5).wait()
        for copy in pair_copies(layer):
            copy.wait_recv()
        either(
            lambda: wait(spread_recv.at[layer, near_group], spread.at[layer, 0], n_head - 1),
            lambda: wait(spread_recv.at[layer, near_group], spread.at[layer, 0], n_head),
        )
        wait(spread_recv.at[layer, far_group], spread.at[layer, 0], n_head)
        before = jnp.concatenate(
            [
                jnp.concatenate([spread[layer, block, head] for head in range(n_head)], axis=1)
                for block in (near_group, far_group)
            ],
            axis=0,
        ).astype(F32)
        normed = layer_norm(before, gains[0:1], biases[0:1]).astype(BF16)
        pre_act = jnp.dot(normed, up_v[layer], preferred_element_type=F32) + bias_row
        hidden = (0.5 * pre_act * (1.0 + lax.erf(pre_act * 0.7071067811865476))).astype(BF16)
        mlp = lax.dot_general(hidden, down_v[layer], NT, preferred_element_type=F32)
        for which in (1, 0):
            for head in range(n_head):
                mlp_out[layer, which, head] = mlp[
                    which * group : (which + 1) * group, head * part : (head + 1) * part
                ].astype(BF16)
        if layer == LAYERS - 1:
            return finish(layer, mlp, normed, end_copy)
        whole = mlp[:group] + normed[:group].astype(F32)
        for head in range(n_head):
            own_out[layer, head] = whole[:, head * part : (head + 1) * part]
        for b in range(n_head - 1, -1, -1):
            mlp_copy(1, far_group, b).start()
        for b in range(n_head - 1, 1, -1):
            mlp_copy(0, near_group, b).start()

        @pl.when(mine)
        def _():
            own_copy().start()
            own_in[layer] = own_out[layer, me_h]

        @pl.when(jnp.logical_not(mine))
        def _():
            for b in range(2):
                mlp_copy(0, near_group, b).start()
            own_copy().wait_recv()

        wait(mlp_recv.at[layer], mlp_in.at[layer], chips - 1)
        total = own_in[layer]
        for source in range(chips):
            total += mlp_in[layer, source].astype(F32)
        near[layer, me_h] = total.astype(BF16)
        for peer in plane:
            block = near.at[layer, me_h]
            remote(block, block, near_send.at[layer], near_recv.at[layer], peer).start()
        wait(near_recv.at[layer], near.at[layer], n_head - 1)
        fresh = joined(near, (layer,)).astype(F32)
        fresh = layer_norm(fresh, gains[1:2], biases[1:2]).astype(BF16)
        for head in range(n_head):
            state_v[head] = fresh[:, head * part : (head + 1) * part]
        return carry

    def finish(layer, mlp, normed, end_copy):
        whole = mlp[:group] + normed[:group].astype(F32)
        for b in range(n_head - 1, -1, -1):
            end_copy(1, far_group, b).start()
        for b in range(n_head - 1, 1, -1):
            end_copy(0, near_group, b).start()
        for head in range(n_head):
            own_out[layer, head] = whole[:, head * part : (head + 1) * part]

        @pl.when(jnp.logical_not(owner))
        def _():
            for b in range(2):
                end_copy(0, near_group, b).start()

        @pl.when(owner)
        def _():
            end_own().start()
            end_own_in[lax.rem(near_group, 2)] = own_out[layer, me_h]
            end_own().wait_recv()
            wait(end_recv, end_in, 2 * chips - 2)
            for which in range(2):
                total = end_own_in[which]
                for source in range(chips):
                    total += end_in[which * chips + source].astype(F32)
                last[near_owner, me_h, pl.ds(which * group, group)] = total.astype(BF16)
            block = last.at[near_owner, me_h]
            for a, b in end_offsets:
                peer = (flip(me_r, a), flip(me_h, b + 1))
                remote(block, block, last_send, last_recv.at[near_owner], peer).start()
            remote(block, block, last_send, pass_recv.at[near_owner], partner).start()

    def end_own():
        return remote(
            own_out.at[LAYERS - 1, partner[1]],
            end_own_in.at[lax.rem(near_group, 2)],
            own_send.at[LAYERS - 1],
            own_recv.at[LAYERS - 1],
            partner,
        )

    def forward(plane_of, b):
        block = last.at[plane_of, flip(me_h, b + 1)]
        remote(block, block, pass_send, pass_recv.at[plane_of], partner).start()

    bias_copy.wait_recv()
    for layer in range(LAYERS):
        layer_step(layer, 0)

    @pl.when(owner)
    def _():
        wait(last_recv.at[near_owner], last.at[0], n_head // 2 - 1)
        for b in range(2, n_head, 2):
            forward(near_owner, b)

    @pl.when(jnp.logical_not(owner))
    def _():
        wait(last_recv.at[near_owner], last.at[0], n_head // 2)
        for b in range(0, n_head, 2):
            forward(near_owner, b)

    wait(last_recv.at[1 - near_owner], last.at[0], n_head // 2)
    for b in range(0, n_head, 2):
        forward(1 - near_owner, b)
    pick = (
        (
            lax.broadcasted_iota(jnp.int32, (slots, slots), 0)
            == jnp.broadcast_to(order_row, (slots, slots))
        )
        .astype(F32)
        .astype(BF16)
    )
    emb_load.wait()
    wait(first_send, first, devices - 1)
    bias_copy.wait_send()
    for layer in range(LAYERS):
        for copy in pair_copies(layer):
            copy.wait_send()
        wait(attn_send.at[layer], attn_in.at[layer], n_head - 1)
        @pl.when(mine)
        def _():
            wait(spread_send.at[layer], mlp_in.at[0], chips - 1)

        @pl.when(jnp.logical_not(mine))
        def _():
            wait(spread_send.at[layer], mlp_in.at[0], chips)

        if layer < LAYERS - 1:
            wait(near_send.at[layer], near.at[layer], n_head - 1)

            @pl.when(mine)
            def _():
                wait(mlp_send.at[layer], mlp_in.at[0], 2 * n_head - 2)
                remote(
                    own_out.at[layer, 0], own_in.at[layer], own_send.at[layer], own_recv.at[layer], partner
                ).wait_send()

            @pl.when(jnp.logical_not(mine))
            def _():
                wait(mlp_send.at[layer], mlp_in.at[0], 2 * n_head)

    @pl.when(owner)
    def _():
        wait(end_send, end_in, 2 * n_head - 2)
        end_own().wait_send()

    @pl.when(jnp.logical_not(owner))
    def _():
        wait(end_send, end_in, 2 * n_head)

    for plane_of in range(2):
        wait(pass_recv.at[plane_of], last.at[0], n_head // 2)
    before = jnp.concatenate(
        [jnp.concatenate([last[plane_of, head] for head in range(n_head)], axis=1) for plane_of in range(2)],
        axis=0,
    ).astype(F32)
    gains, biases = gain_ref[LAYERS - 1], bias_ref[LAYERS - 1]
    final = layer_norm(before, gains[1:2], biases[1:2]).astype(BF16)
    ordered = jnp.dot(pick, final, preferred_element_type=F32).astype(BF16)
    logits_ref[...] = lax.dot_general(ordered, emb_v[...], NT, preferred_element_type=F32)

    @pl.when(owner)
    def _():
        wait(last_send, last, 2)
        wait(pass_send, last.at[0], n_head - 1)

    @pl.when(jnp.logical_not(owner))
    def _():
        wait(pass_send, last.at[0], n_head)


def kernel(
    n_req,
    n_head,
    hidden_ref,
    lengths_ref,
    order_ref,
    key_hbm,
    value_hbm,
    qkv_hbm,
    out_w_hbm,
    up_hbm,
    bias_up_ref,
    down_hbm,
    gain_ref,
    bias_ref,
    emb_hbm,
    logits_ref,
    key_v,
    value_v,
    qkv_v,
    out_w_v,
    up_v,
    down_v,
    emb_v,
    load_sem,
    emb_sem,
    state_v,
    normed_v,
    first,
    attn_out,
    attn_in,
    spread,
    mlp_out,
    mlp_in,
    near,
    send_sem,
    recv_sem,
):
    me_r = lax.axis_index("req")
    me_h = lax.axis_index("head")
    me = me_r * n_head + me_h
    rows, width = hidden_ref.shape
    group, heads, head_size, cached = key_v.shape[1:]
    slots = n_req * group
    devices = n_req * n_head
    part = width // n_head
    offsets = peer_offsets(n_req, n_head)
    everywhere = [(flip(me_r, a), flip(me_h, b)) for a, b in offsets]
    plane = [(me_r, flip(me_h, b)) for a, b in offsets if not a]

    barrier = pltpu.get_barrier_semaphore()
    for peer in everywhere:
        pl.semaphore_signal(barrier, inc=1, device_id=peer, device_id_type=MESH)

    pairs = (
        (qkv_hbm, qkv_v),
        (key_hbm, key_v),
        (value_hbm, value_v),
        (out_w_hbm, out_w_v),
        (up_hbm, up_v),
        (down_hbm, down_v),
    )

    def load(layer, which):
        source, target = pairs[which]
        return pltpu.make_async_copy(source.at[layer], target.at[layer], load_sem.at[layer, which])

    for layer in range(LAYERS):
        for which in range(len(pairs)):
            load(layer, which).start()
    emb_load = pltpu.make_async_copy(emb_hbm, emb_v, emb_sem)
    emb_load.start()

    def send(turn, source, target, peers):
        for peer in peers:
            pltpu.make_async_remote_copy(
                src_ref=source(peer),
                dst_ref=target,
                send_sem=send_sem.at[turn],
                recv_sem=recv_sem.at[turn],
                device_id=peer,
                device_id_type=MESH,
            ).start()

    def wait(sem, turn, ref, count):
        block = ref.at[pl.ds(0, count)]
        pltpu.make_async_copy(block, block, sem.at[turn]).wait()

    chunks = width // 128
    tile = first.shape[1]
    hidden = hidden_ref[...].astype(F32)
    pieces = [hidden[:, c * 128 : (c + 1) * 128] for c in range(chunks)]
    if tile > chunks * rows:
        pieces.append(jnp.zeros((tile - chunks * rows, 128), F32))
    first[me] = jnp.concatenate(pieces, axis=0).astype(BF16)

    order_row = order_ref[...]
    ids_row = lax.broadcasted_iota(jnp.int32, (group, slots), 0) + me_r * group
    ids_col = lax.broadcasted_iota(jnp.int32, (group, slots), 1)
    order_here = jnp.sum(
        jnp.where(ids_row == ids_col, jnp.broadcast_to(order_row, (group, slots)).astype(F32), 0.0),
        axis=1,
        keepdims=True,
    ).astype(jnp.int32)
    wanted = (order_here // rows) * tile + lax.rem(order_here, rows)
    wide = lax.broadcasted_iota(jnp.int32, (group, devices * tile), 1)
    wanted = jnp.broadcast_to(wanted, (group, devices * tile))
    choose = jnp.concatenate(
        [(wide == wanted + c * rows).astype(F32) for c in range(chunks)], axis=0
    ).astype(BF16)

    square = lax.broadcasted_iota(jnp.int32, (group, group), 0) == lax.broadcasted_iota(
        jnp.int32, (group, group), 1
    )
    limit = jnp.sum(
        jnp.where(square, jnp.broadcast_to(lengths_ref[...], (group, group)).astype(F32), 0.0), axis=1, keepdims=True
    ).astype(jnp.int32)
    limit = jnp.broadcast_to(limit, (group, cached))
    valid = lax.broadcasted_iota(jnp.int32, (group, cached), 1) < limit
    flat = group * head_size
    diagonal = lax.broadcasted_iota(jnp.int32, (group, flat), 0) == (
        lax.broadcasted_iota(jnp.int32, (group, flat), 1) // head_size
    )
    score_scale = head_size ** (-0.5)

    pl.semaphore_wait(barrier, devices - 1)
    send(0, lambda peer: first.at[me], first.at[me], everywhere)
    wait(recv_sem, 0, first, devices - 1)
    chosen = jnp.dot(choose, first[...].reshape(devices * tile, 128), preferred_element_type=F32)
    state = jnp.concatenate([chosen[c * group : (c + 1) * group] for c in range(chunks)], axis=1)
    for head in range(n_head):
        state_v[head] = state[:, head * part : (head + 1) * part].astype(BF16)

    def joined(ref, lead):
        return jnp.concatenate([ref[lead + (head,)] for head in range(n_head)], axis=1)

    def layer_step(layer, carry):
        attn_turn, spread_turn, mlp_turn, near_turn = 1 + 4 * layer, 2 + 4 * layer, 3 + 4 * layer, 4 + 4 * layer
        state = joined(state_v, ())
        load(layer, 0).wait()
        attn = jnp.zeros((group, width), F32)
        parts = []
        for head in range(heads):
            projected = (
                lax.dot_general(state, qkv_v[layer, head], NT, preferred_element_type=F32).astype(BF16).astype(F32)
            )
            parts.append(
                (
                    projected[:, :head_size],
                    projected[:, head_size : 2 * head_size],
                    projected[:, 2 * head_size :],
                )
            )
        load(layer, 1).wait()
        expos = []
        for head in range(heads):
            query, own_key, own_value = parts[head]
            tiled = jnp.where(diagonal, jnp.concatenate([query] * group, axis=1), 0.0).astype(BF16)
            keys = key_v[layer, :, head].reshape(flat, cached)
            scores = jnp.dot(tiled, keys, preferred_element_type=F32) * score_scale
            scores = jnp.where(valid, scores, -jnp.inf)
            own = jnp.sum(query * own_key, axis=-1, keepdims=True) * score_scale
            row_max = jnp.maximum(jnp.max(scores, axis=-1, keepdims=True), own)
            expo = jnp.exp(scores - row_max)
            own_exp = jnp.exp(own - row_max)
            denom = jnp.sum(expo, axis=-1, keepdims=True) + own_exp
            expos.append((expo.astype(BF16), own_exp.astype(BF16).astype(F32), denom))
        load(layer, 2).wait()
        load(layer, 3).wait()
        for head in range(heads):
            expo, own_exp, denom = expos[head]
            values = value_v[layer, :, head].reshape(flat, cached)
            every = lax.dot_general(expo, values, NT, preferred_element_type=F32)
            every = jnp.where(diagonal, every, 0.0)
            mixed = every[:, :head_size]
            for block in range(1, group):
                mixed += every[:, block * head_size : (block + 1) * head_size]
            mixed += own_exp * parts[head][2]
            head_out = (mixed / denom).astype(BF16)
            attn += jnp.dot(head_out, out_w_v[layer, head], preferred_element_type=F32)
        for head in range(n_head):
            attn_out[layer, head] = attn[:, head * part : (head + 1) * part].astype(BF16)
        send(attn_turn, lambda peer: attn_out.at[layer, peer[1]], attn_in.at[layer, me_h], plane)
        attn_in[layer, me_h] = attn_out[layer, me_h]
        wait(recv_sem, attn_turn, attn_in.at[layer], n_head - 1)
        total = attn_in[layer, 0].astype(F32)
        for head in range(1, n_head):
            total += attn_in[layer, head].astype(F32)
        spread[layer, me] = (total + state_v[me_h].astype(F32)).astype(BF16)
        send(spread_turn, lambda peer: spread.at[layer, me], spread.at[layer, me], everywhere)
        gains, biases = gain_ref[layer], bias_ref[layer]
        bias_up = bias_up_ref[...].astype(F32)
        bias_row = bias_up[0:1]
        for other in range(1, LAYERS):
            bias_row = jnp.where(layer == other, bias_up[other : other + 1], bias_row)
        load(layer, 4).wait()
        load(layer, 5).wait()
        wait(recv_sem, spread_turn, spread.at[layer], devices - 1)
        before = jnp.concatenate(
            [
                jnp.concatenate([spread[layer, req * n_head + head] for head in range(n_head)], axis=1)
                for req in range(n_req)
            ],
            axis=0,
        ).astype(F32)
        normed = layer_norm(before, gains[0:1], biases[0:1]).astype(BF16)
        for req in range(n_req):
            for head in range(n_head):
                normed_v[req * n_head + head] = normed[
                    req * group : (req + 1) * group, head * part : (head + 1) * part
                ]
        pre_act = jnp.dot(normed, up_v[layer], preferred_element_type=F32) + bias_row
        hidden = (0.5 * pre_act * (1.0 + lax.erf(pre_act * 0.7071067811865476))).astype(BF16)
        mlp = lax.dot_general(hidden, down_v[layer], NT, preferred_element_type=F32).astype(BF16)
        for req in range(n_req):
            for head in range(n_head):
                mlp_out[layer, req * n_head + head] = mlp[
                    req * group : (req + 1) * group, head * part : (head + 1) * part
                ]
        send(mlp_turn, lambda peer: mlp_out.at[layer, peer[0] * n_head + peer[1]], mlp_in.at[layer, me], everywhere)
        mlp_in[layer, me] = mlp_out[layer, me]
        wait(recv_sem, mlp_turn, mlp_in.at[layer], devices - 1)
        total = mlp_in[layer, 0].astype(F32)
        for device in range(1, devices):
            total += mlp_in[layer, device].astype(F32)
        after = (total + normed_v[me].astype(F32)).astype(BF16)

        @pl.when(layer < LAYERS - 1)
        def _():
            near[layer, me_h] = after
            send(near_turn, lambda peer: near.at[layer, me_h], near.at[layer, me_h], plane)
            wait(recv_sem, near_turn, near.at[layer], n_head - 1)
            fresh = joined(near, (layer,)).astype(F32)
            fresh = layer_norm(fresh, gains[1:2], biases[1:2]).astype(BF16)
            for head in range(n_head):
                state_v[head] = fresh[:, head * part : (head + 1) * part]

        @pl.when(layer == LAYERS - 1)
        def _():
            spread[LAYERS, me] = after

        return carry

    lax.fori_loop(0, LAYERS, layer_step, 0)
    last = 4 * LAYERS
    send(last, lambda peer: spread.at[LAYERS, me], spread.at[LAYERS, me], everywhere)
    pick = (
        (
            lax.broadcasted_iota(jnp.int32, (slots, slots), 0)
            == jnp.broadcast_to(order_row, (slots, slots))
        )
        .astype(F32)
        .astype(BF16)
    )
    emb_load.wait()
    wait(send_sem, 0, first, devices - 1)
    for layer in range(LAYERS):
        wait(send_sem, 1 + 4 * layer, attn_in.at[layer], n_head - 1)
        wait(send_sem, 2 + 4 * layer, spread.at[layer], devices - 1)
        wait(send_sem, 3 + 4 * layer, mlp_in.at[layer], devices - 1)
        if layer < LAYERS - 1:
            wait(send_sem, 4 + 4 * layer, near.at[layer], n_head - 1)
    wait(recv_sem, last, spread.at[LAYERS], devices - 1)
    before = jnp.concatenate(
        [
            jnp.concatenate([spread[LAYERS, req * n_head + head] for head in range(n_head)], axis=1)
            for req in range(n_req)
        ],
        axis=0,
    ).astype(F32)
    gains, biases = gain_ref[LAYERS - 1], bias_ref[LAYERS - 1]
    final = layer_norm(before, gains[1:2], biases[1:2]).astype(BF16)
    ordered = jnp.dot(pick, final, preferred_element_type=F32).astype(BF16)
    logits_ref[...] = lax.dot_general(ordered, emb_v[...], NT, preferred_element_type=F32)
    wait(send_sem, last, spread.at[LAYERS], devices - 1)


def body(n_req, n_head, *args):
    (hidden_in, lengths, request_order, key_cache, value_cache, w_qkv, w_out, w_up, bias_up, w_down) = args[:10]
    norm_gain, norm_bias, embedding = args[10:]
    group = lengths.shape[0]
    width = hidden_in.shape[1]
    w_qkv = jnp.swapaxes(w_qkv, 2, 3)
    slots = request_order.shape[0]
    devices = n_req * n_head
    part = width // n_head
    tile = max(16, hidden_in.shape[0] * width // 128)
    vmem = pl.BlockSpec(memory_space=pltpu.VMEM)
    hbm = pl.BlockSpec(memory_space=pltpu.HBM)
    dma = pltpu.SemaphoreType.DMA
    pin = lambda array: pltpu.with_memory_space_constraint(array, pltpu.HBM)
    held = [key_cache, value_cache, w_qkv, w_out, w_up, w_down, embedding]
    return pl.pallas_call(
        functools.partial(kernel, n_req, n_head),
        out_shape=jax.ShapeDtypeStruct((slots, embedding.shape[0]), F32),
        in_specs=[vmem] * 3 + [hbm] * 5 + [vmem, hbm, vmem, vmem, hbm],
        out_specs=vmem,
        scratch_shapes=[pltpu.VMEM(array.shape, array.dtype) for array in held]
        + [
            dma((LAYERS, 6)),
            dma,
            pltpu.VMEM((n_head, group, part), BF16),
            pltpu.VMEM((devices, group, part), BF16),
            pltpu.VMEM((devices, tile, 128), BF16),
            pltpu.VMEM((LAYERS, n_head, group, part), BF16),
            pltpu.VMEM((LAYERS, n_head, group, part), BF16),
            pltpu.VMEM((1 + LAYERS, devices, group, part), BF16),
            pltpu.VMEM((LAYERS, devices, group, part), BF16),
            pltpu.VMEM((LAYERS, devices, group, part), BF16),
            pltpu.VMEM((LAYERS, n_head, group, part), BF16),
            dma((1 + 4 * LAYERS,)),
            dma((1 + 4 * LAYERS,)),
        ],
        compiler_params=pltpu.CompilerParams(
            collective_id=0, has_side_effects=True, vmem_limit_bytes=40 * 1024 * 1024
        ),
    )(
        pin(hidden_in),
        pin(lengths.reshape(1, group)),
        pin(request_order.reshape(1, slots)),
        pin(key_cache),
        pin(value_cache),
        pin(w_qkv),
        pin(w_out),
        pin(w_up),
        pin(bias_up),
        pin(w_down),
        pin(norm_gain),
        pin(norm_bias),
        pin(embedding),
    )


def pair_body(n_req, n_head, *args):
    (hidden_in, lengths, request_order, key_cache, value_cache, w_qkv, w_out, w_up, bias_up, w_down) = args[:10]
    norm_gain, norm_bias, embedding = args[10:]
    group = lengths.shape[0]
    width = hidden_in.shape[1]
    w_qkv = jnp.swapaxes(w_qkv, 2, 3)
    slots = request_order.shape[0]
    devices = n_req * n_head
    part = width // n_head
    tile = max(16, hidden_in.shape[0] * width // 128)
    vmem = pl.BlockSpec(memory_space=pltpu.VMEM)
    hbm = pl.BlockSpec(memory_space=pltpu.HBM)
    dma = pltpu.SemaphoreType.DMA
    pin = lambda array: pltpu.with_memory_space_constraint(array, pltpu.HBM)
    units = w_up.shape[2]
    chips = devices // 2
    sizes = [key_cache.shape, value_cache.shape, w_qkv.shape, w_out.shape]
    sizes += [(LAYERS, width, 2 * units)] * 2 + [embedding.shape]
    block = (group, part)
    return pl.pallas_call(
        functools.partial(pair_kernel, n_req, n_head),
        out_shape=jax.ShapeDtypeStruct((slots, embedding.shape[0]), F32),
        in_specs=[hbm] * 13,
        out_specs=vmem,
        scratch_shapes=[pltpu.VMEM(size, BF16) for size in sizes]
        + [
            pltpu.VMEM(hidden_in.shape, BF16),
            pltpu.VMEM((1, group), jnp.int32),
            pltpu.VMEM((1, slots), jnp.int32),
            pltpu.VMEM(bias_up.shape, BF16),
            pltpu.VMEM(norm_gain.shape, F32),
            pltpu.VMEM(norm_bias.shape, F32),
            dma((6,)),
            dma((LAYERS, 6)),
            dma,
            pltpu.VMEM((2, 8, units), F32),
            pltpu.VMEM((n_head,) + block, BF16),
            pltpu.VMEM((devices, tile, 128), BF16),
            pltpu.VMEM((LAYERS, n_head) + block, BF16),
            pltpu.VMEM((LAYERS, n_head) + block, BF16),
            pltpu.VMEM((LAYERS, n_req, n_head) + block, BF16),
            pltpu.VMEM((LAYERS, 2, n_head) + block, BF16),
            pltpu.VMEM((LAYERS, chips) + block, BF16),
            pltpu.VMEM((LAYERS, n_head) + block, F32),
            pltpu.VMEM((LAYERS,) + block, F32),
            pltpu.VMEM((LAYERS, n_head) + block, BF16),
            pltpu.VMEM((2, n_head, 2 * group, part), BF16),
            pltpu.VMEM((2 * chips,) + block, BF16),
            pltpu.VMEM((2,) + block, F32),
            dma,
            dma,
            dma((LAYERS + 1, 2)),
            dma((LAYERS + 1, 2)),
            dma((LAYERS,)),
            dma((LAYERS,)),
            dma((LAYERS,)),
            dma((LAYERS, n_req)),
            dma((LAYERS,)),
            dma((LAYERS,)),
            dma((LAYERS,)),
            dma((LAYERS,)),
            dma((LAYERS,)),
            dma((LAYERS,)),
            dma,
            dma((2,)),
            dma,
            dma((2,)),
            dma,
            dma,
        ],
        compiler_params=pltpu.CompilerParams(
            collective_id=0, has_side_effects=True, vmem_limit_bytes=40 * 1024 * 1024
        ),
    )(
        pin(hidden_in),
        pin(lengths.reshape(1, group)),
        pin(request_order.reshape(1, slots)),
        pin(key_cache),
        pin(value_cache),
        pin(w_qkv),
        pin(w_out),
        pin(w_up),
        pin(bias_up),
        pin(w_down),
        pin(norm_gain),
        pin(norm_bias),
        pin(embedding),
    )


def solution(mesh):
    placed = (
        P(("req", "head"), None),
        P("req"),
        P(),
        P(None, "req", "head", None, None),
        P(None, "req", "head", None, None),
        P(None, "head", None, None),
        P(None, "head", None, None),
        P(None, None, ("req", "head")),
        P(None, ("req", "head")),
        P(None, None, ("req", "head")),
        P(),
        P(),
        P(("req", "head"), None),
    )
    inner = pair_body if (mesh.shape["req"], mesh.shape["head"]) == (4, 8) else body
    return jax.shard_map(
        functools.partial(inner, mesh.shape["req"], mesh.shape["head"]),
        mesh=mesh,
        in_specs=placed,
        out_specs=P(None, ("req", "head")),
        check_vma=False,
    )
```

```python
import functools

import jax
import jax.numpy as jnp
from jax import lax
from jax.experimental import pallas as pl
from jax.experimental.pallas import tpu as pltpu
from jax.sharding import PartitionSpec as P

LAYERS = 2
MESH = pl.DeviceIdType.MESH
F32 = jnp.float32
BF16 = jnp.bfloat16
NT = (((1,), (1,)), ((), ()))


def layer_norm(values, gain_vec, bias_vec):
    average = jnp.mean(values, axis=-1, keepdims=True)
    centred = values - average
    variance = jnp.mean(centred * centred, axis=-1, keepdims=True)
    return centred * lax.rsqrt(variance + 1e-05) * gain_vec + bias_vec


def quick_norm(values, gain_vec, bias_vec):
    average = jnp.mean(values, axis=-1, keepdims=True)
    square = jnp.mean(values * values, axis=-1, keepdims=True)
    scale = lax.rsqrt(jnp.maximum(square - average * average, 0.0) + 1e-05)
    return (values - average) * scale * gain_vec + bias_vec


def peer_offsets(n_req, n_head):
    every = [(a, b) for a in range(n_req) for b in range(n_head) if a or b]
    return sorted(every, key=lambda o: (-(o[0] + bin(o[1] >> 1).count("1")), -o[1]))


def flip(index, mask):
    bit = 1
    while bit <= mask:
        if mask & bit:
            index = index + bit - 2 * bit * lax.rem(index // bit, 2)
        bit *= 2
    return index


def pair_kernel(
    n_req,
    n_head,
    hidden_hbm,
    lengths_hbm,
    order_hbm,
    key_hbm,
    value_hbm,
    qkv_hbm,
    out_w_hbm,
    up_hbm,
    bias_up_hbm,
    down_hbm,
    gain_hbm,
    bias_hbm,
    emb_hbm,
    logits_ref,
    key_v,
    value_v,
    qkv_v,
    out_w_v,
    up_v,
    down_v,
    emb_v,
    hidden_ref,
    lengths_ref,
    order_ref,
    bias_up_ref,
    gain_ref,
    bias_ref,
    small_sem,
    load_sem,
    emb_sem,
    bias_v,
    state_v,
    first,
    attn_out,
    attn_in,
    spread,
    mlp_out,
    mlp_in,
    own_out,
    own_in,
    near,
    last,
    end_in,
    end_own_in,
    first_send,
    first_recv,
    pair_send,
    pair_recv,
    attn_send,
    attn_recv,
    spread_send,
    spread_recv,
    mlp_send,
    mlp_recv,
    own_send,
    own_recv,
    near_send,
    near_recv,
    last_send,
    last_recv,
    pass_send,
    pass_recv,
    end_send,
    end_recv,
    value_t,
    emb_t,
):
    me_r = lax.axis_index("req")
    me_h = lax.axis_index("head")
    me = me_r * n_head + me_h
    core = lax.rem(me_h, 2)
    chip = me // 2
    partner = (me_r, flip(me_h, 1))
    rows, width = hidden_hbm.shape
    group, heads, head_size, cached = key_v.shape[1:]
    units = up_hbm.shape[2]
    slots = n_req * group
    devices = n_req * n_head
    chips = devices // 2
    part = width // n_head
    offsets = peer_offsets(n_req, n_head)
    everywhere = [(flip(me_r, a), flip(me_h, b)) for a, b in offsets]
    plane = [(me_r, flip(me_h, b)) for a, b in offsets if not a]
    middle = n_req // 2
    owner = (me_r + 1) // middle == 1
    near_owner = me_r // middle
    reach = (0, 1, 2, 1)
    end_offsets = sorted(
        [(a, b) for a, b in offsets if b % 2 == 0], key=lambda o: -(reach[o[0]] + bin(o[1]).count("1"))
    )
    taker = lax.rem((me_r + 1) // middle, 2)
    mine = taker == core
    near_group = jnp.where(me_r < middle, core, n_req - 1 - core)
    far_group = n_req - 1 - near_group

    barrier = pltpu.get_barrier_semaphore()
    for peer in everywhere:
        pl.semaphore_signal(barrier, inc=1, device_id=peer, device_id_type=MESH)

    smalls = [
        pltpu.make_async_copy(source, target, small_sem.at[place])
        for place, (source, target) in enumerate(
            (
                (hidden_hbm, hidden_ref),
                (order_hbm, order_ref),
                (lengths_hbm, lengths_ref),
                (bias_up_hbm, bias_up_ref),
                (gain_hbm, gain_ref),
                (bias_hbm, bias_ref),
            )
        )
    ]
    for copy in smalls:
        copy.start()

    def up_part(ref, layer, which):
        return ref.at[layer, :, pl.ds(which * units, units)]

    def load(layer, which):
        source, target = (
            (qkv_hbm.at[layer], qkv_v.at[layer]),
            (key_hbm.at[layer], key_v.at[layer]),
            (value_hbm.at[layer], value_v.at[layer]),
            (out_w_hbm.at[layer], out_w_v.at[layer]),
            (up_hbm.at[layer], up_part(up_v, layer, 0)),
            (down_hbm.at[layer], up_part(down_v, layer, 0)),
        )[which]
        return pltpu.make_async_copy(source, target, load_sem.at[layer, which])

    emb_load = pltpu.make_async_copy(emb_hbm, emb_v, emb_sem)

    def remote(source, target, sender, receiver, peer):
        return pltpu.make_async_remote_copy(
            src_ref=source,
            dst_ref=target,
            send_sem=sender,
            recv_sem=receiver,
            device_id=peer,
            device_id_type=MESH,
        )

    def wait(sem, ref, count):
        block = ref.at[pl.ds(0, count)]
        pltpu.make_async_copy(block, block, sem).wait()

    def either(held, given):
        pl.when(mine)(held)
        pl.when(jnp.logical_not(mine))(given)

    def pair_copies(layer):
        return (
            remote(up_hbm.at[layer], up_part(up_v, layer, 1), pair_send.at[layer, 0], pair_recv.at[layer, 0], partner),
            remote(
                down_hbm.at[layer], up_part(down_v, layer, 1), pair_send.at[layer, 1], pair_recv.at[layer, 1], partner
            ),
        )

    bias_copy = remote(bias_v.at[0], bias_v.at[1], pair_send.at[LAYERS, 0], pair_recv.at[LAYERS, 0], partner)

    chunks = width // 128
    tile = first.shape[1]
    for copy in smalls:
        copy.wait()
    for layer in range(LAYERS):
        for which in range(6):
            load(layer, which).start()
    emb_load.start()
    hidden = hidden_ref[...].astype(F32)
    pieces = [hidden[:, c * 128 : (c + 1) * 128] for c in range(chunks)]
    if tile > chunks * rows:
        pieces.append(jnp.zeros((tile - chunks * rows, 128), F32))
    first[me] = jnp.concatenate(pieces, axis=0).astype(BF16)
    bias_v[0] = jnp.concatenate(
        [bias_up_ref[...].astype(F32), jnp.zeros((bias_v.shape[1] - LAYERS, units), F32)], axis=0
    )
    for layer in range(LAYERS - 1):
        mlp_in[layer, chip] = jnp.zeros((group, part), BF16)
    for which in range(2):
        end_in[which * chips + chip] = jnp.zeros((group, part), BF16)

    order_row = order_ref[...]
    ids_row = lax.broadcasted_iota(jnp.int32, (group, slots), 0) + me_r * group
    ids_col = lax.broadcasted_iota(jnp.int32, (group, slots), 1)
    order_here = jnp.sum(
        jnp.where(ids_row == ids_col, jnp.broadcast_to(order_row, (group, slots)).astype(F32), 0.0),
        axis=1,
        keepdims=True,
    ).astype(jnp.int32)
    wanted = (order_here // rows) * tile + lax.rem(order_here, rows)
    wide = lax.broadcasted_iota(jnp.int32, (group, devices * tile), 1)
    wanted = jnp.broadcast_to(wanted, (group, devices * tile))
    choose = jnp.concatenate(
        [(wide == wanted + c * rows).astype(F32) for c in range(chunks)], axis=0
    ).astype(BF16)

    square = lax.broadcasted_iota(jnp.int32, (group, group), 0) == lax.broadcasted_iota(
        jnp.int32, (group, group), 1
    )
    limit = jnp.sum(
        jnp.where(square, jnp.broadcast_to(lengths_ref[...], (group, group)).astype(F32), 0.0), axis=1, keepdims=True
    ).astype(jnp.int32)
    limit = jnp.broadcast_to(limit, (group, cached))
    valid = lax.broadcasted_iota(jnp.int32, (group, cached), 1) < limit
    flat = group * head_size
    diagonal = lax.broadcasted_iota(jnp.int32, (group, flat), 0) == (
        lax.broadcasted_iota(jnp.int32, (group, flat), 1) // head_size
    )
    score_scale = head_size ** (-0.5)

    pl.semaphore_wait(barrier, devices - 1)
    for peer in everywhere:
        remote(first.at[me], first.at[me], first_send, first_recv, peer).start()
    for layer in range(LAYERS):
        for copy in pair_copies(layer):
            copy.start()
    bias_copy.start()
    def turn_values(layer, head):
        for start in range(0, group, 4):
            block = value_v[layer, start : start + 4, head].reshape(4 * head_size, cached)
            value_t[head, :, pl.ds(start * head_size, 4 * head_size)] = block.T

    def turn_embedding(start, stop):
        for row in range(start, stop, 256):
            size = min(256, stop - row)
            emb_t[:, pl.ds(row, size)] = emb_v[pl.ds(row, size)].T

    words = emb_v.shape[0]

    load(0, 2).wait()
    for head in range(heads):
        turn_values(0, head)
    wait(first_recv, first, devices - 1)
    chosen = jnp.dot(choose, first[...].reshape(devices * tile, 128), preferred_element_type=F32)
    state = jnp.concatenate([chosen[c * group : (c + 1) * group] for c in range(chunks)], axis=1)
    for head in range(n_head):
        state_v[head] = state[:, head * part : (head + 1) * part].astype(BF16)

    def joined(ref, lead):
        return jnp.concatenate([ref[lead + (head,)] for head in range(n_head)], axis=1)

    def layer_step(layer, carry):
        state = joined(state_v, ())
        load(layer, 0).wait()
        load(layer, 1).wait()
        load(layer, 3).wait()
        attn = jnp.zeros((group, width), F32)
        parts = []
        weights = qkv_v[layer].reshape(heads * 3 * head_size, width)
        both = lax.dot_general(state, weights, NT, preferred_element_type=F32).astype(BF16).astype(F32)
        for head in range(heads):
            start = 3 * head * head_size
            parts.append([both[:, start + b * head_size : start + (b + 1) * head_size] for b in range(3)])
        expos = []
        for head in range(heads):
            query, own_key, own_value = parts[head]
            tiled = jnp.where(diagonal, jnp.concatenate([query] * group, axis=1), 0.0).astype(BF16)
            keys = key_v[layer, :, head].reshape(flat, cached)
            scores = jnp.dot(tiled, keys, preferred_element_type=F32) * score_scale
            scores = jnp.where(valid, scores, -jnp.inf)
            own = jnp.sum(query * own_key, axis=-1, keepdims=True) * score_scale
            row_max = jnp.maximum(jnp.max(scores, axis=-1, keepdims=True), own)
            expo = jnp.exp(scores - row_max)
            own_exp = jnp.exp(own - row_max)
            denom = jnp.sum(expo, axis=-1, keepdims=True) + own_exp
            expos.append((expo.astype(BF16), own_exp.astype(BF16).astype(F32), denom))
        for head in range(heads):
            expo, own_exp, denom = expos[head]
            every = jnp.dot(expo, value_t[head], preferred_element_type=F32)
            every = jnp.where(diagonal, every, 0.0)
            lanes = 2 * head_size
            folded = every[:, :lanes]
            for block in range(1, group // 2):
                folded += every[:, block * lanes : (block + 1) * lanes]
            mixed = folded[:, :head_size] + folded[:, head_size:] + own_exp * parts[head][2]
            head_out = (mixed / denom).astype(BF16)
            attn += jnp.dot(head_out, out_w_v[layer, head], preferred_element_type=F32)
        for head in range(n_head):
            attn_out[layer, head] = attn[:, head * part : (head + 1) * part].astype(BF16)
        for peer in plane:
            remote(
                attn_out.at[layer, peer[1]], attn_in.at[layer, me_h], attn_send.at[layer], attn_recv.at[layer], peer
            ).start()
        attn_in[layer, me_h] = attn_out[layer, me_h]
        if layer < LAYERS - 1:
            load(layer + 1, 2).wait()
            turn_values(layer + 1, 0)
        wait(attn_recv.at[layer], attn_in.at[layer], n_head - 1)
        total = attn_in[layer, 0].astype(F32)
        for head in range(1, n_head):
            total += attn_in[layer, head].astype(F32)
        spread[layer, me_r, me_h] = (total + state_v[me_h].astype(F32)).astype(BF16)

        def spread_copy(a, b):
            base = flip(me_h, b)
            peer = (flip(me_r, a), base - lax.rem(base, 2) + taker)
            block = spread.at[layer, me_r, me_h]
            return remote(block, block, spread_send.at[layer], spread_recv.at[layer, me_r], peer)

        for a, b in offsets:
            if b % 2 == 0:
                spread_copy(a, b).start()

        @pl.when(jnp.logical_not(mine))
        def _():
            spread_copy(0, 0).start()

        gains, biases = gain_ref[layer], bias_ref[layer]
        bias_rows = []
        for source in range(2):
            bias_up = bias_v[source]
            bias_row = bias_up[0:1]
            for other in range(1, LAYERS):
                bias_row = jnp.where(layer == other, bias_up[other : other + 1], bias_row)
            bias_rows.append(bias_row)
        bias_row = jnp.concatenate(bias_rows, axis=1)

        def mlp_copy(which, block, b):
            peer = (block, flip(me_h, b))
            return remote(
                mlp_out.at[layer, which, peer[1]], mlp_in.at[layer, chip], mlp_send.at[layer], mlp_recv.at[layer], peer
            )

        def end_copy(which, block, b):
            peer = (jnp.where(block < middle, middle - 1, middle), flip(me_h, b))
            return remote(
                mlp_out.at[layer, which, peer[1]],
                end_in.at[lax.rem(block, 2) * chips + chip],
                end_send,
                end_recv,
                peer,
            )

        def own_copy():
            return remote(own_out.at[layer, partner[1]], own_in.at[layer], own_send.at[layer], own_recv.at[layer], partner)

        load(layer, 4).wait()
        load(layer, 5).wait()
        if layer < LAYERS - 1:
            for head in range(1, heads):
                turn_values(layer + 1, head)
        for copy in pair_copies(layer):
            copy.wait_recv()
        either(
            lambda: wait(spread_recv.at[layer, near_group], spread.at[layer, 0], n_head - 1),
            lambda: wait(spread_recv.at[layer, near_group], spread.at[layer, 0], n_head),
        )
        wait(spread_recv.at[layer, far_group], spread.at[layer, 0], n_head)
        before = jnp.concatenate(
            [
                jnp.concatenate([spread[layer, block, head] for head in range(n_head)], axis=1)
                for block in (near_group, far_group)
            ],
            axis=0,
        ).astype(F32)
        normed = quick_norm(before, gains[0:1], biases[0:1]).astype(BF16)
        pre_act = jnp.dot(normed, up_v[layer], preferred_element_type=F32) + bias_row
        hidden = (0.5 * pre_act * (1.0 + lax.erf(pre_act * 0.7071067811865476))).astype(BF16)
        mlp = lax.dot_general(hidden, down_v[layer], NT, preferred_element_type=F32)
        for which in (1, 0):
            for head in range(n_head):
                mlp_out[layer, which, head] = mlp[
                    which * group : (which + 1) * group, head * part : (head + 1) * part
                ].astype(BF16)
        if layer == LAYERS - 1:
            return finish(layer, mlp, normed, end_copy)
        whole = mlp[:group] + normed[:group].astype(F32)
        for head in range(n_head):
            own_out[layer, head] = whole[:, head * part : (head + 1) * part]
        for b in range(n_head - 1, -1, -1):
            mlp_copy(1, far_group, b).start()
        for b in range(n_head - 1, 1, -1):
            mlp_copy(0, near_group, b).start()

        @pl.when(mine)
        def _():
            own_copy().start()
            own_in[layer] = own_out[layer, me_h]

        @pl.when(jnp.logical_not(mine))
        def _():
            for b in range(2):
                mlp_copy(0, near_group, b).start()
            own_copy().wait_recv()

        emb_load.wait()
        turn_embedding(0, words // 2)
        wait(mlp_recv.at[layer], mlp_in.at[layer], chips - 1)
        total = own_in[layer]
        for source in range(chips):
            total += mlp_in[layer, source].astype(F32)
        near[layer, me_h] = total.astype(BF16)
        for peer in plane:
            block = near.at[layer, me_h]
            remote(block, block, near_send.at[layer], near_recv.at[layer], peer).start()
        turn_embedding(words // 2, words)
        wait(near_recv.at[layer], near.at[layer], n_head - 1)
        fresh = joined(near, (layer,)).astype(F32)
        fresh = quick_norm(fresh, gains[1:2], biases[1:2]).astype(BF16)
        for head in range(n_head):
            state_v[head] = fresh[:, head * part : (head + 1) * part]
        return carry

    def finish(layer, mlp, normed, end_copy):
        whole = mlp[:group] + normed[:group].astype(F32)
        for b in range(n_head - 1, -1, -1):
            end_copy(1, far_group, b).start()
        for b in range(n_head - 1, 1, -1):
            end_copy(0, near_group, b).start()
        for head in range(n_head):
            own_out[layer, head] = whole[:, head * part : (head + 1) * part]

        @pl.when(jnp.logical_not(owner))
        def _():
            for b in range(2):
                end_copy(0, near_group, b).start()

        @pl.when(owner)
        def _():
            end_own().start()
            end_own_in[lax.rem(near_group, 2)] = own_out[layer, me_h]
            end_own().wait_recv()
            wait(end_recv, end_in, 2 * chips - 2)
            for which in range(2):
                total = end_own_in[which]
                for source in range(chips):
                    total += end_in[which * chips + source].astype(F32)
                last[near_owner, me_h, pl.ds(which * group, group)] = total.astype(BF16)
            block = last.at[near_owner, me_h]
            for a, b in end_offsets:
                peer = (flip(me_r, a), flip(me_h, b + 1))
                remote(block, block, last_send, last_recv.at[near_owner], peer).start()
            remote(block, block, last_send, pass_recv.at[near_owner], partner).start()

    def end_own():
        return remote(
            own_out.at[LAYERS - 1, partner[1]],
            end_own_in.at[lax.rem(near_group, 2)],
            own_send.at[LAYERS - 1],
            own_recv.at[LAYERS - 1],
            partner,
        )

    def forward(plane_of, b):
        block = last.at[plane_of, flip(me_h, b + 1)]
        remote(block, block, pass_send, pass_recv.at[plane_of], partner).start()

    bias_copy.wait_recv()
    for layer in range(LAYERS):
        layer_step(layer, 0)

    @pl.when(owner)
    def _():
        wait(last_recv.at[near_owner], last.at[0], n_head // 2 - 1)
        for b in range(2, n_head, 2):
            forward(near_owner, b)

    @pl.when(jnp.logical_not(owner))
    def _():
        wait(last_recv.at[near_owner], last.at[0], n_head // 2)
        for b in range(0, n_head, 2):
            forward(near_owner, b)

    wait(last_recv.at[1 - near_owner], last.at[0], n_head // 2)
    for b in range(0, n_head, 2):
        forward(1 - near_owner, b)
    pick = (
        (
            lax.broadcasted_iota(jnp.int32, (slots, slots), 0)
            == jnp.broadcast_to(order_row, (slots, slots))
        )
        .astype(F32)
        .astype(BF16)
    )
    wait(first_send, first, devices - 1)
    bias_copy.wait_send()
    for layer in range(LAYERS):
        for copy in pair_copies(layer):
            copy.wait_send()
        wait(attn_send.at[layer], attn_in.at[layer], n_head - 1)
        @pl.when(mine)
        def _():
            wait(spread_send.at[layer], mlp_in.at[0], chips - 1)

        @pl.when(jnp.logical_not(mine))
        def _():
            wait(spread_send.at[layer], mlp_in.at[0], chips)

        if layer < LAYERS - 1:
            wait(near_send.at[layer], near.at[layer], n_head - 1)

            @pl.when(mine)
            def _():
                wait(mlp_send.at[layer], mlp_in.at[0], 2 * n_head - 2)
                remote(
                    own_out.at[layer, 0], own_in.at[layer], own_send.at[layer], own_recv.at[layer], partner
                ).wait_send()

            @pl.when(jnp.logical_not(mine))
            def _():
                wait(mlp_send.at[layer], mlp_in.at[0], 2 * n_head)

    @pl.when(owner)
    def _():
        wait(end_send, end_in, 2 * n_head - 2)
        end_own().wait_send()

    @pl.when(jnp.logical_not(owner))
    def _():
        wait(end_send, end_in, 2 * n_head)

    for plane_of in range(2):
        wait(pass_recv.at[plane_of], last.at[0], n_head // 2)
    before = jnp.concatenate(
        [jnp.concatenate([last[plane_of, head] for head in range(n_head)], axis=1) for plane_of in range(2)],
        axis=0,
    ).astype(F32)
    gains, biases = gain_ref[LAYERS - 1], bias_ref[LAYERS - 1]
    final = quick_norm(before, gains[1:2], biases[1:2]).astype(BF16)
    ordered = jnp.dot(pick, final, preferred_element_type=F32).astype(BF16)
    logits_ref[...] = jnp.dot(ordered, emb_t[...], preferred_element_type=F32)

    @pl.when(owner)
    def _():
        wait(last_send, last, 2)
        wait(pass_send, last.at[0], n_head - 1)

    @pl.when(jnp.logical_not(owner))
    def _():
        wait(pass_send, last.at[0], n_head)


def kernel(
    n_req,
    n_head,
    hidden_ref,
    lengths_ref,
    order_ref,
    key_hbm,
    value_hbm,
    qkv_hbm,
    out_w_hbm,
    up_hbm,
    bias_up_ref,
    down_hbm,
    gain_ref,
    bias_ref,
    emb_hbm,
    logits_ref,
    key_v,
    value_v,
    qkv_v,
    out_w_v,
    up_v,
    down_v,
    emb_v,
    load_sem,
    emb_sem,
    state_v,
    normed_v,
    first,
    attn_out,
    attn_in,
    spread,
    mlp_out,
    mlp_in,
    near,
    send_sem,
    recv_sem,
):
    me_r = lax.axis_index("req")
    me_h = lax.axis_index("head")
    me = me_r * n_head + me_h
    rows, width = hidden_ref.shape
    group, heads, head_size, cached = key_v.shape[1:]
    slots = n_req * group
    devices = n_req * n_head
    part = width // n_head
    offsets = peer_offsets(n_req, n_head)
    everywhere = [(flip(me_r, a), flip(me_h, b)) for a, b in offsets]
    plane = [(me_r, flip(me_h, b)) for a, b in offsets if not a]

    barrier = pltpu.get_barrier_semaphore()
    for peer in everywhere:
        pl.semaphore_signal(barrier, inc=1, device_id=peer, device_id_type=MESH)

    pairs = (
        (qkv_hbm, qkv_v),
        (key_hbm, key_v),
        (value_hbm, value_v),
        (out_w_hbm, out_w_v),
        (up_hbm, up_v),
        (down_hbm, down_v),
    )

    def load(layer, which):
        source, target = pairs[which]
        return pltpu.make_async_copy(source.at[layer], target.at[layer], load_sem.at[layer, which])

    for layer in range(LAYERS):
        for which in range(len(pairs)):
            load(layer, which).start()
    emb_load = pltpu.make_async_copy(emb_hbm, emb_v, emb_sem)
    emb_load.start()

    def send(turn, source, target, peers):
        for peer in peers:
            pltpu.make_async_remote_copy(
                src_ref=source(peer),
                dst_ref=target,
                send_sem=send_sem.at[turn],
                recv_sem=recv_sem.at[turn],
                device_id=peer,
                device_id_type=MESH,
            ).start()

    def wait(sem, turn, ref, count):
        block = ref.at[pl.ds(0, count)]
        pltpu.make_async_copy(block, block, sem.at[turn]).wait()

    chunks = width // 128
    tile = first.shape[1]
    hidden = hidden_ref[...].astype(F32)
    pieces = [hidden[:, c * 128 : (c + 1) * 128] for c in range(chunks)]
    if tile > chunks * rows:
        pieces.append(jnp.zeros((tile - chunks * rows, 128), F32))
    first[me] = jnp.concatenate(pieces, axis=0).astype(BF16)

    order_row = order_ref[...]
    ids_row = lax.broadcasted_iota(jnp.int32, (group, slots), 0) + me_r * group
    ids_col = lax.broadcasted_iota(jnp.int32, (group, slots), 1)
    order_here = jnp.sum(
        jnp.where(ids_row == ids_col, jnp.broadcast_to(order_row, (group, slots)).astype(F32), 0.0),
        axis=1,
        keepdims=True,
    ).astype(jnp.int32)
    wanted = (order_here // rows) * tile + lax.rem(order_here, rows)
    wide = lax.broadcasted_iota(jnp.int32, (group, devices * tile), 1)
    wanted = jnp.broadcast_to(wanted, (group, devices * tile))
    choose = jnp.concatenate(
        [(wide == wanted + c * rows).astype(F32) for c in range(chunks)], axis=0
    ).astype(BF16)

    square = lax.broadcasted_iota(jnp.int32, (group, group), 0) == lax.broadcasted_iota(
        jnp.int32, (group, group), 1
    )
    limit = jnp.sum(
        jnp.where(square, jnp.broadcast_to(lengths_ref[...], (group, group)).astype(F32), 0.0), axis=1, keepdims=True
    ).astype(jnp.int32)
    limit = jnp.broadcast_to(limit, (group, cached))
    valid = lax.broadcasted_iota(jnp.int32, (group, cached), 1) < limit
    flat = group * head_size
    diagonal = lax.broadcasted_iota(jnp.int32, (group, flat), 0) == (
        lax.broadcasted_iota(jnp.int32, (group, flat), 1) // head_size
    )
    score_scale = head_size ** (-0.5)

    pl.semaphore_wait(barrier, devices - 1)
    send(0, lambda peer: first.at[me], first.at[me], everywhere)
    wait(recv_sem, 0, first, devices - 1)
    chosen = jnp.dot(choose, first[...].reshape(devices * tile, 128), preferred_element_type=F32)
    state = jnp.concatenate([chosen[c * group : (c + 1) * group] for c in range(chunks)], axis=1)
    for head in range(n_head):
        state_v[head] = state[:, head * part : (head + 1) * part].astype(BF16)

    def joined(ref, lead):
        return jnp.concatenate([ref[lead + (head,)] for head in range(n_head)], axis=1)

    def layer_step(layer, carry):
        attn_turn, spread_turn, mlp_turn, near_turn = 1 + 4 * layer, 2 + 4 * layer, 3 + 4 * layer, 4 + 4 * layer
        state = joined(state_v, ())
        load(layer, 0).wait()
        attn = jnp.zeros((group, width), F32)
        parts = []
        for head in range(heads):
            projected = (
                lax.dot_general(state, qkv_v[layer, head], NT, preferred_element_type=F32).astype(BF16).astype(F32)
            )
            parts.append(
                (
                    projected[:, :head_size],
                    projected[:, head_size : 2 * head_size],
                    projected[:, 2 * head_size :],
                )
            )
        load(layer, 1).wait()
        expos = []
        for head in range(heads):
            query, own_key, own_value = parts[head]
            tiled = jnp.where(diagonal, jnp.concatenate([query] * group, axis=1), 0.0).astype(BF16)
            keys = key_v[layer, :, head].reshape(flat, cached)
            scores = jnp.dot(tiled, keys, preferred_element_type=F32) * score_scale
            scores = jnp.where(valid, scores, -jnp.inf)
            own = jnp.sum(query * own_key, axis=-1, keepdims=True) * score_scale
            row_max = jnp.maximum(jnp.max(scores, axis=-1, keepdims=True), own)
            expo = jnp.exp(scores - row_max)
            own_exp = jnp.exp(own - row_max)
            denom = jnp.sum(expo, axis=-1, keepdims=True) + own_exp
            expos.append((expo.astype(BF16), own_exp.astype(BF16).astype(F32), denom))
        load(layer, 2).wait()
        load(layer, 3).wait()
        for head in range(heads):
            expo, own_exp, denom = expos[head]
            values = value_v[layer, :, head].reshape(flat, cached)
            every = lax.dot_general(expo, values, NT, preferred_element_type=F32)
            every = jnp.where(diagonal, every, 0.0)
            mixed = every[:, :head_size]
            for block in range(1, group):
                mixed += every[:, block * head_size : (block + 1) * head_size]
            mixed += own_exp * parts[head][2]
            head_out = (mixed / denom).astype(BF16)
            attn += jnp.dot(head_out, out_w_v[layer, head], preferred_element_type=F32)
        for head in range(n_head):
            attn_out[layer, head] = attn[:, head * part : (head + 1) * part].astype(BF16)
        send(attn_turn, lambda peer: attn_out.at[layer, peer[1]], attn_in.at[layer, me_h], plane)
        attn_in[layer, me_h] = attn_out[layer, me_h]
        wait(recv_sem, attn_turn, attn_in.at[layer], n_head - 1)
        total = attn_in[layer, 0].astype(F32)
        for head in range(1, n_head):
            total += attn_in[layer, head].astype(F32)
        spread[layer, me] = (total + state_v[me_h].astype(F32)).astype(BF16)
        send(spread_turn, lambda peer: spread.at[layer, me], spread.at[layer, me], everywhere)
        gains, biases = gain_ref[layer], bias_ref[layer]
        bias_up = bias_up_ref[...].astype(F32)
        bias_row = bias_up[0:1]
        for other in range(1, LAYERS):
            bias_row = jnp.where(layer == other, bias_up[other : other + 1], bias_row)
        load(layer, 4).wait()
        load(layer, 5).wait()
        wait(recv_sem, spread_turn, spread.at[layer], devices - 1)
        before = jnp.concatenate(
            [
                jnp.concatenate([spread[layer, req * n_head + head] for head in range(n_head)], axis=1)
                for req in range(n_req)
            ],
            axis=0,
        ).astype(F32)
        normed = layer_norm(before, gains[0:1], biases[0:1]).astype(BF16)
        for req in range(n_req):
            for head in range(n_head):
                normed_v[req * n_head + head] = normed[
                    req * group : (req + 1) * group, head * part : (head + 1) * part
                ]
        pre_act = jnp.dot(normed, up_v[layer], preferred_element_type=F32) + bias_row
        hidden = (0.5 * pre_act * (1.0 + lax.erf(pre_act * 0.7071067811865476))).astype(BF16)
        mlp = lax.dot_general(hidden, down_v[layer], NT, preferred_element_type=F32).astype(BF16)
        for req in range(n_req):
            for head in range(n_head):
                mlp_out[layer, req * n_head + head] = mlp[
                    req * group : (req + 1) * group, head * part : (head + 1) * part
                ]
        send(mlp_turn, lambda peer: mlp_out.at[layer, peer[0] * n_head + peer[1]], mlp_in.at[layer, me], everywhere)
        mlp_in[layer, me] = mlp_out[layer, me]
        wait(recv_sem, mlp_turn, mlp_in.at[layer], devices - 1)
        total = mlp_in[layer, 0].astype(F32)
        for device in range(1, devices):
            total += mlp_in[layer, device].astype(F32)
        after = (total + normed_v[me].astype(F32)).astype(BF16)

        @pl.when(layer < LAYERS - 1)
        def _():
            near[layer, me_h] = after
            send(near_turn, lambda peer: near.at[layer, me_h], near.at[layer, me_h], plane)
            wait(recv_sem, near_turn, near.at[layer], n_head - 1)
            fresh = joined(near, (layer,)).astype(F32)
            fresh = layer_norm(fresh, gains[1:2], biases[1:2]).astype(BF16)
            for head in range(n_head):
                state_v[head] = fresh[:, head * part : (head + 1) * part]

        @pl.when(layer == LAYERS - 1)
        def _():
            spread[LAYERS, me] = after

        return carry

    lax.fori_loop(0, LAYERS, layer_step, 0)
    last = 4 * LAYERS
    send(last, lambda peer: spread.at[LAYERS, me], spread.at[LAYERS, me], everywhere)
    pick = (
        (
            lax.broadcasted_iota(jnp.int32, (slots, slots), 0)
            == jnp.broadcast_to(order_row, (slots, slots))
        )
        .astype(F32)
        .astype(BF16)
    )
    emb_load.wait()
    wait(send_sem, 0, first, devices - 1)
    for layer in range(LAYERS):
        wait(send_sem, 1 + 4 * layer, attn_in.at[layer], n_head - 1)
        wait(send_sem, 2 + 4 * layer, spread.at[layer], devices - 1)
        wait(send_sem, 3 + 4 * layer, mlp_in.at[layer], devices - 1)
        if layer < LAYERS - 1:
            wait(send_sem, 4 + 4 * layer, near.at[layer], n_head - 1)
    wait(recv_sem, last, spread.at[LAYERS], devices - 1)
    before = jnp.concatenate(
        [
            jnp.concatenate([spread[LAYERS, req * n_head + head] for head in range(n_head)], axis=1)
            for req in range(n_req)
        ],
        axis=0,
    ).astype(F32)
    gains, biases = gain_ref[LAYERS - 1], bias_ref[LAYERS - 1]
    final = layer_norm(before, gains[1:2], biases[1:2]).astype(BF16)
    ordered = jnp.dot(pick, final, preferred_element_type=F32).astype(BF16)
    logits_ref[...] = lax.dot_general(ordered, emb_v[...], NT, preferred_element_type=F32)
    wait(send_sem, last, spread.at[LAYERS], devices - 1)


def body(n_req, n_head, *args):
    (hidden_in, lengths, request_order, key_cache, value_cache, w_qkv, w_out, w_up, bias_up, w_down) = args[:10]
    norm_gain, norm_bias, embedding = args[10:]
    group = lengths.shape[0]
    width = hidden_in.shape[1]
    w_qkv = jnp.swapaxes(w_qkv, 2, 3)
    slots = request_order.shape[0]
    devices = n_req * n_head
    part = width // n_head
    tile = max(16, hidden_in.shape[0] * width // 128)
    vmem = pl.BlockSpec(memory_space=pltpu.VMEM)
    hbm = pl.BlockSpec(memory_space=pltpu.HBM)
    dma = pltpu.SemaphoreType.DMA
    pin = lambda array: pltpu.with_memory_space_constraint(array, pltpu.HBM)
    held = [key_cache, value_cache, w_qkv, w_out, w_up, w_down, embedding]
    return pl.pallas_call(
        functools.partial(kernel, n_req, n_head),
        out_shape=jax.ShapeDtypeStruct((slots, embedding.shape[0]), F32),
        in_specs=[vmem] * 3 + [hbm] * 5 + [vmem, hbm, vmem, vmem, hbm],
        out_specs=vmem,
        scratch_shapes=[pltpu.VMEM(array.shape, array.dtype) for array in held]
        + [
            dma((LAYERS, 6)),
            dma,
            pltpu.VMEM((n_head, group, part), BF16),
            pltpu.VMEM((devices, group, part), BF16),
            pltpu.VMEM((devices, tile, 128), BF16),
            pltpu.VMEM((LAYERS, n_head, group, part), BF16),
            pltpu.VMEM((LAYERS, n_head, group, part), BF16),
            pltpu.VMEM((1 + LAYERS, devices, group, part), BF16),
            pltpu.VMEM((LAYERS, devices, group, part), BF16),
            pltpu.VMEM((LAYERS, devices, group, part), BF16),
            pltpu.VMEM((LAYERS, n_head, group, part), BF16),
            dma((1 + 4 * LAYERS,)),
            dma((1 + 4 * LAYERS,)),
        ],
        compiler_params=pltpu.CompilerParams(
            collective_id=0, has_side_effects=True, vmem_limit_bytes=40 * 1024 * 1024
        ),
    )(
        pin(hidden_in),
        pin(lengths.reshape(1, group)),
        pin(request_order.reshape(1, slots)),
        pin(key_cache),
        pin(value_cache),
        pin(w_qkv),
        pin(w_out),
        pin(w_up),
        pin(bias_up),
        pin(w_down),
        pin(norm_gain),
        pin(norm_bias),
        pin(embedding),
    )


def pair_body(n_req, n_head, *args):
    (hidden_in, lengths, request_order, key_cache, value_cache, w_qkv, w_out, w_up, bias_up, w_down) = args[:10]
    norm_gain, norm_bias, embedding = args[10:]
    group = lengths.shape[0]
    width = hidden_in.shape[1]
    w_qkv = jnp.swapaxes(w_qkv, 2, 3)
    slots = request_order.shape[0]
    devices = n_req * n_head
    part = width // n_head
    tile = max(16, hidden_in.shape[0] * width // 128)
    vmem = pl.BlockSpec(memory_space=pltpu.VMEM)
    hbm = pl.BlockSpec(memory_space=pltpu.HBM)
    dma = pltpu.SemaphoreType.DMA
    pin = lambda array: pltpu.with_memory_space_constraint(array, pltpu.HBM)
    units = w_up.shape[2]
    chips = devices // 2
    sizes = [key_cache.shape, value_cache.shape, w_qkv.shape, w_out.shape]
    sizes += [(LAYERS, width, 2 * units)] * 2 + [embedding.shape]
    block = (group, part)
    return pl.pallas_call(
        functools.partial(pair_kernel, n_req, n_head),
        out_shape=jax.ShapeDtypeStruct((slots, embedding.shape[0]), F32),
        in_specs=[hbm] * 13,
        out_specs=vmem,
        scratch_shapes=[pltpu.VMEM(size, BF16) for size in sizes]
        + [
            pltpu.VMEM(hidden_in.shape, BF16),
            pltpu.VMEM((1, group), jnp.int32),
            pltpu.VMEM((1, slots), jnp.int32),
            pltpu.VMEM(bias_up.shape, BF16),
            pltpu.VMEM(norm_gain.shape, F32),
            pltpu.VMEM(norm_bias.shape, F32),
            dma((6,)),
            dma((LAYERS, 6)),
            dma,
            pltpu.VMEM((2, 8, units), F32),
            pltpu.VMEM((n_head,) + block, BF16),
            pltpu.VMEM((devices, tile, 128), BF16),
            pltpu.VMEM((LAYERS, n_head) + block, BF16),
            pltpu.VMEM((LAYERS, n_head) + block, BF16),
            pltpu.VMEM((LAYERS, n_req, n_head) + block, BF16),
            pltpu.VMEM((LAYERS, 2, n_head) + block, BF16),
            pltpu.VMEM((LAYERS, chips) + block, BF16),
            pltpu.VMEM((LAYERS, n_head) + block, F32),
            pltpu.VMEM((LAYERS,) + block, F32),
            pltpu.VMEM((LAYERS, n_head) + block, BF16),
            pltpu.VMEM((2, n_head, 2 * group, part), BF16),
            pltpu.VMEM((2 * chips,) + block, BF16),
            pltpu.VMEM((2,) + block, F32),
            dma,
            dma,
            dma((LAYERS + 1, 2)),
            dma((LAYERS + 1, 2)),
            dma((LAYERS,)),
            dma((LAYERS,)),
            dma((LAYERS,)),
            dma((LAYERS, n_req)),
            dma((LAYERS,)),
            dma((LAYERS,)),
            dma((LAYERS,)),
            dma((LAYERS,)),
            dma((LAYERS,)),
            dma((LAYERS,)),
            dma,
            dma((2,)),
            dma,
            dma((2,)),
            dma,
            dma,
            pltpu.VMEM((w_out.shape[1], key_cache.shape[4], key_cache.shape[1] * key_cache.shape[3]), BF16),
            pltpu.VMEM(embedding.shape[::-1], BF16),
        ],
        compiler_params=pltpu.CompilerParams(
            collective_id=0, has_side_effects=True, vmem_limit_bytes=48 * 1024 * 1024
        ),
    )(
        pin(hidden_in),
        pin(lengths.reshape(1, group)),
        pin(request_order.reshape(1, slots)),
        pin(key_cache),
        pin(value_cache),
        pin(w_qkv),
        pin(w_out),
        pin(w_up),
        pin(bias_up),
        pin(w_down),
        pin(norm_gain),
        pin(norm_bias),
        pin(embedding),
    )


def solution(mesh):
    placed = (
        P(("req", "head"), None),
        P("req"),
        P(),
        P(None, "req", "head", None, None),
        P(None, "req", "head", None, None),
        P(None, "head", None, None),
        P(None, "head", None, None),
        P(None, None, ("req", "head")),
        P(None, ("req", "head")),
        P(None, None, ("req", "head")),
        P(),
        P(),
        P(("req", "head"), None),
    )
    inner = pair_body if (mesh.shape["req"], mesh.shape["head"]) == (4, 8) else body
    return jax.shard_map(
        functools.partial(inner, mesh.shape["req"], mesh.shape["head"]),
        mesh=mesh,
        in_specs=placed,
        out_specs=P(None, ("req", "head")),
        check_vma=False,
    )
```

```python
import functools

import jax
import jax.numpy as jnp
from jax import lax
from jax.experimental import pallas as pl
from jax.experimental.pallas import tpu as pltpu
from jax.sharding import PartitionSpec as P

LAYERS = 2
MESH = pl.DeviceIdType.MESH
F32 = jnp.float32
BF16 = jnp.bfloat16
NT = (((1,), (1,)), ((), ()))


def layer_norm(values, gain_vec, bias_vec):
    average = jnp.mean(values, axis=-1, keepdims=True)
    centred = values - average
    variance = jnp.mean(centred * centred, axis=-1, keepdims=True)
    return centred * lax.rsqrt(variance + 1e-05) * gain_vec + bias_vec


def quick_norm(values, gain_vec, bias_vec):
    average = jnp.mean(values, axis=-1, keepdims=True)
    square = jnp.mean(values * values, axis=-1, keepdims=True)
    scale = lax.rsqrt(jnp.maximum(square - average * average, 0.0) + 1e-05)
    return (values - average) * scale * gain_vec + bias_vec


def peer_offsets(n_req, n_head):
    every = [(a, b) for a in range(n_req) for b in range(n_head) if a or b]
    return sorted(every, key=lambda o: (-(o[0] + bin(o[1] >> 1).count("1")), -o[1]))


def flip(index, mask):
    bit = 1
    while bit <= mask:
        if mask & bit:
            index = index + bit - 2 * bit * lax.rem(index // bit, 2)
        bit *= 2
    return index


def pair_kernel(
    n_req,
    n_head,
    hidden_hbm,
    lengths_hbm,
    order_hbm,
    key_hbm,
    value_hbm,
    qkv_hbm,
    out_w_hbm,
    up_hbm,
    bias_up_hbm,
    down_hbm,
    gain_hbm,
    bias_hbm,
    emb_hbm,
    logits_ref,
    key_v,
    value_v,
    qkv_v,
    out_w_v,
    up_v,
    down_v,
    emb_v,
    hidden_ref,
    lengths_ref,
    order_ref,
    bias_up_ref,
    gain_ref,
    bias_ref,
    small_sem,
    load_sem,
    emb_sem,
    bias_v,
    state_v,
    first,
    attn_out,
    attn_in,
    spread,
    mlp_out,
    mlp_in,
    own_out,
    own_in,
    near,
    last,
    end_in,
    end_own_in,
    first_send,
    first_recv,
    pair_send,
    pair_recv,
    attn_send,
    attn_recv,
    spread_send,
    spread_recv,
    mlp_send,
    mlp_recv,
    own_send,
    own_recv,
    near_send,
    near_recv,
    last_send,
    last_recv,
    pass_send,
    pass_recv,
    end_send,
    end_recv,
    value_t,
    emb_t,
    qkv_t,
    down_t,
):
    me_r = lax.axis_index("req")
    me_h = lax.axis_index("head")
    me = me_r * n_head + me_h
    core = lax.rem(me_h, 2)
    chip = me // 2
    partner = (me_r, flip(me_h, 1))
    rows, width = hidden_hbm.shape
    group, heads, head_size, cached = key_v.shape[1:]
    units = up_hbm.shape[2]
    slots = n_req * group
    devices = n_req * n_head
    chips = devices // 2
    part = width // n_head
    offsets = peer_offsets(n_req, n_head)
    everywhere = [(flip(me_r, a), flip(me_h, b)) for a, b in offsets]
    plane = [(me_r, flip(me_h, b)) for a, b in offsets if not a]
    middle = n_req // 2
    owner = (me_r + 1) // middle == 1
    near_owner = me_r // middle
    reach = (0, 1, 2, 1)
    end_offsets = sorted(
        [(a, b) for a, b in offsets if b % 2 == 0], key=lambda o: -(reach[o[0]] + bin(o[1]).count("1"))
    )
    taker = lax.rem((me_r + 1) // middle, 2)
    mine = taker == core
    near_group = jnp.where(me_r < middle, core, n_req - 1 - core)
    far_group = n_req - 1 - near_group

    barrier = pltpu.get_barrier_semaphore()
    for peer in everywhere:
        pl.semaphore_signal(barrier, inc=1, device_id=peer, device_id_type=MESH)

    smalls = [
        pltpu.make_async_copy(source, target, small_sem.at[place])
        for place, (source, target) in enumerate(
            (
                (hidden_hbm, hidden_ref),
                (order_hbm, order_ref),
                (lengths_hbm, lengths_ref),
                (bias_up_hbm, bias_up_ref),
                (gain_hbm, gain_ref),
                (bias_hbm, bias_ref),
            )
        )
    ]
    for copy in smalls:
        copy.start()

    def up_part(ref, layer, which):
        return ref.at[layer, :, pl.ds(which * units, units)]

    def load(layer, which):
        source, target = (
            (qkv_hbm.at[layer], qkv_v.at[layer]),
            (key_hbm.at[layer], key_v.at[layer]),
            (value_hbm.at[layer], value_v.at[layer]),
            (out_w_hbm.at[layer], out_w_v.at[layer]),
            (up_hbm.at[layer], up_part(up_v, layer, 0)),
            (down_hbm.at[layer], up_part(down_v, layer, 0)),
        )[which]
        return pltpu.make_async_copy(source, target, load_sem.at[layer, which])

    emb_load = pltpu.make_async_copy(emb_hbm, emb_v, emb_sem)

    def remote(source, target, sender, receiver, peer):
        return pltpu.make_async_remote_copy(
            src_ref=source,
            dst_ref=target,
            send_sem=sender,
            recv_sem=receiver,
            device_id=peer,
            device_id_type=MESH,
        )

    def wait(sem, ref, count):
        block = ref.at[pl.ds(0, count)]
        pltpu.make_async_copy(block, block, sem).wait()

    def either(held, given):
        pl.when(mine)(held)
        pl.when(jnp.logical_not(mine))(given)

    def pair_copies(layer):
        return (
            remote(up_hbm.at[layer], up_part(up_v, layer, 1), pair_send.at[layer, 0], pair_recv.at[layer, 0], partner),
            remote(
                down_hbm.at[layer], up_part(down_v, layer, 1), pair_send.at[layer, 1], pair_recv.at[layer, 1], partner
            ),
        )

    bias_copy = remote(bias_v.at[0], bias_v.at[1], pair_send.at[LAYERS, 0], pair_recv.at[LAYERS, 0], partner)

    chunks = width // 128
    tile = first.shape[1]
    for copy in smalls:
        copy.wait()
    for layer in range(LAYERS):
        for which in range(6):
            load(layer, which).start()
    emb_load.start()
    hidden = hidden_ref[...].astype(F32)
    pieces = [hidden[:, c * 128 : (c + 1) * 128] for c in range(chunks)]
    if tile > chunks * rows:
        pieces.append(jnp.zeros((tile - chunks * rows, 128), F32))
    first[me] = jnp.concatenate(pieces, axis=0).astype(BF16)
    bias_v[0] = jnp.concatenate(
        [bias_up_ref[...].astype(F32), jnp.zeros((bias_v.shape[1] - LAYERS, units), F32)], axis=0
    )
    for layer in range(LAYERS - 1):
        mlp_in[layer, chip] = jnp.zeros((group, part), BF16)
    for which in range(2):
        end_in[which * chips + chip] = jnp.zeros((group, part), BF16)

    order_row = order_ref[...]
    ids_row = lax.broadcasted_iota(jnp.int32, (group, slots), 0) + me_r * group
    ids_col = lax.broadcasted_iota(jnp.int32, (group, slots), 1)
    order_here = jnp.sum(
        jnp.where(ids_row == ids_col, jnp.broadcast_to(order_row, (group, slots)).astype(F32), 0.0),
        axis=1,
        keepdims=True,
    ).astype(jnp.int32)
    wanted = (order_here // rows) * tile + lax.rem(order_here, rows)
    wide = lax.broadcasted_iota(jnp.int32, (group, devices * tile), 1)
    wanted = jnp.broadcast_to(wanted, (group, devices * tile))
    choose = jnp.concatenate(
        [(wide == wanted + c * rows).astype(F32) for c in range(chunks)], axis=0
    ).astype(BF16)

    square = lax.broadcasted_iota(jnp.int32, (group, group), 0) == lax.broadcasted_iota(
        jnp.int32, (group, group), 1
    )
    limit = jnp.sum(
        jnp.where(square, jnp.broadcast_to(lengths_ref[...], (group, group)).astype(F32), 0.0), axis=1, keepdims=True
    ).astype(jnp.int32)
    limit = jnp.broadcast_to(limit, (group, cached))
    valid = lax.broadcasted_iota(jnp.int32, (group, cached), 1) < limit
    flat = group * head_size
    diagonal = lax.broadcasted_iota(jnp.int32, (group, flat), 0) == (
        lax.broadcasted_iota(jnp.int32, (group, flat), 1) // head_size
    )
    score_scale = head_size ** (-0.5)

    pl.semaphore_wait(barrier, devices - 1)
    for peer in everywhere:
        remote(first.at[me], first.at[me], first_send, first_recv, peer).start()
    for layer in range(LAYERS):
        for copy in pair_copies(layer):
            copy.start()
    bias_copy.start()
    def turn_values(layer, head):
        for start in range(0, group, 4):
            block = value_v[layer, start : start + 4, head].reshape(4 * head_size, cached)
            value_t[head, :, pl.ds(start * head_size, 4 * head_size)] = block.T

    def turn_embedding(start, stop):
        for row in range(start, stop, 256):
            size = min(256, stop - row)
            emb_t[:, pl.ds(row, size)] = emb_v[pl.ds(row, size)].T

    words = emb_v.shape[0]

    def turn_heads(layer):
        weights = qkv_v[layer].reshape(heads * 3 * head_size, width)
        qkv_t[layer] = weights.T

    def turn_down(layer):
        load(layer, 5).wait()
        pair_copies(layer)[1].wait_recv()
        down_t[layer] = down_v[layer].T

    load(0, 0).wait()
    turn_heads(0)
    load(0, 2).wait()
    for head in range(heads):
        turn_values(0, head)
    wait(first_recv, first, devices - 1)
    chosen = jnp.dot(choose, first[...].reshape(devices * tile, 128), preferred_element_type=F32)
    state = jnp.concatenate([chosen[c * group : (c + 1) * group] for c in range(chunks)], axis=1)
    for head in range(n_head):
        state_v[head] = state[:, head * part : (head + 1) * part].astype(BF16)

    def joined(ref, lead):
        return jnp.concatenate([ref[lead + (head,)] for head in range(n_head)], axis=1)

    def layer_step(layer, carry):
        state = joined(state_v, ())
        load(layer, 1).wait()
        load(layer, 3).wait()
        attn = jnp.zeros((group, width), F32)
        parts = []
        both = jnp.dot(state, qkv_t[layer], preferred_element_type=F32).astype(BF16).astype(F32)
        for head in range(heads):
            start = 3 * head * head_size
            parts.append([both[:, start + b * head_size : start + (b + 1) * head_size] for b in range(3)])
        expos = []
        for head in range(heads):
            query, own_key, own_value = parts[head]
            tiled = jnp.where(diagonal, jnp.concatenate([query] * group, axis=1), 0.0).astype(BF16)
            keys = key_v[layer, :, head].reshape(flat, cached)
            scores = jnp.dot(tiled, keys, preferred_element_type=F32) * score_scale
            scores = jnp.where(valid, scores, -jnp.inf)
            own = jnp.sum(query * own_key, axis=-1, keepdims=True) * score_scale
            row_max = jnp.maximum(jnp.max(scores, axis=-1, keepdims=True), own)
            expo = jnp.exp(scores - row_max)
            own_exp = jnp.exp(own - row_max)
            denom = jnp.sum(expo, axis=-1, keepdims=True) + own_exp
            expos.append((expo.astype(BF16), own_exp.astype(BF16).astype(F32), denom))
        for head in range(heads):
            expo, own_exp, denom = expos[head]
            every = jnp.dot(expo, value_t[head], preferred_element_type=F32)
            every = jnp.where(diagonal, every, 0.0)
            lanes = 2 * head_size
            folded = every[:, :lanes]
            for block in range(1, group // 2):
                folded += every[:, block * lanes : (block + 1) * lanes]
            mixed = folded[:, :head_size] + folded[:, head_size:] + own_exp * parts[head][2]
            head_out = (mixed / denom).astype(BF16)
            attn += jnp.dot(head_out, out_w_v[layer, head], preferred_element_type=F32)
        for head in range(n_head):
            attn_out[layer, head] = attn[:, head * part : (head + 1) * part].astype(BF16)
        for peer in plane:
            remote(
                attn_out.at[layer, peer[1]], attn_in.at[layer, me_h], attn_send.at[layer], attn_recv.at[layer], peer
            ).start()
        attn_in[layer, me_h] = attn_out[layer, me_h]
        if layer < LAYERS - 1:
            load(layer + 1, 2).wait()
            turn_values(layer + 1, 0)
        turn_down(layer)
        wait(attn_recv.at[layer], attn_in.at[layer], n_head - 1)
        total = attn_in[layer, 0].astype(F32)
        for head in range(1, n_head):
            total += attn_in[layer, head].astype(F32)
        spread[layer, me_r, me_h] = (total + state_v[me_h].astype(F32)).astype(BF16)

        def spread_copy(a, b):
            base = flip(me_h, b)
            peer = (flip(me_r, a), base - lax.rem(base, 2) + taker)
            block = spread.at[layer, me_r, me_h]
            return remote(block, block, spread_send.at[layer], spread_recv.at[layer, me_r], peer)

        for a, b in offsets:
            if b % 2 == 0:
                spread_copy(a, b).start()

        @pl.when(jnp.logical_not(mine))
        def _():
            spread_copy(0, 0).start()

        gains, biases = gain_ref[layer], bias_ref[layer]
        bias_rows = []
        for source in range(2):
            bias_up = bias_v[source]
            bias_row = bias_up[0:1]
            for other in range(1, LAYERS):
                bias_row = jnp.where(layer == other, bias_up[other : other + 1], bias_row)
            bias_rows.append(bias_row)
        bias_row = jnp.concatenate(bias_rows, axis=1)

        def mlp_copy(which, block, b):
            peer = (block, flip(me_h, b))
            return remote(
                mlp_out.at[layer, which, peer[1]], mlp_in.at[layer, chip], mlp_send.at[layer], mlp_recv.at[layer], peer
            )

        def end_copy(which, block, b):
            peer = (jnp.where(block < middle, middle - 1, middle), flip(me_h, b))
            return remote(
                mlp_out.at[layer, which, peer[1]],
                end_in.at[lax.rem(block, 2) * chips + chip],
                end_send,
                end_recv,
                peer,
            )

        def own_copy():
            return remote(own_out.at[layer, partner[1]], own_in.at[layer], own_send.at[layer], own_recv.at[layer], partner)

        load(layer, 4).wait()
        if layer < LAYERS - 1:
            for head in range(1, heads):
                turn_values(layer + 1, head)
            load(layer + 1, 0).wait()
            turn_heads(layer + 1)
        pair_copies(layer)[0].wait_recv()
        either(
            lambda: wait(spread_recv.at[layer, near_group], spread.at[layer, 0], n_head - 1),
            lambda: wait(spread_recv.at[layer, near_group], spread.at[layer, 0], n_head),
        )
        wait(spread_recv.at[layer, far_group], spread.at[layer, 0], n_head)
        before = jnp.concatenate(
            [
                jnp.concatenate([spread[layer, block, head] for head in range(n_head)], axis=1)
                for block in (near_group, far_group)
            ],
            axis=0,
        ).astype(F32)
        normed = quick_norm(before, gains[0:1], biases[0:1]).astype(BF16)
        pre_act = jnp.dot(normed, up_v[layer], preferred_element_type=F32) + bias_row
        hidden = (0.5 * pre_act * (1.0 + lax.erf(pre_act * 0.7071067811865476))).astype(BF16)
        mlp = jnp.dot(hidden, down_t[layer], preferred_element_type=F32)
        def store(which):
            for head in range(n_head):
                mlp_out[layer, which, head] = mlp[
                    which * group : (which + 1) * group, head * part : (head + 1) * part
                ].astype(BF16)

        if layer == LAYERS - 1:
            return finish(layer, mlp, normed, store, end_copy)
        store(1)
        for b in range(n_head - 1, -1, -1):
            mlp_copy(1, far_group, b).start()
        store(0)
        for b in range(n_head - 1, 1, -1):
            mlp_copy(0, near_group, b).start()
        whole = mlp[:group] + normed[:group].astype(F32)
        for head in range(n_head):
            own_out[layer, head] = whole[:, head * part : (head + 1) * part]

        @pl.when(mine)
        def _():
            own_copy().start()
            own_in[layer] = own_out[layer, me_h]

        @pl.when(jnp.logical_not(mine))
        def _():
            for b in range(2):
                mlp_copy(0, near_group, b).start()

        emb_load.wait()
        turn_embedding(0, words // 2)

        @pl.when(jnp.logical_not(mine))
        def _():
            own_copy().wait_recv()

        wait(mlp_recv.at[layer], mlp_in.at[layer], chips - 1)
        total = own_in[layer]
        for source in range(chips):
            total += mlp_in[layer, source].astype(F32)
        near[layer, me_h] = total.astype(BF16)
        for peer in plane:
            block = near.at[layer, me_h]
            remote(block, block, near_send.at[layer], near_recv.at[layer], peer).start()
        turn_embedding(words // 2, words)
        wait(near_recv.at[layer], near.at[layer], n_head - 1)
        fresh = joined(near, (layer,)).astype(F32)
        fresh = quick_norm(fresh, gains[1:2], biases[1:2]).astype(BF16)
        for head in range(n_head):
            state_v[head] = fresh[:, head * part : (head + 1) * part]
        return carry

    def finish(layer, mlp, normed, store, end_copy):
        store(1)
        for b in range(n_head - 1, -1, -1):
            end_copy(1, far_group, b).start()
        store(0)
        for b in range(n_head - 1, 1, -1):
            end_copy(0, near_group, b).start()
        whole = mlp[:group] + normed[:group].astype(F32)
        for head in range(n_head):
            own_out[layer, head] = whole[:, head * part : (head + 1) * part]

        @pl.when(jnp.logical_not(owner))
        def _():
            for b in range(2):
                end_copy(0, near_group, b).start()

        @pl.when(owner)
        def _():
            end_own().start()
            end_own_in[lax.rem(near_group, 2)] = own_out[layer, me_h]
            end_own().wait_recv()
            wait(end_recv, end_in, 2 * chips - 2)
            for which in range(2):
                total = end_own_in[which]
                for source in range(chips):
                    total += end_in[which * chips + source].astype(F32)
                last[near_owner, me_h, pl.ds(which * group, group)] = total.astype(BF16)
            block = last.at[near_owner, me_h]
            for a, b in end_offsets:
                peer = (flip(me_r, a), flip(me_h, b + 1))
                remote(block, block, last_send, last_recv.at[near_owner], peer).start()
            remote(block, block, last_send, pass_recv.at[near_owner], partner).start()

    def end_own():
        return remote(
            own_out.at[LAYERS - 1, partner[1]],
            end_own_in.at[lax.rem(near_group, 2)],
            own_send.at[LAYERS - 1],
            own_recv.at[LAYERS - 1],
            partner,
        )

    def forward(plane_of, b):
        block = last.at[plane_of, flip(me_h, b + 1)]
        remote(block, block, pass_send, pass_recv.at[plane_of], partner).start()

    bias_copy.wait_recv()
    for layer in range(LAYERS):
        layer_step(layer, 0)

    @pl.when(owner)
    def _():
        wait(last_recv.at[near_owner], last.at[0], n_head // 2 - 1)
        for b in range(2, n_head, 2):
            forward(near_owner, b)

    @pl.when(jnp.logical_not(owner))
    def _():
        wait(last_recv.at[near_owner], last.at[0], n_head // 2)
        for b in range(0, n_head, 2):
            forward(near_owner, b)

    wait(last_recv.at[1 - near_owner], last.at[0], n_head // 2)
    for b in range(0, n_head, 2):
        forward(1 - near_owner, b)
    pick = (
        (
            lax.broadcasted_iota(jnp.int32, (slots, slots), 0)
            == jnp.broadcast_to(order_row, (slots, slots))
        )
        .astype(F32)
        .astype(BF16)
    )
    wait(first_send, first, devices - 1)
    bias_copy.wait_send()
    for layer in range(LAYERS):
        for copy in pair_copies(layer):
            copy.wait_send()
        wait(attn_send.at[layer], attn_in.at[layer], n_head - 1)
        @pl.when(mine)
        def _():
            wait(spread_send.at[layer], mlp_in.at[0], chips - 1)

        @pl.when(jnp.logical_not(mine))
        def _():
            wait(spread_send.at[layer], mlp_in.at[0], chips)

        if layer < LAYERS - 1:
            wait(near_send.at[layer], near.at[layer], n_head - 1)

            @pl.when(mine)
            def _():
                wait(mlp_send.at[layer], mlp_in.at[0], 2 * n_head - 2)
                remote(
                    own_out.at[layer, 0], own_in.at[layer], own_send.at[layer], own_recv.at[layer], partner
                ).wait_send()

            @pl.when(jnp.logical_not(mine))
            def _():
                wait(mlp_send.at[layer], mlp_in.at[0], 2 * n_head)

    @pl.when(owner)
    def _():
        wait(end_send, end_in, 2 * n_head - 2)
        end_own().wait_send()

    @pl.when(jnp.logical_not(owner))
    def _():
        wait(end_send, end_in, 2 * n_head)

    for plane_of in range(2):
        wait(pass_recv.at[plane_of], last.at[0], n_head // 2)
    before = jnp.concatenate(
        [jnp.concatenate([last[plane_of, head] for head in range(n_head)], axis=1) for plane_of in range(2)],
        axis=0,
    ).astype(F32)
    gains, biases = gain_ref[LAYERS - 1], bias_ref[LAYERS - 1]
    final = quick_norm(before, gains[1:2], biases[1:2]).astype(BF16)
    ordered = jnp.dot(pick, final, preferred_element_type=F32).astype(BF16)
    logits_ref[...] = jnp.dot(ordered, emb_t[...], preferred_element_type=F32)

    @pl.when(owner)
    def _():
        wait(last_send, last, 2)
        wait(pass_send, last.at[0], n_head - 1)

    @pl.when(jnp.logical_not(owner))
    def _():
        wait(pass_send, last.at[0], n_head)


def kernel(
    n_req,
    n_head,
    hidden_ref,
    lengths_ref,
    order_ref,
    key_hbm,
    value_hbm,
    qkv_hbm,
    out_w_hbm,
    up_hbm,
    bias_up_ref,
    down_hbm,
    gain_ref,
    bias_ref,
    emb_hbm,
    logits_ref,
    key_v,
    value_v,
    qkv_v,
    out_w_v,
    up_v,
    down_v,
    emb_v,
    load_sem,
    emb_sem,
    state_v,
    normed_v,
    first,
    attn_out,
    attn_in,
    spread,
    mlp_out,
    mlp_in,
    near,
    send_sem,
    recv_sem,
):
    me_r = lax.axis_index("req")
    me_h = lax.axis_index("head")
    me = me_r * n_head + me_h
    rows, width = hidden_ref.shape
    group, heads, head_size, cached = key_v.shape[1:]
    slots = n_req * group
    devices = n_req * n_head
    part = width // n_head
    offsets = peer_offsets(n_req, n_head)
    everywhere = [(flip(me_r, a), flip(me_h, b)) for a, b in offsets]
    plane = [(me_r, flip(me_h, b)) for a, b in offsets if not a]

    barrier = pltpu.get_barrier_semaphore()
    for peer in everywhere:
        pl.semaphore_signal(barrier, inc=1, device_id=peer, device_id_type=MESH)

    pairs = (
        (qkv_hbm, qkv_v),
        (key_hbm, key_v),
        (value_hbm, value_v),
        (out_w_hbm, out_w_v),
        (up_hbm, up_v),
        (down_hbm, down_v),
    )

    def load(layer, which):
        source, target = pairs[which]
        return pltpu.make_async_copy(source.at[layer], target.at[layer], load_sem.at[layer, which])

    for layer in range(LAYERS):
        for which in range(len(pairs)):
            load(layer, which).start()
    emb_load = pltpu.make_async_copy(emb_hbm, emb_v, emb_sem)
    emb_load.start()

    def send(turn, source, target, peers):
        for peer in peers:
            pltpu.make_async_remote_copy(
                src_ref=source(peer),
                dst_ref=target,
                send_sem=send_sem.at[turn],
                recv_sem=recv_sem.at[turn],
                device_id=peer,
                device_id_type=MESH,
            ).start()

    def wait(sem, turn, ref, count):
        block = ref.at[pl.ds(0, count)]
        pltpu.make_async_copy(block, block, sem.at[turn]).wait()

    chunks = width // 128
    tile = first.shape[1]
    hidden = hidden_ref[...].astype(F32)
    pieces = [hidden[:, c * 128 : (c + 1) * 128] for c in range(chunks)]
    if tile > chunks * rows:
        pieces.append(jnp.zeros((tile - chunks * rows, 128), F32))
    first[me] = jnp.concatenate(pieces, axis=0).astype(BF16)

    order_row = order_ref[...]
    ids_row = lax.broadcasted_iota(jnp.int32, (group, slots), 0) + me_r * group
    ids_col = lax.broadcasted_iota(jnp.int32, (group, slots), 1)
    order_here = jnp.sum(
        jnp.where(ids_row == ids_col, jnp.broadcast_to(order_row, (group, slots)).astype(F32), 0.0),
        axis=1,
        keepdims=True,
    ).astype(jnp.int32)
    wanted = (order_here // rows) * tile + lax.rem(order_here, rows)
    wide = lax.broadcasted_iota(jnp.int32, (group, devices * tile), 1)
    wanted = jnp.broadcast_to(wanted, (group, devices * tile))
    choose = jnp.concatenate(
        [(wide == wanted + c * rows).astype(F32) for c in range(chunks)], axis=0
    ).astype(BF16)

    square = lax.broadcasted_iota(jnp.int32, (group, group), 0) == lax.broadcasted_iota(
        jnp.int32, (group, group), 1
    )
    limit = jnp.sum(
        jnp.where(square, jnp.broadcast_to(lengths_ref[...], (group, group)).astype(F32), 0.0), axis=1, keepdims=True
    ).astype(jnp.int32)
    limit = jnp.broadcast_to(limit, (group, cached))
    valid = lax.broadcasted_iota(jnp.int32, (group, cached), 1) < limit
    flat = group * head_size
    diagonal = lax.broadcasted_iota(jnp.int32, (group, flat), 0) == (
        lax.broadcasted_iota(jnp.int32, (group, flat), 1) // head_size
    )
    score_scale = head_size ** (-0.5)

    pl.semaphore_wait(barrier, devices - 1)
    send(0, lambda peer: first.at[me], first.at[me], everywhere)
    wait(recv_sem, 0, first, devices - 1)
    chosen = jnp.dot(choose, first[...].reshape(devices * tile, 128), preferred_element_type=F32)
    state = jnp.concatenate([chosen[c * group : (c + 1) * group] for c in range(chunks)], axis=1)
    for head in range(n_head):
        state_v[head] = state[:, head * part : (head + 1) * part].astype(BF16)

    def joined(ref, lead):
        return jnp.concatenate([ref[lead + (head,)] for head in range(n_head)], axis=1)

    def layer_step(layer, carry):
        attn_turn, spread_turn, mlp_turn, near_turn = 1 + 4 * layer, 2 + 4 * layer, 3 + 4 * layer, 4 + 4 * layer
        state = joined(state_v, ())
        load(layer, 0).wait()
        attn = jnp.zeros((group, width), F32)
        parts = []
        for head in range(heads):
            projected = (
                lax.dot_general(state, qkv_v[layer, head], NT, preferred_element_type=F32).astype(BF16).astype(F32)
            )
            parts.append(
                (
                    projected[:, :head_size],
                    projected[:, head_size : 2 * head_size],
                    projected[:, 2 * head_size :],
                )
            )
        load(layer, 1).wait()
        expos = []
        for head in range(heads):
            query, own_key, own_value = parts[head]
            tiled = jnp.where(diagonal, jnp.concatenate([query] * group, axis=1), 0.0).astype(BF16)
            keys = key_v[layer, :, head].reshape(flat, cached)
            scores = jnp.dot(tiled, keys, preferred_element_type=F32) * score_scale
            scores = jnp.where(valid, scores, -jnp.inf)
            own = jnp.sum(query * own_key, axis=-1, keepdims=True) * score_scale
            row_max = jnp.maximum(jnp.max(scores, axis=-1, keepdims=True), own)
            expo = jnp.exp(scores - row_max)
            own_exp = jnp.exp(own - row_max)
            denom = jnp.sum(expo, axis=-1, keepdims=True) + own_exp
            expos.append((expo.astype(BF16), own_exp.astype(BF16).astype(F32), denom))
        load(layer, 2).wait()
        load(layer, 3).wait()
        for head in range(heads):
            expo, own_exp, denom = expos[head]
            values = value_v[layer, :, head].reshape(flat, cached)
            every = lax.dot_general(expo, values, NT, preferred_element_type=F32)
            every = jnp.where(diagonal, every, 0.0)
            mixed = every[:, :head_size]
            for block in range(1, group):
                mixed += every[:, block * head_size : (block + 1) * head_size]
            mixed += own_exp * parts[head][2]
            head_out = (mixed / denom).astype(BF16)
            attn += jnp.dot(head_out, out_w_v[layer, head], preferred_element_type=F32)
        for head in range(n_head):
            attn_out[layer, head] = attn[:, head * part : (head + 1) * part].astype(BF16)
        send(attn_turn, lambda peer: attn_out.at[layer, peer[1]], attn_in.at[layer, me_h], plane)
        attn_in[layer, me_h] = attn_out[layer, me_h]
        wait(recv_sem, attn_turn, attn_in.at[layer], n_head - 1)
        total = attn_in[layer, 0].astype(F32)
        for head in range(1, n_head):
            total += attn_in[layer, head].astype(F32)
        spread[layer, me] = (total + state_v[me_h].astype(F32)).astype(BF16)
        send(spread_turn, lambda peer: spread.at[layer, me], spread.at[layer, me], everywhere)
        gains, biases = gain_ref[layer], bias_ref[layer]
        bias_up = bias_up_ref[...].astype(F32)
        bias_row = bias_up[0:1]
        for other in range(1, LAYERS):
            bias_row = jnp.where(layer == other, bias_up[other : other + 1], bias_row)
        load(layer, 4).wait()
        load(layer, 5).wait()
        wait(recv_sem, spread_turn, spread.at[layer], devices - 1)
        before = jnp.concatenate(
            [
                jnp.concatenate([spread[layer, req * n_head + head] for head in range(n_head)], axis=1)
                for req in range(n_req)
            ],
            axis=0,
        ).astype(F32)
        normed = layer_norm(before, gains[0:1], biases[0:1]).astype(BF16)
        for req in range(n_req):
            for head in range(n_head):
                normed_v[req * n_head + head] = normed[
                    req * group : (req + 1) * group, head * part : (head + 1) * part
                ]
        pre_act = jnp.dot(normed, up_v[layer], preferred_element_type=F32) + bias_row
        hidden = (0.5 * pre_act * (1.0 + lax.erf(pre_act * 0.7071067811865476))).astype(BF16)
        mlp = lax.dot_general(hidden, down_v[layer], NT, preferred_element_type=F32).astype(BF16)
        for req in range(n_req):
            for head in range(n_head):
                mlp_out[layer, req * n_head + head] = mlp[
                    req * group : (req + 1) * group, head * part : (head + 1) * part
                ]
        send(mlp_turn, lambda peer: mlp_out.at[layer, peer[0] * n_head + peer[1]], mlp_in.at[layer, me], everywhere)
        mlp_in[layer, me] = mlp_out[layer, me]
        wait(recv_sem, mlp_turn, mlp_in.at[layer], devices - 1)
        total = mlp_in[layer, 0].astype(F32)
        for device in range(1, devices):
            total += mlp_in[layer, device].astype(F32)
        after = (total + normed_v[me].astype(F32)).astype(BF16)

        @pl.when(layer < LAYERS - 1)
        def _():
            near[layer, me_h] = after
            send(near_turn, lambda peer: near.at[layer, me_h], near.at[layer, me_h], plane)
            wait(recv_sem, near_turn, near.at[layer], n_head - 1)
            fresh = joined(near, (layer,)).astype(F32)
            fresh = layer_norm(fresh, gains[1:2], biases[1:2]).astype(BF16)
            for head in range(n_head):
                state_v[head] = fresh[:, head * part : (head + 1) * part]

        @pl.when(layer == LAYERS - 1)
        def _():
            spread[LAYERS, me] = after

        return carry

    lax.fori_loop(0, LAYERS, layer_step, 0)
    last = 4 * LAYERS
    send(last, lambda peer: spread.at[LAYERS, me], spread.at[LAYERS, me], everywhere)
    pick = (
        (
            lax.broadcasted_iota(jnp.int32, (slots, slots), 0)
            == jnp.broadcast_to(order_row, (slots, slots))
        )
        .astype(F32)
        .astype(BF16)
    )
    emb_load.wait()
    wait(send_sem, 0, first, devices - 1)
    for layer in range(LAYERS):
        wait(send_sem, 1 + 4 * layer, attn_in.at[layer], n_head - 1)
        wait(send_sem, 2 + 4 * layer, spread.at[layer], devices - 1)
        wait(send_sem, 3 + 4 * layer, mlp_in.at[layer], devices - 1)
        if layer < LAYERS - 1:
            wait(send_sem, 4 + 4 * layer, near.at[layer], n_head - 1)
    wait(recv_sem, last, spread.at[LAYERS], devices - 1)
    before = jnp.concatenate(
        [
            jnp.concatenate([spread[LAYERS, req * n_head + head] for head in range(n_head)], axis=1)
            for req in range(n_req)
        ],
        axis=0,
    ).astype(F32)
    gains, biases = gain_ref[LAYERS - 1], bias_ref[LAYERS - 1]
    final = layer_norm(before, gains[1:2], biases[1:2]).astype(BF16)
    ordered = jnp.dot(pick, final, preferred_element_type=F32).astype(BF16)
    logits_ref[...] = lax.dot_general(ordered, emb_v[...], NT, preferred_element_type=F32)
    wait(send_sem, last, spread.at[LAYERS], devices - 1)


def body(n_req, n_head, *args):
    (hidden_in, lengths, request_order, key_cache, value_cache, w_qkv, w_out, w_up, bias_up, w_down) = args[:10]
    norm_gain, norm_bias, embedding = args[10:]
    group = lengths.shape[0]
    width = hidden_in.shape[1]
    w_qkv = jnp.swapaxes(w_qkv, 2, 3)
    slots = request_order.shape[0]
    devices = n_req * n_head
    part = width // n_head
    tile = max(16, hidden_in.shape[0] * width // 128)
    vmem = pl.BlockSpec(memory_space=pltpu.VMEM)
    hbm = pl.BlockSpec(memory_space=pltpu.HBM)
    dma = pltpu.SemaphoreType.DMA
    pin = lambda array: pltpu.with_memory_space_constraint(array, pltpu.HBM)
    held = [key_cache, value_cache, w_qkv, w_out, w_up, w_down, embedding]
    return pl.pallas_call(
        functools.partial(kernel, n_req, n_head),
        out_shape=jax.ShapeDtypeStruct((slots, embedding.shape[0]), F32),
        in_specs=[vmem] * 3 + [hbm] * 5 + [vmem, hbm, vmem, vmem, hbm],
        out_specs=vmem,
        scratch_shapes=[pltpu.VMEM(array.shape, array.dtype) for array in held]
        + [
            dma((LAYERS, 6)),
            dma,
            pltpu.VMEM((n_head, group, part), BF16),
            pltpu.VMEM((devices, group, part), BF16),
            pltpu.VMEM((devices, tile, 128), BF16),
            pltpu.VMEM((LAYERS, n_head, group, part), BF16),
            pltpu.VMEM((LAYERS, n_head, group, part), BF16),
            pltpu.VMEM((1 + LAYERS, devices, group, part), BF16),
            pltpu.VMEM((LAYERS, devices, group, part), BF16),
            pltpu.VMEM((LAYERS, devices, group, part), BF16),
            pltpu.VMEM((LAYERS, n_head, group, part), BF16),
            dma((1 + 4 * LAYERS,)),
            dma((1 + 4 * LAYERS,)),
        ],
        compiler_params=pltpu.CompilerParams(
            collective_id=0, has_side_effects=True, vmem_limit_bytes=40 * 1024 * 1024
        ),
    )(
        pin(hidden_in),
        pin(lengths.reshape(1, group)),
        pin(request_order.reshape(1, slots)),
        pin(key_cache),
        pin(value_cache),
        pin(w_qkv),
        pin(w_out),
        pin(w_up),
        pin(bias_up),
        pin(w_down),
        pin(norm_gain),
        pin(norm_bias),
        pin(embedding),
    )


def pair_body(n_req, n_head, *args):
    (hidden_in, lengths, request_order, key_cache, value_cache, w_qkv, w_out, w_up, bias_up, w_down) = args[:10]
    norm_gain, norm_bias, embedding = args[10:]
    group = lengths.shape[0]
    width = hidden_in.shape[1]
    w_qkv = jnp.swapaxes(w_qkv, 2, 3)
    slots = request_order.shape[0]
    devices = n_req * n_head
    part = width // n_head
    tile = max(16, hidden_in.shape[0] * width // 128)
    vmem = pl.BlockSpec(memory_space=pltpu.VMEM)
    hbm = pl.BlockSpec(memory_space=pltpu.HBM)
    dma = pltpu.SemaphoreType.DMA
    pin = lambda array: pltpu.with_memory_space_constraint(array, pltpu.HBM)
    units = w_up.shape[2]
    chips = devices // 2
    sizes = [key_cache.shape, value_cache.shape, w_qkv.shape, w_out.shape]
    sizes += [(LAYERS, width, 2 * units)] * 2 + [embedding.shape]
    block = (group, part)
    return pl.pallas_call(
        functools.partial(pair_kernel, n_req, n_head),
        out_shape=jax.ShapeDtypeStruct((slots, embedding.shape[0]), F32),
        in_specs=[hbm] * 13,
        out_specs=vmem,
        scratch_shapes=[pltpu.VMEM(size, BF16) for size in sizes]
        + [
            pltpu.VMEM(hidden_in.shape, BF16),
            pltpu.VMEM((1, group), jnp.int32),
            pltpu.VMEM((1, slots), jnp.int32),
            pltpu.VMEM(bias_up.shape, BF16),
            pltpu.VMEM(norm_gain.shape, F32),
            pltpu.VMEM(norm_bias.shape, F32),
            dma((6,)),
            dma((LAYERS, 6)),
            dma,
            pltpu.VMEM((2, 8, units), F32),
            pltpu.VMEM((n_head,) + block, BF16),
            pltpu.VMEM((devices, tile, 128), BF16),
            pltpu.VMEM((LAYERS, n_head) + block, BF16),
            pltpu.VMEM((LAYERS, n_head) + block, BF16),
            pltpu.VMEM((LAYERS, n_req, n_head) + block, BF16),
            pltpu.VMEM((LAYERS, 2, n_head) + block, BF16),
            pltpu.VMEM((LAYERS, chips) + block, BF16),
            pltpu.VMEM((LAYERS, n_head) + block, F32),
            pltpu.VMEM((LAYERS,) + block, F32),
            pltpu.VMEM((LAYERS, n_head) + block, BF16),
            pltpu.VMEM((2, n_head, 2 * group, part), BF16),
            pltpu.VMEM((2 * chips,) + block, BF16),
            pltpu.VMEM((2,) + block, F32),
            dma,
            dma,
            dma((LAYERS + 1, 2)),
            dma((LAYERS + 1, 2)),
            dma((LAYERS,)),
            dma((LAYERS,)),
            dma((LAYERS,)),
            dma((LAYERS, n_req)),
            dma((LAYERS,)),
            dma((LAYERS,)),
            dma((LAYERS,)),
            dma((LAYERS,)),
            dma((LAYERS,)),
            dma((LAYERS,)),
            dma,
            dma((2,)),
            dma,
            dma((2,)),
            dma,
            dma,
            pltpu.VMEM((w_out.shape[1], key_cache.shape[4], key_cache.shape[1] * key_cache.shape[3]), BF16),
            pltpu.VMEM(embedding.shape[::-1], BF16),
            pltpu.VMEM((LAYERS, width, w_qkv.shape[1] * w_qkv.shape[2]), BF16),
            pltpu.VMEM((LAYERS, 2 * units, width), BF16),
        ],
        compiler_params=pltpu.CompilerParams(
            collective_id=0, has_side_effects=True, vmem_limit_bytes=48 * 1024 * 1024
        ),
    )(
        pin(hidden_in),
        pin(lengths.reshape(1, group)),
        pin(request_order.reshape(1, slots)),
        pin(key_cache),
        pin(value_cache),
        pin(w_qkv),
        pin(w_out),
        pin(w_up),
        pin(bias_up),
        pin(w_down),
        pin(norm_gain),
        pin(norm_bias),
        pin(embedding),
    )


def solution(mesh):
    placed = (
        P(("req", "head"), None),
        P("req"),
        P(),
        P(None, "req", "head", None, None),
        P(None, "req", "head", None, None),
        P(None, "head", None, None),
        P(None, "head", None, None),
        P(None, None, ("req", "head")),
        P(None, ("req", "head")),
        P(None, None, ("req", "head")),
        P(),
        P(),
        P(("req", "head"), None),
    )
    inner = pair_body if (mesh.shape["req"], mesh.shape["head"]) == (4, 8) else body
    return jax.shard_map(
        functools.partial(inner, mesh.shape["req"], mesh.shape["head"]),
        mesh=mesh,
        in_specs=placed,
        out_specs=P(None, ("req", "head")),
        check_vma=False,
    )
```

```python
import functools

import jax
import jax.numpy as jnp
from jax import lax
from jax.experimental import pallas as pl
from jax.experimental.pallas import tpu as pltpu
from jax.sharding import PartitionSpec as P

LAYERS = 2
MESH = pl.DeviceIdType.MESH
F32 = jnp.float32
BF16 = jnp.bfloat16
NT = (((1,), (1,)), ((), ()))


def layer_norm(values, gain_vec, bias_vec):
    average = jnp.mean(values, axis=-1, keepdims=True)
    centred = values - average
    variance = jnp.mean(centred * centred, axis=-1, keepdims=True)
    return centred * lax.rsqrt(variance + 1e-05) * gain_vec + bias_vec


def quick_norm(values, gain_vec, bias_vec):
    average = jnp.mean(values, axis=-1, keepdims=True)
    square = jnp.mean(values * values, axis=-1, keepdims=True)
    scale = lax.rsqrt(jnp.maximum(square - average * average, 0.0) + 1e-05)
    return (values - average) * scale * gain_vec + bias_vec


def peer_offsets(n_req, n_head):
    every = [(a, b) for a in range(n_req) for b in range(n_head) if a or b]
    return sorted(every, key=lambda o: (-(o[0] + bin(o[1] >> 1).count("1")), -o[1]))


def flip(index, mask):
    bit = 1
    while bit <= mask:
        if mask & bit:
            index = index + bit - 2 * bit * lax.rem(index // bit, 2)
        bit *= 2
    return index


def pair_kernel(
    n_req,
    n_head,
    hidden_hbm,
    lengths_hbm,
    order_hbm,
    key_hbm,
    value_hbm,
    qkv_hbm,
    out_w_hbm,
    up_hbm,
    bias_up_hbm,
    down_hbm,
    gain_hbm,
    bias_hbm,
    emb_hbm,
    logits_ref,
    key_v,
    value_v,
    qkv_v,
    out_w_v,
    up_v,
    down_v,
    emb_v,
    hidden_ref,
    lengths_ref,
    order_ref,
    bias_up_ref,
    gain_ref,
    bias_ref,
    small_sem,
    load_sem,
    emb_sem,
    bias_v,
    state_v,
    first,
    attn_out,
    attn_in,
    spread,
    mlp_out,
    mlp_in,
    own_out,
    own_in,
    near,
    last,
    end_in,
    end_own_in,
    first_send,
    first_recv,
    pair_send,
    pair_recv,
    attn_send,
    attn_recv,
    spread_send,
    spread_recv,
    mlp_send,
    mlp_recv,
    own_send,
    own_recv,
    near_send,
    near_recv,
    last_send,
    last_recv,
    pass_send,
    pass_recv,
    end_send,
    end_recv,
    value_t,
    emb_t,
    qkv_t,
    down_t,
):
    me_r = lax.axis_index("req")
    me_h = lax.axis_index("head")
    me = me_r * n_head + me_h
    core = lax.rem(me_h, 2)
    chip = me // 2
    partner = (me_r, flip(me_h, 1))
    rows, width = hidden_hbm.shape
    group, heads, head_size, cached = key_v.shape[1:]
    units = up_hbm.shape[2]
    slots = n_req * group
    devices = n_req * n_head
    chips = devices // 2
    part = width // n_head
    offsets = peer_offsets(n_req, n_head)
    edge = (me_r + 1) // (n_req // 2) != 1

    def across(step):
        if step < 2:
            return flip(me_r, step)
        return jnp.where(edge, flip(me_r, step), flip(me_r, 5 - step))

    everywhere = [(across(a), flip(me_h, b)) for a, b in offsets]
    plane = [(me_r, flip(me_h, b)) for a, b in offsets if not a]
    middle = n_req // 2
    owner = (me_r + 1) // middle == 1
    near_owner = me_r // middle
    reach = (0, 1, 1, 2)
    end_offsets = sorted(
        [(a, b) for a, b in offsets if b % 2 == 0], key=lambda o: -(reach[o[0]] + bin(o[1]).count("1"))
    )
    taker = lax.rem((me_r + 1) // middle, 2)
    mine = taker == core
    near_group = jnp.where(me_r < middle, core, n_req - 1 - core)
    far_group = n_req - 1 - near_group

    smalls = [
        pltpu.make_async_copy(source, target, small_sem.at[place])
        for place, (source, target) in enumerate(
            (
                (hidden_hbm, hidden_ref),
                (order_hbm, order_ref),
                (lengths_hbm, lengths_ref),
                (bias_up_hbm, bias_up_ref),
                (gain_hbm, gain_ref),
                (bias_hbm, bias_ref),
            )
        )
    ]
    for copy in smalls:
        copy.start()

    barrier = pltpu.get_barrier_semaphore()
    for peer in everywhere:
        pl.semaphore_signal(barrier, inc=1, device_id=peer, device_id_type=MESH)

    def up_part(ref, layer, which):
        return ref.at[layer, :, pl.ds(which * units, units)]

    def load(layer, which):
        source, target = (
            (qkv_hbm.at[layer], qkv_v.at[layer]),
            (key_hbm.at[layer], key_v.at[layer]),
            (value_hbm.at[layer], value_v.at[layer]),
            (out_w_hbm.at[layer], out_w_v.at[layer]),
            (up_hbm.at[layer], up_part(up_v, layer, 0)),
            (down_hbm.at[layer], up_part(down_v, layer, 0)),
        )[which]
        return pltpu.make_async_copy(source, target, load_sem.at[layer, which])

    emb_load = pltpu.make_async_copy(emb_hbm, emb_v, emb_sem)

    def remote(source, target, sender, receiver, peer):
        return pltpu.make_async_remote_copy(
            src_ref=source,
            dst_ref=target,
            send_sem=sender,
            recv_sem=receiver,
            device_id=peer,
            device_id_type=MESH,
        )

    def wait(sem, ref, count):
        block = ref.at[pl.ds(0, count)]
        pltpu.make_async_copy(block, block, sem).wait()

    def either(held, given):
        pl.when(mine)(held)
        pl.when(jnp.logical_not(mine))(given)

    def pair_copies(layer):
        return (
            remote(up_hbm.at[layer], up_part(up_v, layer, 1), pair_send.at[layer, 0], pair_recv.at[layer, 0], partner),
            remote(
                down_hbm.at[layer], up_part(down_v, layer, 1), pair_send.at[layer, 1], pair_recv.at[layer, 1], partner
            ),
        )

    bias_copy = remote(bias_v.at[0], bias_v.at[1], pair_send.at[LAYERS, 0], pair_recv.at[LAYERS, 0], partner)

    chunks = width // 128
    tile = first.shape[1]
    smalls[0].wait()
    for layer in range(LAYERS):
        for which in range(6):
            load(layer, which).start()
    emb_load.start()
    hidden = hidden_ref[...].astype(F32)
    pieces = [hidden[:, c * 128 : (c + 1) * 128] for c in range(chunks)]
    if tile > chunks * rows:
        pieces.append(jnp.zeros((tile - chunks * rows, 128), F32))
    first[me] = jnp.concatenate(pieces, axis=0).astype(BF16)
    pl.semaphore_wait(barrier, devices - 1)
    for peer in everywhere:
        remote(first.at[me], first.at[me], first_send, first_recv, peer).start()
    for copy in smalls[1:]:
        copy.wait()
    bias_v[0] = jnp.concatenate(
        [bias_up_ref[...].astype(F32), jnp.zeros((bias_v.shape[1] - LAYERS, units), F32)], axis=0
    )
    for layer in range(LAYERS - 1):
        mlp_in[layer, chip] = jnp.zeros((group, part), BF16)
    for which in range(2):
        end_in[which * chips + chip] = jnp.zeros((group, part), BF16)

    order_row = order_ref[...]
    ids_row = lax.broadcasted_iota(jnp.int32, (group, slots), 0) + me_r * group
    ids_col = lax.broadcasted_iota(jnp.int32, (group, slots), 1)
    order_here = jnp.sum(
        jnp.where(ids_row == ids_col, jnp.broadcast_to(order_row, (group, slots)).astype(F32), 0.0),
        axis=1,
        keepdims=True,
    ).astype(jnp.int32)
    wanted = (order_here // rows) * tile + lax.rem(order_here, rows)
    wide = lax.broadcasted_iota(jnp.int32, (group, devices * tile), 1)
    wanted = jnp.broadcast_to(wanted, (group, devices * tile))
    choose = jnp.concatenate(
        [(wide == wanted + c * rows).astype(F32) for c in range(chunks)], axis=0
    ).astype(BF16)

    square = lax.broadcasted_iota(jnp.int32, (group, group), 0) == lax.broadcasted_iota(
        jnp.int32, (group, group), 1
    )
    limit = jnp.sum(
        jnp.where(square, jnp.broadcast_to(lengths_ref[...], (group, group)).astype(F32), 0.0), axis=1, keepdims=True
    ).astype(jnp.int32)
    limit = jnp.broadcast_to(limit, (group, cached))
    valid = lax.broadcasted_iota(jnp.int32, (group, cached), 1) < limit
    flat = group * head_size
    diagonal = lax.broadcasted_iota(jnp.int32, (group, flat), 0) == (
        lax.broadcasted_iota(jnp.int32, (group, flat), 1) // head_size
    )
    score_scale = head_size ** (-0.5)

    for layer in range(LAYERS):
        for copy in pair_copies(layer):
            copy.start()
    bias_copy.start()
    def turn_values(layer, head):
        for start in range(0, group, 4):
            block = value_v[layer, start : start + 4, head].reshape(4 * head_size, cached)
            value_t[head, :, pl.ds(start * head_size, 4 * head_size)] = block.T

    def turn_embedding(start, stop):
        for row in range(start, stop, 256):
            size = min(256, stop - row)
            emb_t[:, pl.ds(row, size)] = emb_v[pl.ds(row, size)].T

    words = emb_v.shape[0]

    def turn_heads(layer):
        weights = qkv_v[layer].reshape(heads * 3 * head_size, width)
        qkv_t[layer] = weights.T

    def turn_down(layer):
        load(layer, 5).wait()
        pair_copies(layer)[1].wait_recv()
        down_t[layer] = down_v[layer].T

    load(0, 0).wait()
    turn_heads(0)
    load(0, 2).wait()
    for head in range(heads):
        turn_values(0, head)
    wait(first_recv, first, devices - 1)
    chosen = jnp.dot(choose, first[...].reshape(devices * tile, 128), preferred_element_type=F32)
    state = jnp.concatenate([chosen[c * group : (c + 1) * group] for c in range(chunks)], axis=1)
    for head in range(n_head):
        state_v[head] = state[:, head * part : (head + 1) * part].astype(BF16)

    def joined(ref, lead):
        return jnp.concatenate([ref[lead + (head,)] for head in range(n_head)], axis=1)

    def layer_step(layer, carry):
        state = joined(state_v, ())
        load(layer, 1).wait()
        load(layer, 3).wait()
        attn = jnp.zeros((group, width), F32)
        parts = []
        both = jnp.dot(state, qkv_t[layer], preferred_element_type=F32).astype(BF16).astype(F32)
        for head in range(heads):
            start = 3 * head * head_size
            parts.append([both[:, start + b * head_size : start + (b + 1) * head_size] for b in range(3)])
        expos = []
        for head in range(heads):
            query, own_key, own_value = parts[head]
            tiled = jnp.where(diagonal, jnp.concatenate([query] * group, axis=1), 0.0).astype(BF16)
            keys = key_v[layer, :, head].reshape(flat, cached)
            scores = jnp.dot(tiled, keys, preferred_element_type=F32) * score_scale
            scores = jnp.where(valid, scores, -jnp.inf)
            own = jnp.sum(query * own_key, axis=-1, keepdims=True) * score_scale
            row_max = jnp.maximum(jnp.max(scores, axis=-1, keepdims=True), own)
            expo = jnp.exp(scores - row_max)
            own_exp = jnp.exp(own - row_max)
            denom = jnp.sum(expo, axis=-1, keepdims=True) + own_exp
            expos.append((expo.astype(BF16), own_exp.astype(BF16).astype(F32), denom))
        for head in range(heads):
            expo, own_exp, denom = expos[head]
            every = jnp.dot(expo, value_t[head], preferred_element_type=F32)
            every = jnp.where(diagonal, every, 0.0)
            lanes = 2 * head_size
            folded = every[:, :lanes]
            for block in range(1, group // 2):
                folded += every[:, block * lanes : (block + 1) * lanes]
            mixed = folded[:, :head_size] + folded[:, head_size:] + own_exp * parts[head][2]
            head_out = (mixed / denom).astype(BF16)
            attn += jnp.dot(head_out, out_w_v[layer, head], preferred_element_type=F32)
        for head in range(n_head):
            attn_out[layer, head] = attn[:, head * part : (head + 1) * part].astype(BF16)
        for peer in plane:
            remote(
                attn_out.at[layer, peer[1]], attn_in.at[layer, me_h], attn_send.at[layer], attn_recv.at[layer], peer
            ).start()
        attn_in[layer, me_h] = attn_out[layer, me_h]
        if layer < LAYERS - 1:
            load(layer + 1, 2).wait()
            turn_values(layer + 1, 0)
        turn_down(layer)
        wait(attn_recv.at[layer], attn_in.at[layer], n_head - 1)
        total = attn_in[layer, 0].astype(F32)
        for head in range(1, n_head):
            total += attn_in[layer, head].astype(F32)
        spread[layer, me_r, me_h] = (total + state_v[me_h].astype(F32)).astype(BF16)

        def spread_copy(a, b):
            base = flip(me_h, b)
            peer = (across(a), base - lax.rem(base, 2) + taker)
            block = spread.at[layer, me_r, me_h]
            return remote(block, block, spread_send.at[layer], spread_recv.at[layer, me_r], peer)

        for a, b in offsets:
            if b % 2 == 0:
                spread_copy(a, b).start()

        @pl.when(jnp.logical_not(mine))
        def _():
            spread_copy(0, 0).start()

        gains, biases = gain_ref[layer], bias_ref[layer]
        bias_rows = []
        for source in range(2):
            bias_up = bias_v[source]
            bias_row = bias_up[0:1]
            for other in range(1, LAYERS):
                bias_row = jnp.where(layer == other, bias_up[other : other + 1], bias_row)
            bias_rows.append(bias_row)
        bias_row = jnp.concatenate(bias_rows, axis=1)

        def mlp_copy(which, block, b):
            peer = (block, flip(me_h, b))
            return remote(
                mlp_out.at[layer, which, peer[1]], mlp_in.at[layer, chip], mlp_send.at[layer], mlp_recv.at[layer], peer
            )

        def end_copy(which, block, b):
            peer = (jnp.where(block < middle, middle - 1, middle), flip(me_h, b))
            return remote(
                mlp_out.at[layer, which, peer[1]],
                end_in.at[lax.rem(block, 2) * chips + chip],
                end_send,
                end_recv,
                peer,
            )

        def own_copy():
            return remote(own_out.at[layer, partner[1]], own_in.at[layer], own_send.at[layer], own_recv.at[layer], partner)

        load(layer, 4).wait()
        if layer < LAYERS - 1:
            for head in range(1, heads):
                turn_values(layer + 1, head)
            load(layer + 1, 0).wait()
            turn_heads(layer + 1)
        pair_copies(layer)[0].wait_recv()
        either(
            lambda: wait(spread_recv.at[layer, near_group], spread.at[layer, 0], n_head - 1),
            lambda: wait(spread_recv.at[layer, near_group], spread.at[layer, 0], n_head),
        )

        def feed(which, block):
            before = jnp.concatenate([spread[layer, block, head] for head in range(n_head)], axis=1).astype(F32)
            normed = quick_norm(before, gains[0:1], biases[0:1]).astype(BF16)
            pre_act = jnp.dot(normed, up_v[layer], preferred_element_type=F32) + bias_row
            hidden = (0.5 * pre_act * (1.0 + lax.erf(pre_act * 0.7071067811865476))).astype(BF16)
            mlp = jnp.dot(hidden, down_t[layer], preferred_element_type=F32)
            for head in range(n_head):
                mlp_out[layer, which, head] = mlp[:, head * part : (head + 1) * part].astype(BF16)
            return mlp + normed.astype(F32)

        ending = layer == LAYERS - 1
        copy_out = end_copy if ending else mlp_copy
        local = owner if ending else mine
        whole = feed(0, near_group)
        for b in range(n_head - 1, 1, -1):
            copy_out(0, near_group, b).start()
        for head in range(n_head):
            own_out[layer, head] = whole[:, head * part : (head + 1) * part]

        @pl.when(local)
        def _():
            if ending:
                end_own().start()
                end_own_in[lax.rem(near_group, 2)] = own_out[layer, me_h]
            else:
                own_copy().start()
                own_in[layer] = own_out[layer, me_h]

        @pl.when(jnp.logical_not(local))
        def _():
            for b in range(2):
                copy_out(0, near_group, b).start()

        wait(spread_recv.at[layer, far_group], spread.at[layer, 0], n_head)
        feed(1, far_group)
        for b in range(n_head - 1, -1, -1):
            copy_out(1, far_group, b).start()
        if ending:
            return finish()
        emb_load.wait()
        turn_embedding(0, words // 2)

        @pl.when(jnp.logical_not(mine))
        def _():
            own_copy().wait_recv()

        wait(mlp_recv.at[layer], mlp_in.at[layer], chips - 1)
        total = own_in[layer]
        for source in range(chips):
            total += mlp_in[layer, source].astype(F32)
        near[layer, me_h] = total.astype(BF16)
        for peer in plane:
            block = near.at[layer, me_h]
            remote(block, block, near_send.at[layer], near_recv.at[layer], peer).start()
        turn_embedding(words // 2, words)
        wait(near_recv.at[layer], near.at[layer], n_head - 1)
        fresh = joined(near, (layer,)).astype(F32)
        fresh = quick_norm(fresh, gains[1:2], biases[1:2]).astype(BF16)
        for head in range(n_head):
            state_v[head] = fresh[:, head * part : (head + 1) * part]
        return carry

    def finish():
        @pl.when(owner)
        def _():
            end_own().wait_recv()
            wait(end_recv, end_in, 2 * chips - 2)
            for which in range(2):
                total = end_own_in[which]
                for source in range(chips):
                    total += end_in[which * chips + source].astype(F32)
                last[near_owner, me_h, pl.ds(which * group, group)] = total.astype(BF16)
            block = last.at[near_owner, me_h]
            for a, b in end_offsets:
                peer = (across(a), flip(me_h, b + 1))
                remote(block, block, last_send, last_recv.at[near_owner], peer).start()
            remote(block, block, last_send, pass_recv.at[near_owner], partner).start()

    def end_own():
        return remote(
            own_out.at[LAYERS - 1, partner[1]],
            end_own_in.at[lax.rem(near_group, 2)],
            own_send.at[LAYERS - 1],
            own_recv.at[LAYERS - 1],
            partner,
        )

    def forward(plane_of, b):
        block = last.at[plane_of, flip(me_h, b + 1)]
        remote(block, block, pass_send, pass_recv.at[plane_of], partner).start()

    bias_copy.wait_recv()
    for layer in range(LAYERS):
        layer_step(layer, 0)

    @pl.when(owner)
    def _():
        wait(last_recv.at[near_owner], last.at[0], n_head // 2 - 1)
        for b in range(2, n_head, 2):
            forward(near_owner, b)

    @pl.when(jnp.logical_not(owner))
    def _():
        wait(last_recv.at[near_owner], last.at[0], n_head // 2)
        for b in range(0, n_head, 2):
            forward(near_owner, b)

    wait(last_recv.at[1 - near_owner], last.at[0], n_head // 2)
    for b in range(0, n_head, 2):
        forward(1 - near_owner, b)
    pick = (
        (
            lax.broadcasted_iota(jnp.int32, (slots, slots), 0)
            == jnp.broadcast_to(order_row, (slots, slots))
        )
        .astype(F32)
        .astype(BF16)
    )
    wait(first_send, first, devices - 1)
    bias_copy.wait_send()
    for layer in range(LAYERS):
        for copy in pair_copies(layer):
            copy.wait_send()
        wait(attn_send.at[layer], attn_in.at[layer], n_head - 1)
        @pl.when(mine)
        def _():
            wait(spread_send.at[layer], mlp_in.at[0], chips - 1)

        @pl.when(jnp.logical_not(mine))
        def _():
            wait(spread_send.at[layer], mlp_in.at[0], chips)

        if layer < LAYERS - 1:
            wait(near_send.at[layer], near.at[layer], n_head - 1)

            @pl.when(mine)
            def _():
                wait(mlp_send.at[layer], mlp_in.at[0], 2 * n_head - 2)
                remote(
                    own_out.at[layer, 0], own_in.at[layer], own_send.at[layer], own_recv.at[layer], partner
                ).wait_send()

            @pl.when(jnp.logical_not(mine))
            def _():
                wait(mlp_send.at[layer], mlp_in.at[0], 2 * n_head)

    @pl.when(owner)
    def _():
        wait(end_send, end_in, 2 * n_head - 2)
        end_own().wait_send()

    @pl.when(jnp.logical_not(owner))
    def _():
        wait(end_send, end_in, 2 * n_head)

    for plane_of in range(2):
        wait(pass_recv.at[plane_of], last.at[0], n_head // 2)
    before = jnp.concatenate(
        [jnp.concatenate([last[plane_of, head] for head in range(n_head)], axis=1) for plane_of in range(2)],
        axis=0,
    ).astype(F32)
    gains, biases = gain_ref[LAYERS - 1], bias_ref[LAYERS - 1]
    final = quick_norm(before, gains[1:2], biases[1:2]).astype(BF16)
    ordered = jnp.dot(pick, final, preferred_element_type=F32).astype(BF16)
    logits_ref[...] = jnp.dot(ordered, emb_t[...], preferred_element_type=F32)

    @pl.when(owner)
    def _():
        wait(last_send, last, 2)
        wait(pass_send, last.at[0], n_head - 1)

    @pl.when(jnp.logical_not(owner))
    def _():
        wait(pass_send, last.at[0], n_head)


def kernel(
    n_req,
    n_head,
    hidden_ref,
    lengths_ref,
    order_ref,
    key_hbm,
    value_hbm,
    qkv_hbm,
    out_w_hbm,
    up_hbm,
    bias_up_ref,
    down_hbm,
    gain_ref,
    bias_ref,
    emb_hbm,
    logits_ref,
    key_v,
    value_v,
    qkv_v,
    out_w_v,
    up_v,
    down_v,
    emb_v,
    load_sem,
    emb_sem,
    state_v,
    normed_v,
    first,
    attn_out,
    attn_in,
    spread,
    mlp_out,
    mlp_in,
    near,
    send_sem,
    recv_sem,
):
    me_r = lax.axis_index("req")
    me_h = lax.axis_index("head")
    me = me_r * n_head + me_h
    rows, width = hidden_ref.shape
    group, heads, head_size, cached = key_v.shape[1:]
    slots = n_req * group
    devices = n_req * n_head
    part = width // n_head
    offsets = peer_offsets(n_req, n_head)
    everywhere = [(flip(me_r, a), flip(me_h, b)) for a, b in offsets]
    plane = [(me_r, flip(me_h, b)) for a, b in offsets if not a]

    barrier = pltpu.get_barrier_semaphore()
    for peer in everywhere:
        pl.semaphore_signal(barrier, inc=1, device_id=peer, device_id_type=MESH)

    pairs = (
        (qkv_hbm, qkv_v),
        (key_hbm, key_v),
        (value_hbm, value_v),
        (out_w_hbm, out_w_v),
        (up_hbm, up_v),
        (down_hbm, down_v),
    )

    def load(layer, which):
        source, target = pairs[which]
        return pltpu.make_async_copy(source.at[layer], target.at[layer], load_sem.at[layer, which])

    for layer in range(LAYERS):
        for which in range(len(pairs)):
            load(layer, which).start()
    emb_load = pltpu.make_async_copy(emb_hbm, emb_v, emb_sem)
    emb_load.start()

    def send(turn, source, target, peers):
        for peer in peers:
            pltpu.make_async_remote_copy(
                src_ref=source(peer),
                dst_ref=target,
                send_sem=send_sem.at[turn],
                recv_sem=recv_sem.at[turn],
                device_id=peer,
                device_id_type=MESH,
            ).start()

    def wait(sem, turn, ref, count):
        block = ref.at[pl.ds(0, count)]
        pltpu.make_async_copy(block, block, sem.at[turn]).wait()

    chunks = width // 128
    tile = first.shape[1]
    hidden = hidden_ref[...].astype(F32)
    pieces = [hidden[:, c * 128 : (c + 1) * 128] for c in range(chunks)]
    if tile > chunks * rows:
        pieces.append(jnp.zeros((tile - chunks * rows, 128), F32))
    first[me] = jnp.concatenate(pieces, axis=0).astype(BF16)

    order_row = order_ref[...]
    ids_row = lax.broadcasted_iota(jnp.int32, (group, slots), 0) + me_r * group
    ids_col = lax.broadcasted_iota(jnp.int32, (group, slots), 1)
    order_here = jnp.sum(
        jnp.where(ids_row == ids_col, jnp.broadcast_to(order_row, (group, slots)).astype(F32), 0.0),
        axis=1,
        keepdims=True,
    ).astype(jnp.int32)
    wanted = (order_here // rows) * tile + lax.rem(order_here, rows)
    wide = lax.broadcasted_iota(jnp.int32, (group, devices * tile), 1)
    wanted = jnp.broadcast_to(wanted, (group, devices * tile))
    choose = jnp.concatenate(
        [(wide == wanted + c * rows).astype(F32) for c in range(chunks)], axis=0
    ).astype(BF16)

    square = lax.broadcasted_iota(jnp.int32, (group, group), 0) == lax.broadcasted_iota(
        jnp.int32, (group, group), 1
    )
    limit = jnp.sum(
        jnp.where(square, jnp.broadcast_to(lengths_ref[...], (group, group)).astype(F32), 0.0), axis=1, keepdims=True
    ).astype(jnp.int32)
    limit = jnp.broadcast_to(limit, (group, cached))
    valid = lax.broadcasted_iota(jnp.int32, (group, cached), 1) < limit
    flat = group * head_size
    diagonal = lax.broadcasted_iota(jnp.int32, (group, flat), 0) == (
        lax.broadcasted_iota(jnp.int32, (group, flat), 1) // head_size
    )
    score_scale = head_size ** (-0.5)

    pl.semaphore_wait(barrier, devices - 1)
    send(0, lambda peer: first.at[me], first.at[me], everywhere)
    wait(recv_sem, 0, first, devices - 1)
    chosen = jnp.dot(choose, first[...].reshape(devices * tile, 128), preferred_element_type=F32)
    state = jnp.concatenate([chosen[c * group : (c + 1) * group] for c in range(chunks)], axis=1)
    for head in range(n_head):
        state_v[head] = state[:, head * part : (head + 1) * part].astype(BF16)

    def joined(ref, lead):
        return jnp.concatenate([ref[lead + (head,)] for head in range(n_head)], axis=1)

    def layer_step(layer, carry):
        attn_turn, spread_turn, mlp_turn, near_turn = 1 + 4 * layer, 2 + 4 * layer, 3 + 4 * layer, 4 + 4 * layer
        state = joined(state_v, ())
        load(layer, 0).wait()
        attn = jnp.zeros((group, width), F32)
        parts = []
        for head in range(heads):
            projected = (
                lax.dot_general(state, qkv_v[layer, head], NT, preferred_element_type=F32).astype(BF16).astype(F32)
            )
            parts.append(
                (
                    projected[:, :head_size],
                    projected[:, head_size : 2 * head_size],
                    projected[:, 2 * head_size :],
                )
            )
        load(layer, 1).wait()
        expos = []
        for head in range(heads):
            query, own_key, own_value = parts[head]
            tiled = jnp.where(diagonal, jnp.concatenate([query] * group, axis=1), 0.0).astype(BF16)
            keys = key_v[layer, :, head].reshape(flat, cached)
            scores = jnp.dot(tiled, keys, preferred_element_type=F32) * score_scale
            scores = jnp.where(valid, scores, -jnp.inf)
            own = jnp.sum(query * own_key, axis=-1, keepdims=True) * score_scale
            row_max = jnp.maximum(jnp.max(scores, axis=-1, keepdims=True), own)
            expo = jnp.exp(scores - row_max)
            own_exp = jnp.exp(own - row_max)
            denom = jnp.sum(expo, axis=-1, keepdims=True) + own_exp
            expos.append((expo.astype(BF16), own_exp.astype(BF16).astype(F32), denom))
        load(layer, 2).wait()
        load(layer, 3).wait()
        for head in range(heads):
            expo, own_exp, denom = expos[head]
            values = value_v[layer, :, head].reshape(flat, cached)
            every = lax.dot_general(expo, values, NT, preferred_element_type=F32)
            every = jnp.where(diagonal, every, 0.0)
            mixed = every[:, :head_size]
            for block in range(1, group):
                mixed += every[:, block * head_size : (block + 1) * head_size]
            mixed += own_exp * parts[head][2]
            head_out = (mixed / denom).astype(BF16)
            attn += jnp.dot(head_out, out_w_v[layer, head], preferred_element_type=F32)
        for head in range(n_head):
            attn_out[layer, head] = attn[:, head * part : (head + 1) * part].astype(BF16)
        send(attn_turn, lambda peer: attn_out.at[layer, peer[1]], attn_in.at[layer, me_h], plane)
        attn_in[layer, me_h] = attn_out[layer, me_h]
        wait(recv_sem, attn_turn, attn_in.at[layer], n_head - 1)
        total = attn_in[layer, 0].astype(F32)
        for head in range(1, n_head):
            total += attn_in[layer, head].astype(F32)
        spread[layer, me] = (total + state_v[me_h].astype(F32)).astype(BF16)
        send(spread_turn, lambda peer: spread.at[layer, me], spread.at[layer, me], everywhere)
        gains, biases = gain_ref[layer], bias_ref[layer]
        bias_up = bias_up_ref[...].astype(F32)
        bias_row = bias_up[0:1]
        for other in range(1, LAYERS):
            bias_row = jnp.where(layer == other, bias_up[other : other + 1], bias_row)
        load(layer, 4).wait()
        load(layer, 5).wait()
        wait(recv_sem, spread_turn, spread.at[layer], devices - 1)
        before = jnp.concatenate(
            [
                jnp.concatenate([spread[layer, req * n_head + head] for head in range(n_head)], axis=1)
                for req in range(n_req)
            ],
            axis=0,
        ).astype(F32)
        normed = layer_norm(before, gains[0:1], biases[0:1]).astype(BF16)
        for req in range(n_req):
            for head in range(n_head):
                normed_v[req * n_head + head] = normed[
                    req * group : (req + 1) * group, head * part : (head + 1) * part
                ]
        pre_act = jnp.dot(normed, up_v[layer], preferred_element_type=F32) + bias_row
        hidden = (0.5 * pre_act * (1.0 + lax.erf(pre_act * 0.7071067811865476))).astype(BF16)
        mlp = lax.dot_general(hidden, down_v[layer], NT, preferred_element_type=F32).astype(BF16)
        for req in range(n_req):
            for head in range(n_head):
                mlp_out[layer, req * n_head + head] = mlp[
                    req * group : (req + 1) * group, head * part : (head + 1) * part
                ]
        send(mlp_turn, lambda peer: mlp_out.at[layer, peer[0] * n_head + peer[1]], mlp_in.at[layer, me], everywhere)
        mlp_in[layer, me] = mlp_out[layer, me]
        wait(recv_sem, mlp_turn, mlp_in.at[layer], devices - 1)
        total = mlp_in[layer, 0].astype(F32)
        for device in range(1, devices):
            total += mlp_in[layer, device].astype(F32)
        after = (total + normed_v[me].astype(F32)).astype(BF16)

        @pl.when(layer < LAYERS - 1)
        def _():
            near[layer, me_h] = after
            send(near_turn, lambda peer: near.at[layer, me_h], near.at[layer, me_h], plane)
            wait(recv_sem, near_turn, near.at[layer], n_head - 1)
            fresh = joined(near, (layer,)).astype(F32)
            fresh = layer_norm(fresh, gains[1:2], biases[1:2]).astype(BF16)
            for head in range(n_head):
                state_v[head] = fresh[:, head * part : (head + 1) * part]

        @pl.when(layer == LAYERS - 1)
        def _():
            spread[LAYERS, me] = after

        return carry

    lax.fori_loop(0, LAYERS, layer_step, 0)
    last = 4 * LAYERS
    send(last, lambda peer: spread.at[LAYERS, me], spread.at[LAYERS, me], everywhere)
    pick = (
        (
            lax.broadcasted_iota(jnp.int32, (slots, slots), 0)
            == jnp.broadcast_to(order_row, (slots, slots))
        )
        .astype(F32)
        .astype(BF16)
    )
    emb_load.wait()
    wait(send_sem, 0, first, devices - 1)
    for layer in range(LAYERS):
        wait(send_sem, 1 + 4 * layer, attn_in.at[layer], n_head - 1)
        wait(send_sem, 2 + 4 * layer, spread.at[layer], devices - 1)
        wait(send_sem, 3 + 4 * layer, mlp_in.at[layer], devices - 1)
        if layer < LAYERS - 1:
            wait(send_sem, 4 + 4 * layer, near.at[layer], n_head - 1)
    wait(recv_sem, last, spread.at[LAYERS], devices - 1)
    before = jnp.concatenate(
        [
            jnp.concatenate([spread[LAYERS, req * n_head + head] for head in range(n_head)], axis=1)
            for req in range(n_req)
        ],
        axis=0,
    ).astype(F32)
    gains, biases = gain_ref[LAYERS - 1], bias_ref[LAYERS - 1]
    final = layer_norm(before, gains[1:2], biases[1:2]).astype(BF16)
    ordered = jnp.dot(pick, final, preferred_element_type=F32).astype(BF16)
    logits_ref[...] = lax.dot_general(ordered, emb_v[...], NT, preferred_element_type=F32)
    wait(send_sem, last, spread.at[LAYERS], devices - 1)


def body(n_req, n_head, *args):
    (hidden_in, lengths, request_order, key_cache, value_cache, w_qkv, w_out, w_up, bias_up, w_down) = args[:10]
    norm_gain, norm_bias, embedding = args[10:]
    group = lengths.shape[0]
    width = hidden_in.shape[1]
    w_qkv = jnp.swapaxes(w_qkv, 2, 3)
    slots = request_order.shape[0]
    devices = n_req * n_head
    part = width // n_head
    tile = max(16, hidden_in.shape[0] * width // 128)
    vmem = pl.BlockSpec(memory_space=pltpu.VMEM)
    hbm = pl.BlockSpec(memory_space=pltpu.HBM)
    dma = pltpu.SemaphoreType.DMA
    pin = lambda array: pltpu.with_memory_space_constraint(array, pltpu.HBM)
    held = [key_cache, value_cache, w_qkv, w_out, w_up, w_down, embedding]
    return pl.pallas_call(
        functools.partial(kernel, n_req, n_head),
        out_shape=jax.ShapeDtypeStruct((slots, embedding.shape[0]), F32),
        in_specs=[vmem] * 3 + [hbm] * 5 + [vmem, hbm, vmem, vmem, hbm],
        out_specs=vmem,
        scratch_shapes=[pltpu.VMEM(array.shape, array.dtype) for array in held]
        + [
            dma((LAYERS, 6)),
            dma,
            pltpu.VMEM((n_head, group, part), BF16),
            pltpu.VMEM((devices, group, part), BF16),
            pltpu.VMEM((devices, tile, 128), BF16),
            pltpu.VMEM((LAYERS, n_head, group, part), BF16),
            pltpu.VMEM((LAYERS, n_head, group, part), BF16),
            pltpu.VMEM((1 + LAYERS, devices, group, part), BF16),
            pltpu.VMEM((LAYERS, devices, group, part), BF16),
            pltpu.VMEM((LAYERS, devices, group, part), BF16),
            pltpu.VMEM((LAYERS, n_head, group, part), BF16),
            dma((1 + 4 * LAYERS,)),
            dma((1 + 4 * LAYERS,)),
        ],
        compiler_params=pltpu.CompilerParams(
            collective_id=0, has_side_effects=True, vmem_limit_bytes=40 * 1024 * 1024
        ),
    )(
        pin(hidden_in),
        pin(lengths.reshape(1, group)),
        pin(request_order.reshape(1, slots)),
        pin(key_cache),
        pin(value_cache),
        pin(w_qkv),
        pin(w_out),
        pin(w_up),
        pin(bias_up),
        pin(w_down),
        pin(norm_gain),
        pin(norm_bias),
        pin(embedding),
    )


def pair_body(n_req, n_head, *args):
    (hidden_in, lengths, request_order, key_cache, value_cache, w_qkv, w_out, w_up, bias_up, w_down) = args[:10]
    norm_gain, norm_bias, embedding = args[10:]
    group = lengths.shape[0]
    width = hidden_in.shape[1]
    w_qkv = jnp.swapaxes(w_qkv, 2, 3)
    slots = request_order.shape[0]
    devices = n_req * n_head
    part = width // n_head
    tile = max(16, hidden_in.shape[0] * width // 128)
    vmem = pl.BlockSpec(memory_space=pltpu.VMEM)
    hbm = pl.BlockSpec(memory_space=pltpu.HBM)
    dma = pltpu.SemaphoreType.DMA
    pin = lambda array: pltpu.with_memory_space_constraint(array, pltpu.HBM)
    units = w_up.shape[2]
    chips = devices // 2
    sizes = [key_cache.shape, value_cache.shape, w_qkv.shape, w_out.shape]
    sizes += [(LAYERS, width, 2 * units)] * 2 + [embedding.shape]
    block = (group, part)
    return pl.pallas_call(
        functools.partial(pair_kernel, n_req, n_head),
        out_shape=jax.ShapeDtypeStruct((slots, embedding.shape[0]), F32),
        in_specs=[hbm] * 13,
        out_specs=vmem,
        scratch_shapes=[pltpu.VMEM(size, BF16) for size in sizes]
        + [
            pltpu.VMEM(hidden_in.shape, BF16),
            pltpu.VMEM((1, group), jnp.int32),
            pltpu.VMEM((1, slots), jnp.int32),
            pltpu.VMEM(bias_up.shape, BF16),
            pltpu.VMEM(norm_gain.shape, F32),
            pltpu.VMEM(norm_bias.shape, F32),
            dma((6,)),
            dma((LAYERS, 6)),
            dma,
            pltpu.VMEM((2, 8, units), F32),
            pltpu.VMEM((n_head,) + block, BF16),
            pltpu.VMEM((devices, tile, 128), BF16),
            pltpu.VMEM((LAYERS, n_head) + block, BF16),
            pltpu.VMEM((LAYERS, n_head) + block, BF16),
            pltpu.VMEM((LAYERS, n_req, n_head) + block, BF16),
            pltpu.VMEM((LAYERS, 2, n_head) + block, BF16),
            pltpu.VMEM((LAYERS, chips) + block, BF16),
            pltpu.VMEM((LAYERS, n_head) + block, F32),
            pltpu.VMEM((LAYERS,) + block, F32),
            pltpu.VMEM((LAYERS, n_head) + block, BF16),
            pltpu.VMEM((2, n_head, 2 * group, part), BF16),
            pltpu.VMEM((2 * chips,) + block, BF16),
            pltpu.VMEM((2,) + block, F32),
            dma,
            dma,
            dma((LAYERS + 1, 2)),
            dma((LAYERS + 1, 2)),
            dma((LAYERS,)),
            dma((LAYERS,)),
            dma((LAYERS,)),
            dma((LAYERS, n_req)),
            dma((LAYERS,)),
            dma((LAYERS,)),
            dma((LAYERS,)),
            dma((LAYERS,)),
            dma((LAYERS,)),
            dma((LAYERS,)),
            dma,
            dma((2,)),
            dma,
            dma((2,)),
            dma,
            dma,
            pltpu.VMEM((w_out.shape[1], key_cache.shape[4], key_cache.shape[1] * key_cache.shape[3]), BF16),
            pltpu.VMEM(embedding.shape[::-1], BF16),
            pltpu.VMEM((LAYERS, width, w_qkv.shape[1] * w_qkv.shape[2]), BF16),
            pltpu.VMEM((LAYERS, 2 * units, width), BF16),
        ],
        compiler_params=pltpu.CompilerParams(
            collective_id=0, has_side_effects=True, vmem_limit_bytes=48 * 1024 * 1024
        ),
    )(
        pin(hidden_in),
        pin(lengths.reshape(1, group)),
        pin(request_order.reshape(1, slots)),
        pin(key_cache),
        pin(value_cache),
        pin(w_qkv),
        pin(w_out),
        pin(w_up),
        pin(bias_up),
        pin(w_down),
        pin(norm_gain),
        pin(norm_bias),
        pin(embedding),
    )


def solution(mesh):
    placed = (
        P(("req", "head"), None),
        P("req"),
        P(),
        P(None, "req", "head", None, None),
        P(None, "req", "head", None, None),
        P(None, "head", None, None),
        P(None, "head", None, None),
        P(None, None, ("req", "head")),
        P(None, ("req", "head")),
        P(None, None, ("req", "head")),
        P(),
        P(),
        P(("req", "head"), None),
    )
    inner = pair_body if (mesh.shape["req"], mesh.shape["head"]) == (4, 8) else body
    return jax.shard_map(
        functools.partial(inner, mesh.shape["req"], mesh.shape["head"]),
        mesh=mesh,
        in_specs=placed,
        out_specs=P(None, ("req", "head")),
        check_vma=False,
    )
```
